32 devices in a mesh: dp: 4 (over y, core), fsdp: 8 (over z, x).
Axes of the slice: x: 2, y: 2, z: 4, core: 2. Of those that a mesh axis runs over, the one named last changes fastest.
Arguments:
- block_in: bfloat16 [160, 197, 768], P(('dp', 'fsdp')), may hold values from -6 to 6
- cotangent: bfloat16 [160, 197, 768], P(('dp', 'fsdp')), may hold values from -6 to 6
- image_live: int32 [160], P(('dp', 'fsdp')), may hold values from 0 to 1, as said below
- image_set: int32 [160], P(('dp', 'fsdp')), may hold values from 0 to 7
- expert_routes: int32 [160, 197, 2], P(('dp', 'fsdp')), may hold values from 0 to 7, as said below
- expert_slots: int32 [160, 197, 2], P(('dp', 'fsdp')), may hold values from -1 to 383, as said below
- gain_attn: bfloat16 [768], P(('dp', 'fsdp')), may hold values from 0.099609375 to 1.8984375
- gain_moe: bfloat16 [768], P(('dp', 'fsdp')), may hold values from 0.099609375 to 1.8984375
- w_qkv: bfloat16 [768, 2304], P(('dp', 'fsdp')), may hold values from -0.21875 to 0.21875
- w_out: bfloat16 [768, 768], P(('dp', 'fsdp')), may hold values from -0.875 to 0.875
- w_router: bfloat16 [768, 8], P(('dp', 'fsdp')), may hold values from -0.109375 to 0.109375
- w_up: bfloat16 [8, 768, 3072], P(None, None, ('dp', 'fsdp')), may hold values from -0.21875 to 0.21875
- w_down: bfloat16 [8, 768, 3072], P(None, None, ('dp', 'fsdp')), may hold values from -0.875 to 0.875
- qkv_adapter_first: bfloat16 [768, 128], P(('dp', 'fsdp')), may hold values from -0.21875 to 0.21875
- qkv_adapter_second: bfloat16 [128, 2304], P(None, ('dp', 'fsdp')), may hold values from -2 to 2
- output_adapter_first: bfloat16 [768, 128], P(('dp', 'fsdp')), may hold values from -0.875 to 0.875
- output_adapter_second: bfloat16 [128, 768], P(None, ('dp', 'fsdp')), may hold values from -2 to 2
- router_adapter_first: bfloat16 [768, 128], P(('dp', 'fsdp')), may hold values from -0.21875 to 0.21875
- router_adapter_second: bfloat16 [1024], P(('dp', 'fsdp')), may hold values from -1 to 1
- up_adapter_first: bfloat16 [8, 768, 128], P(None, ('dp', 'fsdp')), may hold values from -0.21875 to 0.21875
- up_adapter_second: bfloat16 [8, 128, 3072], P(None, None, ('dp', 'fsdp')), may hold values from -2 to 2
- down_adapter_first: bfloat16 [8, 128, 3072], P(None, None, ('dp', 'fsdp')), may hold values from -0.109375 to 0.109375
- down_adapter_second: bfloat16 [8, 128, 768], P(None, None, ('dp', 'fsdp')), may hold values from -6 to 6
Outputs:
- block_out: bfloat16 [160, 197, 768], P(('dp', 'fsdp'))
- input_grad: bfloat16 [160, 197, 768], P(('dp', 'fsdp'))
- grad_qkv_down: float32 [768, 128], P(('dp', 'fsdp'))
- grad_qkv_up: float32 [128, 2304], P(None, ('dp', 'fsdp'))
- grad_out_down: float32 [768, 128], P(('dp', 'fsdp'))
- grad_out_up: float32 [128, 768], P(None, ('dp', 'fsdp'))
- grad_router_down: float32 [768, 128], P(('dp', 'fsdp'))
- router_second_gradient: float32 [1024], P(('dp', 'fsdp'))
- grad_up_down: float32 [8, 768, 128], P(None, ('dp', 'fsdp'))
- grad_up_up: float32 [8, 128, 3072], P(None, None, ('dp', 'fsdp'))
- grad_down_down: float32 [8, 128, 3072], P(None, None, ('dp', 'fsdp'))
- grad_down_up: float32 [8, 128, 768], P(None, None, ('dp', 'fsdp'))
The draws below stay inside these ranges and needn't reach their ends.
Inputs may be any that keep to these rules, and one draw needn't show every extreme that they name: `expert_routes`: A token's two experts differ. In each device's block of 985 tokens some expert is named by 384 or more of them. `expert_slots`: within each device's block of 985 tokens, taken token by token and, inside a token, choice by choice, the choices that name one expert get slots 0, 1, 2, ... in turn; a choice past slot 383 gets -1. Each (expert, slot) pair is used at most once in a block, and slot 383 is used in every block. `image_live`: in each device's block of 5 image slots the live ones come first and at least one is live; some block is all live.
All inputs are finite; a program needn't handle non-finite values.
Results may differ from the reference program's by a relative error of at most 0.018.
Values may be sent and summed in bfloat16 or wider, within the bound.
No kernel may reach another device: no remote copies, remote signals or barrier semaphores. Data moves between devices by JAX's collectives and lax.ppermute only.
A program may use at most 448 MiB of HBM per device.

```python
import math
import jax
import jax.numpy as jnp
from jax import lax

MODEL_WIDTH = 768
HEADS = 12
HEAD = 64
HIDDEN_UNITS = 3072
EXPERT_COUNT = 8
LENGTH = 197
ADAPTER_SETS = 8
ADAPTER_RANK = 16
IMG_DEV = 5
TOK_DEV = 985
ADAPTER_COLUMNS = 128
CAP = 384
IMAGES = 160


def routing_pair(key):
    base = jax.random.fold_in(key, 11)
    blocks = IMAGES // IMG_DEV
    pick_hot, pick_order, pick_first, pick_offset = jax.random.split(base, 4)
    hot_expert = jax.random.randint(pick_hot, (blocks, 1), 0, EXPERT_COUNT)
    shuffled = jax.vmap(lambda subkey: jax.random.permutation(subkey, TOK_DEV))(jax.random.split(pick_order, blocks))
    forced = shuffled < CAP
    first_pick = jnp.where(forced, hot_expert, jax.random.randint(pick_first, (blocks, TOK_DEV), 0, EXPERT_COUNT))
    second = (first_pick + jax.random.randint(pick_offset, (blocks, TOK_DEV), 1, EXPERT_COUNT)) % EXPERT_COUNT
    routes_all = jnp.stack([first_pick, second], axis=-1).astype(jnp.int32)
    assigned = routes_all.reshape(blocks, 2 * TOK_DEV)
    onehot = (assigned[..., None] == jnp.arange(EXPERT_COUNT, dtype=jnp.int32)).astype(jnp.int32)
    before = jnp.cumsum(onehot, axis=1) - onehot
    position = jnp.sum(before * onehot, axis=-1)
    slot_all = jnp.where(position < CAP, position, -1).astype(jnp.int32)
    return (routes_all.reshape(IMAGES, LENGTH, 2), slot_all.reshape(IMAGES, LENGTH, 2))


def draw_expert_routes(key, part):
    return routing_pair(key)[0]


def draw_expert_slots(key, part):
    return routing_pair(key)[1]


def draw_image_live(key, part):
    base = jax.random.fold_in(key, 23)
    blocks = IMAGES // IMG_DEV
    pick_count, pick_full = jax.random.split(base, 2)
    counts_img = jax.random.randint(pick_count, (blocks,), 1, IMG_DEV + 1)
    full_block = jax.random.randint(pick_full, (), 0, blocks)
    counts_img = jnp.where(jnp.arange(blocks, dtype=jnp.int32) == full_block, IMG_DEV, counts_img)
    live_mask = (jnp.arange(IMG_DEV, dtype=jnp.int32)[None, :] < counts_img[:, None]).astype(jnp.int32)
    return live_mask.reshape(IMAGES)


def plant(drawn, own_key, low, top_value):
    index_at = [jax.random.randint(jax.random.fold_in(own_key, axis), (), 0, length) for axis, length in enumerate(drawn.shape)]
    widest = drawn.shape.index(max(drawn.shape))
    beside = index_at[:widest] + [(index_at[widest] + 1) % drawn.shape[widest]] + index_at[widest + 1:]
    return drawn.at[tuple(index_at)].set(low).at[tuple(beside)].set(top_value)


def level_of(key, extent, shards, smallest, high):
    level, own = 1.0, jax.random.fold_in(key, 6)
    for dim, blocks in shards:
        heights = jnp.exp(jax.random.uniform(jax.random.fold_in(own, dim), (blocks,), jnp.float32, smallest / len(shards), high / len(shards)))
        level = level * jnp.repeat(heights, extent[dim] // blocks).reshape([-1 if axis == dim else 1 for axis in range(len(extent))])
    return level


def centred(own_key, shape, deviation, reach, cuts=(), kind=jnp.bfloat16):
    result = deviation * jax.random.normal(own_key, shape, jnp.float32)
    if cuts:
        result = result * level_of(own_key, shape, cuts, -0.22, 0.18)
    return jnp.clip(result, -reach, reach).astype(kind)


def setup_inputs(seed: int = 0) -> dict:
    streams_of = jax.random.split(jax.random.key(seed), 24)
    return {
        "block_in": centred(streams_of[0], (IMAGES, LENGTH, MODEL_WIDTH), 1.0, 6.0, ((0, 32),)),
        "cotangent": centred(streams_of[1], (IMAGES, LENGTH, MODEL_WIDTH), 1.0, 6.0, ((0, 32),)),
        "image_live": draw_image_live(jax.random.fold_in(streams_of[23], 71), 0),
        "image_set": plant(jax.random.randint(streams_of[3], (IMAGES,), 0, ADAPTER_SETS), jax.random.fold_in(streams_of[3], 1), 0, ADAPTER_SETS - 1).astype(jnp.int32),
        "expert_routes": draw_expert_routes(jax.random.fold_in(streams_of[23], 71), 0),
        "expert_slots": draw_expert_slots(jax.random.fold_in(streams_of[23], 71), 0),
        "gain_attn": jnp.clip(1.0 + 0.18 * jax.random.normal(streams_of[6], (MODEL_WIDTH,), jnp.float32), 0.099609375, 1.8984375).astype(jnp.bfloat16),
        "gain_moe": jnp.clip(1.0 + 0.18 * jax.random.normal(streams_of[7], (MODEL_WIDTH,), jnp.float32), 0.099609375, 1.8984375).astype(jnp.bfloat16),
        "w_qkv": centred(streams_of[8], (MODEL_WIDTH, 3 * MODEL_WIDTH), MODEL_WIDTH ** -0.5, 0.21875, ((0, 32),)),
        "w_out": centred(streams_of[9], (MODEL_WIDTH, MODEL_WIDTH), (MODEL_WIDTH // 16) ** -0.5, 0.875, ((0, 32),)),
        "w_router": centred(streams_of[10], (MODEL_WIDTH, EXPERT_COUNT), (4 * MODEL_WIDTH) ** -0.5, 0.109375, ((0, 32),)),
        "w_up": centred(streams_of[11], (EXPERT_COUNT, MODEL_WIDTH, HIDDEN_UNITS), MODEL_WIDTH ** -0.5, 0.21875, ((2, 32),)),
        "w_down": centred(streams_of[12], (EXPERT_COUNT, MODEL_WIDTH, HIDDEN_UNITS), (HIDDEN_UNITS // 64) ** -0.5, 0.875, ((2, 32),)),
        "qkv_adapter_first": centred(streams_of[13], (MODEL_WIDTH, ADAPTER_COLUMNS), MODEL_WIDTH ** -0.5, 0.21875, ((0, 32),)),
        "qkv_adapter_second": centred(streams_of[14], (ADAPTER_COLUMNS, 3 * MODEL_WIDTH), 0.125, 2.0, ((1, 32),)),
        "output_adapter_first": centred(streams_of[15], (MODEL_WIDTH, ADAPTER_COLUMNS), (MODEL_WIDTH // 16) ** -0.5, 0.875, ((0, 32),)),
        "output_adapter_second": centred(streams_of[16], (ADAPTER_COLUMNS, MODEL_WIDTH), 0.125, 2.0, ((1, 32),)),
        "router_adapter_first": centred(streams_of[17], (MODEL_WIDTH, ADAPTER_COLUMNS), MODEL_WIDTH ** -0.5, 0.21875, ((0, 32),)),
        "router_adapter_second": centred(streams_of[18], (ADAPTER_COLUMNS * EXPERT_COUNT,), 0.0625, 1.0, ((0, 32),)),
        "up_adapter_first": centred(streams_of[19], (EXPERT_COUNT, MODEL_WIDTH, ADAPTER_COLUMNS), MODEL_WIDTH ** -0.5, 0.21875, ((1, 32),)),
        "up_adapter_second": centred(streams_of[20], (EXPERT_COUNT, ADAPTER_COLUMNS, HIDDEN_UNITS), 0.125, 2.0, ((2, 32),)),
        "down_adapter_first": centred(streams_of[21], (EXPERT_COUNT, ADAPTER_COLUMNS, HIDDEN_UNITS), HIDDEN_UNITS ** -0.5, 0.109375, ((2, 32),)),
        "down_adapter_second": centred(streams_of[22], (EXPERT_COUNT, ADAPTER_COLUMNS, MODEL_WIDTH), 1.0, 6.0, ((2, 32),)),
    }


@jax.custom_vjp
def reduced_precision(v):
    return lax.optimization_barrier(v.astype(jnp.bfloat16)).astype(jnp.float32)

@jax.custom_vjp
def reduced_backward(v):
    return v

def low_keep(v):
    return (reduced_precision(v), None)

def low_pass(kept, grad):
    return (grad,)

def back_keep(v):
    return (v, None)

def back_low(kept, grad):
    return (reduced_precision(grad),)
reduced_precision.defvjp(low_keep, low_pass)
reduced_backward.defvjp(back_keep, back_low)
HIGHEST = lax.Precision.HIGHEST

def matrix_product(first_mat, second_mat):
    return jnp.dot(first_mat, second_mat, precision=HIGHEST, preferred_element_type=jnp.float32)

def layer_norm(values, gain_vec):
    mean_val = lax.optimization_barrier(jnp.mean(values, axis=-1, keepdims=True))
    centered = values - mean_val
    variance = lax.optimization_barrier(jnp.mean(centered * centered, axis=-1, keepdims=True))
    return centered * lax.rsqrt(variance + 1e-06) * gain_vec

def block_forward(hidden_in, adapters, frozen, live_img, set_img, route_img, slot_img):
    qkv_adapter_first, qkv_adapter_second, output_adapter_first, output_adapter_second, router_adapter_first, router_adapter_second, up_adapter_first, up_adapter_second, down_adapter_first, down_adapter_second = adapters
    gain_attn, gain_moe, w_qkv, w_out, w_router, w_up, w_down = frozen
    tok_count = IMG_DEV * LENGTH
    hidden = hidden_in.reshape(tok_count, MODEL_WIDTH)
    token_adapter_set = jnp.repeat(set_img, LENGTH)
    column_indices = jnp.arange(ADAPTER_SETS * ADAPTER_RANK, dtype=jnp.int32) // ADAPTER_RANK
    adapter_column_mask = (token_adapter_set[:, None] == column_indices[None, :]).astype(jnp.float32)
    live_tok = jnp.repeat(live_img, LENGTH).astype(jnp.float32)
    first_input = reduced_precision(layer_norm(hidden, gain_attn))
    qkv_adapter_delta = reduced_backward(reduced_precision(adapter_column_mask * matrix_product(first_input, qkv_adapter_first)))
    qkv = reduced_backward(reduced_precision(matrix_product(first_input, w_qkv) + matrix_product(qkv_adapter_delta, qkv_adapter_second)))
    qkv = qkv.reshape(IMG_DEV, LENGTH, 3, HEADS, HEAD)
    queries = qkv[:, :, 0]
    key_rows = qkv[:, :, 1]
    values = qkv[:, :, 2]
    score_scale = 1.0 / math.sqrt(HEAD)
    scores = reduced_backward(score_scale * jnp.einsum('bqhd,bkhd->bhqk', queries, key_rows, precision=HIGHEST))
    attn_probs = jax.nn.softmax(scores, axis=-1)
    attention_output = jnp.einsum('bhqk,bkhd->bqhd', reduced_precision(attn_probs), values, precision=HIGHEST).reshape(tok_count, MODEL_WIDTH)
    attention_output = reduced_backward(reduced_precision(attention_output))
    output_adapter_delta = reduced_backward(reduced_precision(adapter_column_mask * matrix_product(attention_output, output_adapter_first)))
    branch = reduced_backward(matrix_product(attention_output, w_out) + matrix_product(output_adapter_delta, output_adapter_second))
    middle = hidden + branch
    second_input = reduced_precision(layer_norm(middle, gain_moe))
    router_adapter_delta = reduced_backward(reduced_precision(adapter_column_mask * matrix_product(second_input, router_adapter_first)))
    logits = reduced_backward(matrix_product(second_input, w_router) + matrix_product(router_adapter_delta, router_adapter_second.reshape(ADAPTER_SETS * ADAPTER_RANK, EXPERT_COUNT)))
    router_probs = jax.nn.softmax(logits, axis=-1)
    route_tok = route_img.reshape(tok_count, 2)
    slot_tok = slot_img.reshape(tok_count, 2)
    is_kept = slot_tok >= 0
    target = jnp.where(is_kept, route_tok * CAP + slot_tok, EXPERT_COUNT * CAP)
    token_ids = jnp.repeat(jnp.arange(tok_count, dtype=jnp.int32), 2)
    slot_owner = jnp.full((EXPERT_COUNT * CAP + 1,), tok_count, jnp.int32).at[target.reshape(-1)].set(token_ids)[:EXPERT_COUNT * CAP]
    padded = jnp.concatenate([second_input, jnp.zeros((1, MODEL_WIDTH), jnp.float32)], axis=0)
    expert_in = padded[slot_owner].reshape(EXPERT_COUNT, CAP, MODEL_WIDTH)
    row_set = jnp.concatenate([token_adapter_set, jnp.full((1,), -1, jnp.int32)], axis=0)[slot_owner].reshape(EXPERT_COUNT, CAP)
    row_mask = (row_set[..., None] == column_indices).astype(jnp.float32)
    adapt_u = reduced_backward(reduced_precision(row_mask * jnp.einsum('ecd,edr->ecr', expert_in, up_adapter_first, precision=HIGHEST)))
    pre_gelu = reduced_backward(jnp.einsum('ecd,edf->ecf', expert_in, w_up, precision=HIGHEST) + jnp.einsum('ecr,erf->ecf', adapt_u, up_adapter_second, precision=HIGHEST))
    active = reduced_precision(jax.nn.gelu(pre_gelu))
    adapt_d = reduced_backward(reduced_precision(row_mask * jnp.einsum('ecf,erf->ecr', active, down_adapter_first, precision=HIGHEST)))
    expert_out = reduced_backward(jnp.einsum('ecf,edf->ecd', active, w_down, precision=HIGHEST) + jnp.einsum('ecr,erd->ecd', adapt_d, down_adapter_second, precision=HIGHEST))
    flat_out = jnp.concatenate([expert_out.reshape(EXPERT_COUNT * CAP, MODEL_WIDTH), jnp.zeros((1, MODEL_WIDTH), jnp.float32)], axis=0)
    gate_values = jnp.take_along_axis(router_probs, route_tok, axis=1) * is_kept.astype(jnp.float32)
    mixed = lax.optimization_barrier(jnp.sum(gate_values[..., None] * flat_out[target], axis=1))
    return (middle + mixed) * live_tok[:, None]

def reference(block_in, cotangent, image_live, image_set, expert_routes, expert_slots, gain_attn, gain_moe, w_qkv, w_out, w_router, w_up, w_down, qkv_adapter_first, qkv_adapter_second, output_adapter_first, output_adapter_second, router_adapter_first, router_adapter_second, up_adapter_first, up_adapter_second, down_adapter_first, down_adapter_second):
    blocks = block_in.shape[0] // IMG_DEV
    frozen = tuple((item.astype(jnp.float32) for item in (gain_attn, gain_moe, w_qkv, w_out, w_router, w_up, w_down)))
    adapters = tuple((item.astype(jnp.float32) for item in (qkv_adapter_first, qkv_adapter_second, output_adapter_first, output_adapter_second, router_adapter_first, router_adapter_second, up_adapter_first, up_adapter_second, down_adapter_first, down_adapter_second)))
    pieces = (block_in.reshape(blocks, IMG_DEV, LENGTH, MODEL_WIDTH), cotangent.reshape(blocks, IMG_DEV, LENGTH, MODEL_WIDTH), image_live.reshape(blocks, IMG_DEV), image_set.reshape(blocks, IMG_DEV), expert_routes.reshape(blocks, IMG_DEV, LENGTH, 2), expert_slots.reshape(blocks, IMG_DEV, LENGTH, 2))

    def one_block(running, piece):
        block_val, block_cot, live_img, set_img, route_img, slot_img = piece

        def forward(hidden_in, adapter_set):
            return block_forward(hidden_in, adapter_set, frozen, live_img, set_img, route_img, slot_img)
        result_rows, pullback = jax.vjp(forward, block_val.astype(jnp.float32), adapters)
        grad_input, grad_adapters = pullback(block_cot.astype(jnp.float32).reshape(IMG_DEV * LENGTH, MODEL_WIDTH))
        running = jax.tree.map(lambda total, extra: total + extra, running, grad_adapters)
        return (running, (result_rows.astype(jnp.bfloat16).reshape(IMG_DEV, LENGTH, MODEL_WIDTH), grad_input.astype(jnp.bfloat16)))
    initial = jax.tree.map(jnp.zeros_like, adapters)
    totals, (outputs, grads) = lax.scan(one_block, initial, pieces)
    block_out = outputs.reshape(blocks * IMG_DEV, LENGTH, MODEL_WIDTH)
    input_grad = grads.reshape(blocks * IMG_DEV, LENGTH, MODEL_WIDTH)
    return (block_out, input_grad, totals[0], totals[1], totals[2], totals[3], totals[4], totals[5], totals[6], totals[7], totals[8], totals[9])
```

```python
import functools
import math

import jax
import jax.numpy as jnp
from jax import lax
from jax.experimental import pallas as pl
from jax.experimental.pallas import tpu as pltpu
from jax.sharding import PartitionSpec as P

D = 768
HEADS = 12
HEAD = 64
NE = 8
LEN = 197
LP = 208
SL = 256
AC = 128
RANK = 16
CAP = 384
IMG = 5
GRP = 4
EL = NE // GRP
ROWS = GRP * CAP
RT = 256
DW = D + AC
EPS = 1e-06
F32 = jnp.float32
BF = jnp.bfloat16
AXES = ("dp", "fsdp")
VMEM = 60 * 1000 * 1024


def nn(a, b):
    return lax.dot_general(a, b, (((1,), (0,)), ((), ())), preferred_element_type=F32)


def nt(a, b):
    return lax.dot_general(a, b, (((1,), (1,)), ((), ())), preferred_element_type=F32)


def adapter_mask(rows, which):
    lane = lax.broadcasted_iota(jnp.int32, (rows, AC), 1)
    return jnp.where(lane // RANK == which, 1.0, 0.0).astype(F32)


def norm_parts(v):
    mean = jnp.mean(v, axis=-1, keepdims=True)
    cen = v - mean
    var = jnp.mean(cen * cen, axis=-1, keepdims=True)
    inv = lax.rsqrt(var + EPS)
    return cen * inv, inv


def norm_back(g, unit, inv, gain):
    s = g * gain
    return inv * (
        s
        - jnp.mean(s, axis=-1, keepdims=True)
        - unit * jnp.mean(s * unit, axis=-1, keepdims=True)
    )


def params(n):
    return pltpu.CompilerParams(dimension_semantics=("arbitrary",) * n, vmem_limit_bytes=VMEM)


def whole(shape):
    zeros = (0,) * len(shape)
    return pl.BlockSpec(shape, lambda *_: zeros, pipeline_mode=pl.Buffered(1))


def per_image(shape):
    rest = (0,) * (len(shape) - 1)
    return pl.BlockSpec(shape, lambda i, *_: (i,) + rest)


def fwd_kernel(sets, x_ref, g_ref, wq, wk, wv, wo, b4, a2t, rm, qkv_ref, att_ref, mid_ref, x2_ref, ad_ref, pr_ref, hid):
    mask = adapter_mask(LP, sets[pl.program_id(0)])
    hid[...] = jnp.zeros((LP, D), F32)
    hid[0:LEN, :] = x_ref[0].astype(F32)
    hidden = hid[...]
    unit, _ = norm_parts(hidden)
    x1 = (unit * g_ref[0:1, :]).astype(BF)
    aq = (mask * nn(x1, b4[:, 0:AC])).astype(BF)
    ad_ref[0, :, 0:AC] = aq
    for j, w in enumerate((wq, wk, wv)):
        part = nn(x1, w[...]) + nt(aq, a2t[j * D:(j + 1) * D, :])
        qkv_ref[0, :, j * D:(j + 1) * D] = part.astype(BF)
    lane = lax.broadcasted_iota(jnp.int32, (LP, 2 * HEAD), 1)
    keyok = lax.broadcasted_iota(jnp.int32, (LP, LP), 1) < LEN
    scale = 1.0 / math.sqrt(HEAD)
    for h in range(HEADS // 2):
        at = h * 2 * HEAD
        q = qkv_ref[0, :, at:at + 2 * HEAD]
        k = qkv_ref[0, :, D + at:D + at + 2 * HEAD]
        v = qkv_ref[0, :, 2 * D + at:2 * D + at + 2 * HEAD]
        outs = []
        for half in range(2):
            mine = (lane >= HEAD) if half else (lane < HEAD)
            s = nt(jnp.where(mine, q, jnp.zeros_like(q)), k) * scale
            s = jnp.where(keyok, s, -1e30)
            e = jnp.exp(s - jnp.max(s, axis=-1, keepdims=True))
            p = e * (1.0 / jnp.sum(e, axis=-1, keepdims=True))
            outs.append(nn(p.astype(BF), v))
        att_ref[0, :, at:at + 2 * HEAD] = jnp.where(lane < HEAD, outs[0], outs[1]).astype(BF)
    att = att_ref[0]
    ao = (mask * nn(att, b4[:, AC:2 * AC])).astype(BF)
    ad_ref[0, :, AC:2 * AC] = ao
    middle = hidden + nn(att, wo[...]) + nt(ao, b4[:, 3 * AC:4 * AC])
    mid_ref[0] = middle
    unit2, _ = norm_parts(middle)
    x2 = (unit2 * g_ref[1:2, :]).astype(BF)
    x2_ref[0] = x2
    ar = (mask * nn(x2, b4[:, 2 * AC:3 * AC])).astype(BF)
    ad_ref[0, :, 2 * AC:3 * AC] = ar
    logits = nn(x2, b4[:, 4 * AC:5 * AC]) + nn(ar, rm[...])
    elane = lax.broadcasted_iota(jnp.int32, (LP, AC), 1)
    logits = jnp.where(elane < NE, logits, -1e30)
    e = jnp.exp(logits - jnp.max(logits, axis=-1, keepdims=True))
    probs = e * (1.0 / jnp.sum(e, axis=-1, keepdims=True))
    padded = jnp.concatenate([probs, jnp.zeros((SL - LP, AC), F32)], axis=0)
    pr_ref[0] = jnp.transpose(padded)[0:NE, :]


def attention_forward(block_in, sets, gains, wq, wk, wv, wo, b4, a2t, rm):
    n = block_in.shape[0]
    sq = whole((D, D))
    return pl.pallas_call(
        fwd_kernel,
        grid_spec=pltpu.PrefetchScalarGridSpec(
            num_scalar_prefetch=1,
            grid=(n,),
            in_specs=[per_image((1, LEN, D)), whole((8, D)), sq, sq, sq, sq, sq, whole((3 * D, AC)), whole((AC, AC))],
            out_specs=[
                per_image((1, LP, 3 * D)),
                per_image((1, LP, D)),
                per_image((1, LP, D)),
                per_image((1, LP, D)),
                per_image((1, LP, 3 * AC)),
                per_image((1, NE, SL)),
            ],
            scratch_shapes=[pltpu.VMEM((LP, D), F32)],
        ),
        out_shape=[
            jax.ShapeDtypeStruct((n, LP, 3 * D), BF),
            jax.ShapeDtypeStruct((n, LP, D), BF),
            jax.ShapeDtypeStruct((n, LP, D), F32),
            jax.ShapeDtypeStruct((n, LP, D), BF),
            jax.ShapeDtypeStruct((n, LP, 3 * AC), BF),
            jax.ShapeDtypeStruct((n, NE, SL), F32),
        ],
        compiler_params=params(1),
        name="attention_forward",
    )(sets, block_in, gains, wq, wk, wv, wo, b4, a2t, rm)


def dispatch_kernel(offs, sets, slot_ref, gate_ref, x2_ref, cot_ref, u1_ref, d2_ref, xa_ref, ga_ref, mk_ref, acc, cpad):
    e = pl.program_id(0)
    b = pl.program_id(1)

    @pl.when(b == 0)
    def _():
        xa_ref[...] = jnp.zeros_like(xa_ref)
        ga_ref[...] = jnp.zeros_like(ga_ref)
        mk_ref[...] = jnp.zeros_like(mk_ref)

    acc[...] = jnp.zeros_like(acc)
    cpad[...] = jnp.zeros_like(cpad)
    gcol = jnp.transpose(gate_ref[0, 0])
    rows = lax.broadcasted_iota(jnp.int32, (CAP, LP), 0)
    for i in range(IMG):
        pick = jnp.where(rows == slot_ref[0, 0, i:i + 1, 0:LP], 1.0, 0.0).astype(BF)
        cpad[0:LEN, :] = cot_ref[0, i].astype(F32)
        gg = (cpad[...] * gcol[0:LP, i:i + 1]).astype(BF)
        acc[:, 0:D] += nn(pick, x2_ref[0, i])
        acc[:, D:2 * D] += nn(pick, gg)
        acc[:, 2 * D:] += nn(pick, adapter_mask(LP, sets[b * IMG + i]).astype(BF))
    mk = acc[:, 2 * D:]
    xs = acc[:, 0:D].astype(BF)
    gs = acc[:, D:2 * D].astype(BF)
    at = pl.multiple_of(offs[e * (GRP + 1) + b], 16)
    here = pl.ds(at, CAP)
    xa_ref[0, here, 0:D] = xs
    xa_ref[0, here, D:DW] = (mk * nn(xs, u1_ref[0])).astype(BF)
    ga_ref[0, here, 0:D] = gs
    ga_ref[0, here, D:DW] = (mk * nn(gs, d2_ref[0])).astype(BF)
    mk_ref[0, here, :] = mk.astype(BF)


def dispatch(offs, sets, slots, gates, x2, cot, u1, d2):
    return pl.pallas_call(
        dispatch_kernel,
        grid_spec=pltpu.PrefetchScalarGridSpec(
            num_scalar_prefetch=2,
            grid=(EL, GRP),
            in_specs=[
                pl.BlockSpec((1, 1, 8, SL), lambda e, b, *_: (b, e, 0, 0)),
                pl.BlockSpec((1, 1, 8, SL), lambda e, b, *_: (b, e, 0, 0)),
                pl.BlockSpec((1, IMG, LP, D), lambda e, b, *_: (b, 0, 0, 0)),
                pl.BlockSpec((1, IMG, LEN, D), lambda e, b, *_: (b, 0, 0, 0)),
                pl.BlockSpec((1, D, AC), lambda e, b, *_: (e, 0, 0)),
                pl.BlockSpec((1, D, AC), lambda e, b, *_: (e, 0, 0)),
            ],
            out_specs=[
                pl.BlockSpec((1, ROWS, DW), lambda e, b, *_: (e, 0, 0)),
                pl.BlockSpec((1, ROWS, DW), lambda e, b, *_: (e, 0, 0)),
                pl.BlockSpec((1, ROWS, AC), lambda e, b, *_: (e, 0, 0)),
            ],
            scratch_shapes=[pltpu.VMEM((CAP, 2 * D + AC), F32), pltpu.VMEM((LP, D), F32)],
        ),
        out_shape=[
            jax.ShapeDtypeStruct((EL, ROWS, DW), BF),
            jax.ShapeDtypeStruct((EL, ROWS, DW), BF),
            jax.ShapeDtypeStruct((EL, ROWS, AC), BF),
        ],
        compiler_params=params(2),
        name="dispatch",
    )(offs, sets, slots, gates, x2, cot, u1, d2)


def expert_kernel(first, e, offs, xa_ref, ga_ref, w_ref, *refs):
    if first:
        a1, a2, gu_ref, gd_ref, at_ref = refs
    else:
        p1, p2, a1, a2, gu_ref, gd_ref, at_ref = refs
    total = offs[e * (GRP + 1) + GRP]
    tiles = (total + (RT - 1)) // RT

    @pl.when(pl.program_id(0) == 0)
    def _():
        if first:
            a1[...] = jnp.zeros_like(a1)
            a2[...] = jnp.zeros_like(a2)
        else:
            a1[...] = p1[...]
            a2[...] = p2[...]
        at_ref[0] = jnp.transpose(xa_ref[0, :, D:DW].astype(F32)).astype(BF)
        at_ref[1] = jnp.transpose(ga_ref[0, :, D:DW].astype(F32)).astype(BF)

    wu = w_ref[0, :, 0:DW]
    wd = w_ref[0, :, DW:2 * DW]
    hb = w_ref.shape[1]
    c0 = math.sqrt(2.0 / math.pi)

    def step(t, carry):
        gu, gd = carry
        here = pl.ds(pl.multiple_of(t * RT, RT), RT)
        x = xa_ref[0, here, :]
        g = ga_ref[0, here, :]
        pre = nt(x, wu)
        gact = nt(g, wd)
        sq = pre * pre
        th = jnp.tanh(c0 * pre * (1.0 + 0.044715 * sq))
        half = 0.5 * (1.0 + th)
        act = (pre * half).astype(BF)
        slope = half + 0.5 * pre * (1.0 - th * th) * (c0 * (1.0 + 3 * 0.044715 * sq))
        gp = (slope * gact).astype(BF)
        a1[here, :] += nn(act, wd)
        a2[here, :] += nn(gp, wu)
        gu = gu + nn(at_ref[0, :, here], gp)
        gd = gd + nn(at_ref[1, :, here], act)
        return gu, gd

    zero = jnp.zeros((AC, hb), F32)
    gu, gd = lax.fori_loop(0, tiles, step, (zero, zero))
    gu_ref[0] = gu.astype(BF)
    gd_ref[0] = gd.astype(BF)


def expert_part(e, offs, xa, ga, w, prev):
    n, hb, _ = w.shape
    first = prev is None
    acc = whole((ROWS, DW))
    rows = pl.BlockSpec((1, ROWS, DW), lambda i, *_: (e, 0, 0))
    in_specs = [rows, rows, pl.BlockSpec((1, hb, 2 * DW), lambda i, *_: (i, 0, 0))]
    args = [xa, ga, w]
    alias = {}
    if not first:
        in_specs += [acc, acc]
        args += list(prev)
        alias = {4: 0, 5: 1}
    gspec = pl.BlockSpec((1, AC, hb), lambda i, *_: (i, 0, 0))
    return pl.pallas_call(
        functools.partial(expert_kernel, first, e),
        grid_spec=pltpu.PrefetchScalarGridSpec(
            num_scalar_prefetch=1,
            grid=(n,),
            in_specs=in_specs,
            out_specs=[acc, acc, gspec, gspec],
            scratch_shapes=[pltpu.VMEM((2, AC, ROWS), BF)],
        ),
        out_shape=[
            jax.ShapeDtypeStruct((ROWS, DW), F32),
            jax.ShapeDtypeStruct((ROWS, DW), F32),
            jax.ShapeDtypeStruct((n, AC, hb), BF),
            jax.ShapeDtypeStruct((n, AC, hb), BF),
        ],
        input_output_aliases=alias,
        compiler_params=params(1),
        name="expert_part",
    )(offs, *args)


def combine_kernel(offs, first_expert, a10, a20, a11, a21, xa_ref, ga_ref, mk_ref, u1_ref, d2_ref, slot_ref, gate_ref, cot_ref,
                   y_ref, g_ref, dot_ref, gud_ref, gdu_ref, ob, gb):
    b = pl.program_id(0)

    @pl.when(b == 0)
    def _():
        ob[...] = jnp.zeros_like(ob)
        gb[...] = jnp.zeros_like(gb)
        for e, (a1, a2) in enumerate(((a10, a20), (a11, a21))):
            total = offs[e * (GRP + 1) + GRP]
            tiles = (total + (RT - 1)) // RT

            def step(t, carry):
                gud, gdu = carry
                here = pl.ds(pl.multiple_of(t * RT, RT), RT)
                mk = mk_ref[e, here, :].astype(F32)
                adt = (mk * a1[here, D:DW]).astype(BF)
                aut = (mk * a2[here, D:DW]).astype(BF)
                ob[e, here, :] = (a1[here, 0:D] + nt(adt, d2_ref[e])).astype(BF)
                gb[e, here, :] = (a2[here, 0:D] + nt(aut, u1_ref[e])).astype(BF)
                autt = jnp.transpose(aut.astype(F32)).astype(BF)
                adtt = jnp.transpose(adt.astype(F32)).astype(BF)
                gud = gud + nn(autt, xa_ref[e, here, 0:D])
                gdu = gdu + nn(adtt, ga_ref[e, here, 0:D])
                return gud, gdu

            zero = jnp.zeros((AC, D), F32)
            gud, gdu = lax.fori_loop(0, tiles, step, (zero, zero))
            gud_ref[e] = jnp.transpose(gud).astype(BF)
            gdu_ref[e] = jnp.transpose(gdu).astype(BF)

    lanes = lax.broadcasted_iota(jnp.int32, (LP, CAP), 1).astype(F32)
    dlane = lax.broadcasted_iota(jnp.int32, (LP, AC), 1)
    scol = [jnp.transpose(slot_ref[0, e].astype(F32)) for e in range(EL)]
    gcol = [jnp.transpose(gate_ref[0, e]) for e in range(EL)]
    for i in range(IMG):
        y = jnp.zeros((LP, D), F32)
        g = jnp.zeros((LP, D), F32)
        dots = jnp.zeros((LP, AC), F32)
        cot = jnp.concatenate([cot_ref[0, i].astype(F32), jnp.zeros((LP - LEN, D), F32)], axis=0)
        for e in range(EL):
            at = pl.multiple_of(offs[e * (GRP + 1) + b], 16)
            here = pl.ds(at, CAP)
            pick = jnp.where(scol[e][0:LP, i:i + 1] == lanes, 1.0, 0.0).astype(BF)
            ye = nn(pick, ob[e, here, :])
            g = g + nn(pick, gb[e, here, :])
            y = y + gcol[e][0:LP, i:i + 1] * ye
            dot = jnp.sum(ye * cot, axis=-1, keepdims=True)
            dots = dots + jnp.where(dlane == first_expert[0] + e, dot, 0.0)
        y_ref[0, i] = y.astype(BF)
        g_ref[0, i] = g.astype(BF)
        full = jnp.concatenate([dots, jnp.zeros((SL - LP, AC), F32)], axis=0)
        dot_ref[0, i] = jnp.transpose(full)[0:NE, :]


def combine(offs, first_expert, accs, xa, ga, mk, u1, d2, slots, gates, cot):
    acc = whole((ROWS, DW))
    rows = whole((EL, ROWS, DW))
    block = lambda *shape: pl.BlockSpec((1,) + shape, lambda b, *_: (b,) + (0,) * len(shape))
    return pl.pallas_call(
        combine_kernel,
        grid_spec=pltpu.PrefetchScalarGridSpec(
            num_scalar_prefetch=2,
            grid=(GRP,),
            in_specs=[acc, acc, acc, acc, rows, rows, whole((EL, ROWS, AC)), whole((EL, D, AC)), whole((EL, D, AC)),
                      block(EL, 8, SL), block(EL, 8, SL), block(IMG, LEN, D)],
            out_specs=[block(IMG, LP, D), block(IMG, LP, D), block(IMG, NE, SL), whole((EL, D, AC)), whole((EL, D, AC))],
            scratch_shapes=[pltpu.VMEM((EL, ROWS, D), BF), pltpu.VMEM((EL, ROWS, D), BF)],
        ),
        out_shape=[
            jax.ShapeDtypeStruct((GRP, IMG, LP, D), BF),
            jax.ShapeDtypeStruct((GRP, IMG, LP, D), BF),
            jax.ShapeDtypeStruct((GRP, IMG, NE, SL), F32),
            jax.ShapeDtypeStruct((EL, D, AC), BF),
            jax.ShapeDtypeStruct((EL, D, AC), BF),
        ],
        compiler_params=params(1),
        name="combine",
    )(offs, first_expert, accs[0][0], accs[0][1], accs[1][0], accs[1][1], xa, ga, mk, u1, d2, slots, gates, cot)


def bwd_kernel(sets, live, x_ref, cot_ref, gin_ref, dot_ref, pr_ref, mid_ref, y_ref, qkv_ref, att_ref, x2_ref, ad_ref, g_ref,
               wq, wk, wv, wo, b4, a2t, rm, out_ref, ig_ref, acc_ref, hid, gq, acc):
    i = pl.program_id(0)
    mask = adapter_mask(LP, sets[i])
    alive = live[i].astype(F32)
    aq = ad_ref[0, :, 0:AC]
    ao = ad_ref[0, :, AC:2 * AC]
    ar = ad_ref[0, :, 2 * AC:3 * AC]

    @pl.when(i == 0)
    def _():
        acc[...] = jnp.zeros_like(acc)

    def tr(v):
        return jnp.transpose(v.astype(F32)).astype(BF)

    hid[...] = jnp.zeros((LP, D), F32)
    hid[0:LEN, :] = cot_ref[0].astype(F32) * alive
    gfin = hid[...]
    elane = lax.broadcasted_iota(jnp.int32, (LP, AC), 1)
    zrow = jnp.zeros((AC - NE, SL), F32)
    probs = jnp.transpose(jnp.concatenate([pr_ref[0], zrow], axis=0))[0:LP, :]
    gprobs = jnp.transpose(jnp.concatenate([dot_ref[0], zrow], axis=0))[0:LP, :]
    gl = probs * (gprobs - jnp.sum(gprobs * probs, axis=-1, keepdims=True))
    gl = jnp.where(elane < NE, gl, 0.0).astype(BF)
    gar = (mask * nt(gl, rm[...])).astype(BF)
    gtwo = gin_ref[0] + nt(gl, b4[:, 4 * AC:5 * AC]) + nt(gar, b4[:, 2 * AC:3 * AC])
    middle = mid_ref[0]
    out_ref[0] = ((middle + y_ref[0].astype(F32)) * alive)[0:LEN, :].astype(BF)
    unit2, inv2 = norm_parts(middle)
    gmid = gfin + norm_back(gtwo, unit2, inv2, g_ref[1:2, :])
    gbr = gmid.astype(BF)
    gao = (mask * nn(gbr, b4[:, 3 * AC:4 * AC])).astype(BF)
    gatt = (nt(gbr, wo[...]) + nt(gao, b4[:, AC:2 * AC])).astype(BF)
    gart = tr(gar)
    acc[:, 4 * D:5 * D] += nn(tr(gao), att_ref[0])
    acc[:, 5 * D:6 * D] += nn(tr(ao), gbr)
    acc[:, 6 * D:7 * D] += nn(gart, x2_ref[0])
    acc[:, 7 * D:] += nn(tr(ar), gl)

    lane = lax.broadcasted_iota(jnp.int32, (LP, 2 * HEAD), 1)
    keyok = lax.broadcasted_iota(jnp.int32, (LP, LP), 0) < LEN
    drow = lax.broadcasted_iota(jnp.int32, (2 * HEAD, LP), 0)
    scale = 1.0 / math.sqrt(HEAD)
    for h in range(HEADS // 2):
        at = h * 2 * HEAD
        q = qkv_ref[0, :, at:at + 2 * HEAD]
        k = qkv_ref[0, :, D + at:D + at + 2 * HEAD]
        v = qkv_ref[0, :, 2 * D + at:2 * D + at + 2 * HEAD]
        go = gatt[:, at:at + 2 * HEAD]
        kt = tr(k)
        dq, dk, dv = [], [], []
        for half in range(2):
            mine = (lane >= HEAD) if half else (lane < HEAD)
            s = nt(k, jnp.where(mine, q, jnp.zeros_like(q))) * scale
            s = jnp.where(keyok, s, -1e30)
            ex = jnp.exp(s - jnp.max(s, axis=0, keepdims=True))
            p = ex * (1.0 / jnp.sum(ex, axis=0, keepdims=True))
            dv.append(nn(p.astype(BF), go))
            dp = nt(v, jnp.where(mine, go, jnp.zeros_like(go)))
            gs = (p * (dp - jnp.sum(dp * p, axis=0, keepdims=True))).astype(BF)
            dk.append(nn(gs, q))
            dq.append(nn(kt, gs))
        dqt = jnp.where(drow < HEAD, dq[0], dq[1]) * scale
        gq[:, at:at + 2 * HEAD] = jnp.transpose(dqt).astype(BF)
        gq[:, D + at:D + at + 2 * HEAD] = (jnp.where(lane < HEAD, dk[0], dk[1]) * scale).astype(BF)
        gq[:, 2 * D + at:2 * D + at + 2 * HEAD] = jnp.where(lane < HEAD, dv[0], dv[1]).astype(BF)
    gqkv = gq[...]
    gaq = (mask * nn(gqkv, a2t[...])).astype(BF)
    hid[...] = jnp.zeros((LP, D), F32)
    hid[0:LEN, :] = x_ref[0].astype(F32)
    unit1, inv1 = norm_parts(hid[...])
    x1 = (unit1 * g_ref[0:1, :]).astype(BF)
    acc[:, 0:D] += nn(tr(gaq), x1)
    acc[:, D:4 * D] += nn(tr(aq), gqkv)
    gone = nt(gaq, b4[:, 0:AC])
    for j, w in enumerate((wq, wk, wv)):
        gone = gone + nt(gqkv[:, j * D:(j + 1) * D], w[...])
    ig = gmid + norm_back(gone, unit1, inv1, g_ref[0:1, :])
    ig_ref[0] = ig[0:LEN, :].astype(BF)

    @pl.when(i == pl.num_programs(0) - 1)
    def _():
        for c in range(acc.shape[1] // AC):
            acc_ref[c * AC:(c + 1) * AC, :] = jnp.transpose(acc[:, c * AC:(c + 1) * AC])


def backward(sets, live, block_in, cot, gin, dots, probs, mid, y, qkv, att, x2, ad, gains, wq, wk, wv, wo, b4, a2t, rm):
    n = block_in.shape[0]
    sq = whole((D, D))
    na = 7 * D + AC
    return pl.pallas_call(
        bwd_kernel,
        grid_spec=pltpu.PrefetchScalarGridSpec(
            num_scalar_prefetch=2,
            grid=(n,),
            in_specs=[
                per_image((1, LEN, D)), per_image((1, LEN, D)), per_image((1, LP, D)), per_image((1, NE, SL)), per_image((1, NE, SL)),
                per_image((1, LP, D)), per_image((1, LP, D)), per_image((1, LP, 3 * D)), per_image((1, LP, D)), per_image((1, LP, D)),
                per_image((1, LP, 3 * AC)), whole((8, D)), sq, sq, sq, sq, sq, whole((3 * D, AC)), whole((AC, AC)),
            ],
            out_specs=[per_image((1, LEN, D)), per_image((1, LEN, D)), whole((na, AC))],
            scratch_shapes=[pltpu.VMEM((LP, D), F32), pltpu.VMEM((LP, 3 * D), BF), pltpu.VMEM((AC, na), F32)],
        ),
        out_shape=[
            jax.ShapeDtypeStruct((n, LEN, D), BF),
            jax.ShapeDtypeStruct((n, LEN, D), BF),
            jax.ShapeDtypeStruct((na, AC), F32),
        ],
        compiler_params=params(1),
        name="backward",
    )(sets, live, block_in, cot, gin, dots, probs, mid, y, qkv, att, x2, ad, gains, wq, wk, wv, wo, b4, a2t, rm)


def on_device(dpn, fsn, block_in, cotangent, image_live, image_set, expert_routes, expert_slots, gain_attn, gain_moe, w_qkv, w_out,
              w_router, w_up, w_down, qkv_first, qkv_second, out_first, out_second, router_first, router_second, up_first,
              up_second, down_first, down_second):
    ndev = dpn * fsn
    nx = 1 << ((fsn.bit_length() - 1) // 2)
    nz = fsn // nx
    ng = dpn // GRP
    r = D // ndev
    hs = w_up.shape[2]
    d = lax.axis_index("dp")
    q = d % GRP
    rings = [
        (nz, "fsdp", [(f, ((f // nx + 1) % nz) * nx + f % nx) for f in range(fsn)]),
        (nx, "fsdp", [(f, (f // nx) * nx + (f % nx + 1) % nx) for f in range(fsn)]),
        (ng, "dp", [(a, (a + GRP) % dpn) for a in range(dpn)]),
    ]

    def swap(v, bit):
        return lax.ppermute(v, "dp", [(a, a ^ bit) for a in range(dpn)])

    rel = [0, 2, 1, 3]

    tr = jnp.transpose
    small = jnp.concatenate(
        [
            qkv_first, out_first, router_first, tr(out_second),
            jnp.concatenate([w_router, gain_attn[:, None], gain_moe[:, None], jnp.zeros((r, AC - NE - 2), BF)], axis=1),
            jnp.zeros((r, AC), BF).at[0, 0:router_second.shape[0]].set(router_second),
        ],
        axis=1,
    )
    a2s = tr(qkv_second).reshape(3, r, AC)
    second = jnp.concatenate([a2s[0], a2s[1], a2s[2], jnp.zeros((r, 3 * AC), BF)], axis=1)
    front = jnp.stack([w_qkv[:, 0:D], w_qkv[:, D:2 * D], w_qkv[:, 2 * D:], w_out, small, second])
    front = lax.all_gather(front.reshape(6 * r, D), AXES, axis=0, tiled=True).reshape(ndev, 6, r, D)
    wq, wk, wv, wo, b4 = (front[:, j].reshape(D, D) for j in range(5))
    a2t = tr(front[:, 5, :, 0:3 * AC].reshape(ndev, r, 3, AC), (0, 2, 1, 3)).reshape(3 * D, AC)
    gains = jnp.concatenate(
        [b4[:, 4 * AC + NE].reshape(1, D), b4[:, 4 * AC + NE + 1].reshape(1, D), jnp.zeros((6, D), BF)], axis=0
    ).astype(F32)
    rm = front[:, 4, 0, 5 * AC:5 * AC + router_second.shape[0]].reshape(AC, NE)
    rm = jnp.pad(rm, ((0, 0), (0, AC - NE)))

    wpk = jnp.concatenate([tr(w_up, (0, 2, 1)), tr(up_second, (0, 2, 1)), tr(w_down, (0, 2, 1)), tr(down_first, (0, 2, 1))], axis=2)
    wpk = wpk.reshape(GRP, EL, hs, 2 * DW)
    own = [lax.dynamic_index_in_dim(wpk, q ^ j, 0, keepdims=False) for j in range(GRP)]
    got = swap(jnp.stack([own[2], own[3]]), 2)
    mine = jnp.stack([own[0], got[0]])
    sib = swap(jnp.stack([own[1], got[1]]), 1)
    mine = jnp.concatenate([mine, sib], axis=0)
    units = [mine[:, e].reshape(GRP * hs, 2 * DW) for e in range(EL)]
    parts = []
    for e in range(EL):
        held = [units[e]]
        for n, axis, perm in rings:
            rows = [held]
            for _ in range(n - 1):
                rows.append([lax.ppermute(v, axis, perm) for v in rows[-1]])
            held = [v for row in rows for v in row]
        parts.append(held)

    route = expert_routes.reshape(IMG, LEN, 2)
    slot = expert_slots.reshape(IMG, LEN, 2)
    ids = jnp.arange(NE, dtype=jnp.int32)[None, :, None, None]
    ok = (route[:, None] == ids) & (slot[:, None] >= 0) & (image_live[:, None, None, None] > 0)
    mine_slots = jnp.max(jnp.where(ok, slot[:, None], -1), axis=-1)
    mine_slots = jnp.pad(mine_slots, ((0, 8 - IMG), (0, 0), (0, SL - LEN)), constant_values=-1)
    mine_slots = tr(mine_slots, (1, 0, 2))

    def group(v):
        two = jnp.stack([v, swap(v, 2)])
        return jnp.concatenate([two, swap(two, 1)], axis=0)

    all_slots = lax.dynamic_slice_in_dim(group(mine_slots), q * EL, EL, axis=1)
    counts = jnp.max(all_slots, axis=(2, 3)) + 1
    steps = (counts + 15) // 16 * 16
    offs = jnp.concatenate([jnp.zeros((1, EL), jnp.int32), jnp.cumsum(steps, axis=0)], axis=0)
    offs = tr(offs).reshape(-1).astype(jnp.int32)
    all_sets = group(image_set).reshape(-1)
    cots = group(cotangent)

    ef = jnp.concatenate([up_first, tr(down_second, (0, 2, 1))], axis=2)
    ef = lax.all_gather(ef, AXES, axis=0, tiled=False)
    ef = lax.dynamic_slice_in_dim(ef, q * EL, EL, axis=1)
    ef = tr(ef, (1, 0, 2, 3)).reshape(EL, D, 2 * AC)
    u1, d2 = ef[:, :, 0:AC], ef[:, :, AC:]

    qkv, att, mid, x2, ad, probs = attention_forward(block_in, image_set, gains, wq, wk, wv, wo, b4, a2t, rm)
    x2s = group(x2)
    gates = lax.dynamic_slice_in_dim(tr(group(jnp.pad(probs, ((0, 8 - IMG), (0, 0), (0, 0)))), (0, 2, 1, 3)), q * EL, EL, axis=1)

    xa, ga, mk = dispatch(offs, all_sets, all_slots, gates, x2s, cots, u1, d2)

    accs, gus, gds = [], [], []
    for e in range(EL):
        w = jnp.stack(parts[e])
        a1, a2, gu, gd = expert_part(e, offs, xa, ga, w.reshape(-1, 2 * CAP, 2 * DW), None)
        accs.append((a1, a2))
        shape = (AC, w.shape[0], GRP, hs)
        unroll = lambda v: tr(v, (1, 0, 2)).reshape(shape)
        gus.append(unroll(gu))
        gds.append(unroll(gd))

    ysum, gsum, dots, gud, gdu = combine(offs, (q * EL).reshape(1), accs, xa, ga, mk, u1, d2, all_slots, gates, cots)

    def home(v, dt):
        half = v[0:2].astype(F32) + swap(v[2:4], 1).astype(F32)
        return half[0] + swap(half[1].astype(dt), 2).astype(F32)

    gin = home(gsum, BF)
    dots = home(dots, F32)
    ymine = home(ysum, BF).astype(BF)

    block_out, input_grad, acc = backward(image_set, image_live, block_in, cotangent, gin, dots, probs, mid, ymine, qkv, att, x2, ad,
                                          gains, wq, wk, wv, wo, b4, a2t, rm)

    eg = jnp.stack([jnp.stack(gus), jnp.stack(gds)])
    pieces = [eg[:, :, :, j] for j in range(eg.shape[3])]
    for n, axis, perm in reversed(rings):
        back = [(b, a) for a, b in perm]
        cut = len(pieces) // n
        rows = [pieces[k * cut:(k + 1) * cut] for k in range(n)]
        total = rows[n - 1]
        for k in range(n - 2, -1, -1):
            total = [(lax.ppermute(v, axis, back).astype(F32) + u.astype(F32)).astype(BF) for v, u in zip(total, rows[k])]
        pieces = total
    piece = pieces[0]

    def owners(v):
        sib = swap(v[2:4], 1)
        near = jnp.stack([v[0], sib[0]])
        far = swap(jnp.stack([v[1], sib[1]]), 2)
        got = jnp.concatenate([near, far], axis=0)
        order = [0, 1, 2, 3]
        at = jnp.stack([q ^ j for j in order])
        place = jnp.argsort(at)
        return jnp.take(got, place, axis=0)

    eg = owners(tr(piece, (3, 0, 1, 2, 4)))
    eg = tr(eg, (1, 0, 2, 3, 4)).reshape(2, NE, AC, hs).astype(F32)

    ff = jnp.stack([gud, gdu])
    ff = ff.reshape(2, EL, ng, GRP, fsn, r, AC)
    ff = jnp.moveaxis(ff, 3, 0)
    ff = jnp.stack([lax.dynamic_index_in_dim(ff, q ^ j, 0, keepdims=False) for j in rel])
    ff = lax.psum_scatter(ff, "fsdp", scatter_dimension=4, tiled=False)
    held = ff
    for _ in range(ng - 1):
        held = lax.ppermute(held, "dp", rings[2][2])
        ff = ff + held
    ff = lax.dynamic_index_in_dim(ff, d // GRP, 3, keepdims=False)
    ff = owners(ff)
    ff = tr(ff, (1, 0, 2, 3, 4)).reshape(2, NE, r, AC).astype(F32)

    per = lambda v, k: v.reshape(ndev, k * r, AC)
    nrs = router_second.shape[0]
    rs = tr(acc[7 * D:7 * D + NE, :]).reshape(ndev, nrs)
    rs = jnp.pad(rs, ((0, 0), (0, AC - nrs)))[:, None]
    sm = jnp.concatenate([per(acc[0:D], 1), per(acc[D:4 * D], 3), per(acc[4 * D:5 * D], 1), per(acc[5 * D:6 * D], 1),
                          per(acc[6 * D:7 * D], 1), rs, jnp.zeros((ndev, 7, AC), F32)], axis=1)
    sm = lax.psum_scatter(sm.astype(BF), AXES, scatter_dimension=0, tiled=False).astype(F32)
    return (
        block_out,
        input_grad,
        sm[0:r],
        tr(sm[r:4 * r]),
        sm[4 * r:5 * r],
        tr(sm[5 * r:6 * r]),
        sm[6 * r:7 * r],
        sm[7 * r, 0:nrs],
        ff[0],
        eg[0],
        eg[1],
        tr(ff[1], (0, 2, 1)),
    )


def solution(mesh):
    dpn, fsn = mesh.shape["dp"], mesh.shape["fsdp"]
    both = ("dp", "fsdp")
    return jax.shard_map(
        functools.partial(on_device, dpn, fsn),
        mesh=mesh,
        in_specs=(
            P(both, None, None),
            P(both, None, None),
            P(both),
            P(both),
            P(both, None, None),
            P(both, None, None),
            P(both),
            P(both),
            P(both, None),
            P(both, None),
            P(both, None),
            P(None, None, both),
            P(None, None, both),
            P(both, None),
            P(None, both),
            P(both, None),
            P(None, both),
            P(both, None),
            P(both),
            P(None, both, None),
            P(None, None, both),
            P(None, None, both),
            P(None, None, both),
        ),
        out_specs=(
            P(both, None, None),
            P(both, None, None),
            P(both, None),
            P(None, both),
            P(both, None),
            P(None, both),
            P(both, None),
            P(both),
            P(None, both, None),
            P(None, None, both),
            P(None, None, both),
            P(None, None, both),
        ),
        check_vma=False,
    )
```

```python
import functools
import math

import jax
import jax.numpy as jnp
from jax import lax
from jax.experimental import pallas as pl
from jax.experimental.pallas import tpu as pltpu
from jax.sharding import PartitionSpec as P

D = 768
HEADS = 12
HEAD = 64
NE = 8
LEN = 197
LP = 208
SL = 256
AC = 128
RANK = 16
CAP = 384
IMG = 5
GRP = 4
EL = NE // GRP
ROWS = GRP * CAP
RT = 256
DW = D + AC
WIN = 256
LG = LP + 16
EPS = 1e-06
F32 = jnp.float32
BF = jnp.bfloat16
AXES = ("dp", "fsdp")
VMEM = 60 * 1000 * 1024


def nn(a, b):
    return lax.dot_general(a, b, (((1,), (0,)), ((), ())), preferred_element_type=F32)


def nt(a, b):
    return lax.dot_general(a, b, (((1,), (1,)), ((), ())), preferred_element_type=F32)


def adapter_mask(rows, which):
    lane = lax.broadcasted_iota(jnp.int32, (rows, AC), 1)
    return jnp.where(lane // RANK == which, 1.0, 0.0).astype(F32)


def norm_parts(v):
    mean = jnp.mean(v, axis=-1, keepdims=True)
    cen = v - mean
    var = jnp.mean(cen * cen, axis=-1, keepdims=True)
    inv = lax.rsqrt(var + EPS)
    return cen * inv, inv


def norm_back(g, unit, inv, gain):
    s = g * gain
    return inv * (
        s
        - jnp.mean(s, axis=-1, keepdims=True)
        - unit * jnp.mean(s * unit, axis=-1, keepdims=True)
    )


def params(n):
    return pltpu.CompilerParams(dimension_semantics=("arbitrary",) * n, vmem_limit_bytes=VMEM)


def cost(us):
    return pl.CostEstimate(flops=int(us * 1.15e9), transcendentals=0, bytes_accessed=0)


def whole(shape):
    zeros = (0,) * len(shape)
    return pl.BlockSpec(shape, lambda *_: zeros, pipeline_mode=pl.Buffered(1))


def per_image(shape):
    rest = (0,) * (len(shape) - 1)
    return pl.BlockSpec(shape, lambda i, *_: (i,) + rest)


def fwd_kernel(sets, x_ref, g_ref, wq, wk, wv, wo, b4, a2t, rm, qkv_ref, att_ref, mid_ref, x2_ref, ad_ref, pr_ref, hid):
    mask = adapter_mask(LP, sets[pl.program_id(0)])
    hid[...] = jnp.zeros((LP, D), F32)
    hid[0:LEN, :] = x_ref[0].astype(F32)
    hidden = hid[...]
    unit, _ = norm_parts(hidden)
    x1 = (unit * g_ref[0:1, :]).astype(BF)
    aq = (mask * nn(x1, b4[:, 0:AC])).astype(BF)
    ad_ref[0, :, 0:AC] = aq
    for j, w in enumerate((wq, wk, wv)):
        part = nn(x1, w[...]) + nt(aq, a2t[j * D:(j + 1) * D, :])
        qkv_ref[0, :, j * D:(j + 1) * D] = part.astype(BF)
    lane = lax.broadcasted_iota(jnp.int32, (LP, 2 * HEAD), 1)
    keyok = lax.broadcasted_iota(jnp.int32, (LP, LP), 1) < LEN
    scale = 1.0 / math.sqrt(HEAD)
    for h in range(HEADS // 2):
        at = h * 2 * HEAD
        q = qkv_ref[0, :, at:at + 2 * HEAD]
        k = qkv_ref[0, :, D + at:D + at + 2 * HEAD]
        v = qkv_ref[0, :, 2 * D + at:2 * D + at + 2 * HEAD]
        outs = []
        for half in range(2):
            mine = (lane >= HEAD) if half else (lane < HEAD)
            s = nt(jnp.where(mine, q, jnp.zeros_like(q)), k) * scale
            s = jnp.where(keyok, s, -1e30)
            e = jnp.exp(s - jnp.max(s, axis=-1, keepdims=True))
            p = e * (1.0 / jnp.sum(e, axis=-1, keepdims=True))
            outs.append(nn(p.astype(BF), v))
        att_ref[0, :, at:at + 2 * HEAD] = jnp.where(lane < HEAD, outs[0], outs[1]).astype(BF)
    att = att_ref[0]
    ao = (mask * nn(att, b4[:, AC:2 * AC])).astype(BF)
    ad_ref[0, :, AC:2 * AC] = ao
    middle = hidden + nn(att, wo[...]) + nt(ao, b4[:, 3 * AC:4 * AC])
    mid_ref[0] = middle
    unit2, _ = norm_parts(middle)
    x2 = (unit2 * g_ref[1:2, :]).astype(BF)
    x2_ref[0] = x2
    ar = (mask * nn(x2, b4[:, 2 * AC:3 * AC])).astype(BF)
    ad_ref[0, :, 2 * AC:3 * AC] = ar
    logits = nn(x2, b4[:, 4 * AC:5 * AC]) + nn(ar, rm[...])
    elane = lax.broadcasted_iota(jnp.int32, (LP, AC), 1)
    logits = jnp.where(elane < NE, logits, -1e30)
    e = jnp.exp(logits - jnp.max(logits, axis=-1, keepdims=True))
    probs = e * (1.0 / jnp.sum(e, axis=-1, keepdims=True))
    padded = jnp.concatenate([probs, jnp.zeros((SL - LP, AC), F32)], axis=0)
    pr_ref[0] = jnp.transpose(padded)[0:NE, :]


def attention_forward(block_in, sets, gains, wq, wk, wv, wo, b4, a2t, rm):
    n = block_in.shape[0]
    sq = whole((D, D))
    return pl.pallas_call(
        fwd_kernel,
        grid_spec=pltpu.PrefetchScalarGridSpec(
            num_scalar_prefetch=1,
            grid=(n,),
            in_specs=[per_image((1, LEN, D)), whole((8, D)), sq, sq, sq, sq, sq, whole((3 * D, AC)), whole((AC, AC))],
            out_specs=[
                per_image((1, LP, 3 * D)),
                per_image((1, LP, D)),
                per_image((1, LP, D)),
                per_image((1, LP, D)),
                per_image((1, LP, 3 * AC)),
                per_image((1, NE, SL)),
            ],
            scratch_shapes=[pltpu.VMEM((LP, D), F32)],
        ),
        out_shape=[
            jax.ShapeDtypeStruct((n, LP, 3 * D), BF),
            jax.ShapeDtypeStruct((n, LP, D), BF),
            jax.ShapeDtypeStruct((n, LP, D), F32),
            jax.ShapeDtypeStruct((n, LP, D), BF),
            jax.ShapeDtypeStruct((n, LP, 3 * AC), BF),
            jax.ShapeDtypeStruct((n, NE, SL), F32),
        ],
        compiler_params=params(1),
        cost_estimate=cost(28),
        name="attention_forward",
    )(sets, block_in, gains, wq, wk, wv, wo, b4, a2t, rm)


def window(base, first, limit):
    at = jnp.minimum(base + first // 16 * 16, limit - WIN)
    return pl.multiple_of(at, 16)


def fetch_blocks(at_start, b, sets):
    def copies(k):
        return [pltpu.make_async_copy(refs[k], buf.at[k], sems.at[k]) for refs, buf, sems in sets]

    @pl.when(at_start)
    def _():
        for k in range(GRP):
            for c in copies(k):
                c.start()

    for k in range(GRP):
        @pl.when(b == k)
        def _(k=k):
            for c in copies(k):
                c.wait()


def dispatch_kernel(offs, firsts, sets, slot_ref, gate_ref, *refs):
    x2_refs, cot_refs = refs[0:GRP], refs[GRP:2 * GRP]
    u1_ref, d2_ref, xa_ref, ga_ref, mk_ref, acc, cpad, x2_buf, cot_buf, x2_sem, cot_sem = refs[2 * GRP:]
    e = pl.program_id(0)
    b = pl.program_id(1)

    @pl.when(e == 0)
    def _():
        fetch_blocks(b == 0, b, ((x2_refs, x2_buf, x2_sem), (cot_refs, cot_buf, cot_sem)))

    @pl.when(b == 0)
    def _():
        xa_ref[...] = jnp.zeros_like(xa_ref)
        ga_ref[...] = jnp.zeros_like(ga_ref)
        mk_ref[...] = jnp.zeros_like(mk_ref)

    acc[...] = jnp.zeros_like(acc)
    cpad[...] = jnp.zeros_like(cpad)
    gcol = jnp.transpose(gate_ref[0, 0])
    rows = lax.broadcasted_iota(jnp.int32, (WIN, LP), 0)
    for i in range(IMG):
        first = firsts[(b * EL + e) * IMG + i]

        @pl.when(first < CAP)
        def _():
            at = window(0, first, CAP)
            here = pl.ds(at, WIN)
            pick = jnp.where(rows + at == slot_ref[0, 0, i:i + 1, 0:LP], 1.0, 0.0).astype(BF)
            cpad[0:LEN, :] = cot_buf[b, i].astype(F32)
            gg = (cpad[...] * gcol[0:LP, i:i + 1]).astype(BF)
            acc[here, 0:D] += nn(pick, x2_buf[b, i])
            acc[here, D:2 * D] += nn(pick, gg)
            acc[here, 2 * D:] += nn(pick, adapter_mask(LP, sets[b * IMG + i]).astype(BF))

    mk = acc[:, 2 * D:]
    xs = acc[:, 0:D].astype(BF)
    gs = acc[:, D:2 * D].astype(BF)
    at = pl.multiple_of(offs[e * (GRP + 1) + b], 16)
    here = pl.ds(at, CAP)
    xa_ref[0, here, 0:D] = xs
    xa_ref[0, here, D:DW] = (mk * nn(xs, u1_ref[0])).astype(BF)
    ga_ref[0, here, 0:D] = gs
    ga_ref[0, here, D:DW] = (mk * nn(gs, d2_ref[0])).astype(BF)
    mk_ref[0, here, :] = mk.astype(BF)


def dispatch(offs, firsts, sets, slots, gates, x2, cot, u1, d2):
    return pl.pallas_call(
        dispatch_kernel,
        grid_spec=pltpu.PrefetchScalarGridSpec(
            num_scalar_prefetch=3,
            grid=(EL, GRP),
            in_specs=[
                pl.BlockSpec((1, 1, 8, SL), lambda e, b, *_: (b, e, 0, 0)),
                pl.BlockSpec((1, 1, 8, SL), lambda e, b, *_: (b, e, 0, 0)),
            ] + [pl.BlockSpec(memory_space=pl.ANY)] * (2 * GRP) + [
                pl.BlockSpec((1, D, AC), lambda e, b, *_: (e, 0, 0)),
                pl.BlockSpec((1, D, AC), lambda e, b, *_: (e, 0, 0)),
            ],
            out_specs=[
                pl.BlockSpec((1, ROWS, DW), lambda e, b, *_: (e, 0, 0)),
                pl.BlockSpec((1, ROWS, DW), lambda e, b, *_: (e, 0, 0)),
                pl.BlockSpec((1, ROWS, AC), lambda e, b, *_: (e, 0, 0)),
            ],
            scratch_shapes=[
                pltpu.VMEM((CAP, 2 * D + AC), F32), pltpu.VMEM((LP, D), F32), pltpu.VMEM((GRP, IMG, LP, D), BF),
                pltpu.VMEM((GRP, IMG, LEN, D), BF), pltpu.SemaphoreType.DMA((GRP,)), pltpu.SemaphoreType.DMA((GRP,)),
            ],
        ),
        out_shape=[
            jax.ShapeDtypeStruct((EL, ROWS, DW), BF),
            jax.ShapeDtypeStruct((EL, ROWS, DW), BF),
            jax.ShapeDtypeStruct((EL, ROWS, AC), BF),
        ],
        compiler_params=params(2),
        cost_estimate=cost(1),
        name="dispatch",
    )(offs, firsts, sets, slots, gates, *x2, *cot, u1, d2)


def flip(v):
    return jnp.transpose(v.astype(F32)).astype(BF)


def gelu_parts(pre):
    c0 = math.sqrt(2.0 / math.pi)
    sq = pre * pre
    th = jnp.tanh(c0 * pre * (1.0 + 0.044715 * sq))
    half = 0.5 * (1.0 + th)
    slope = half + 0.5 * pre * (1.0 - th * th) * (c0 * (1.0 + 3 * 0.044715 * sq))
    return pre * half, slope


def fetch_weights(pieces, wbuf, sems, pairs):
    s = pl.program_id(0) * pairs + pl.program_id(1)
    hp = pieces[0].shape[1]

    def copy(t, half):
        e, p = divmod(t, pairs)
        src = pieces[2 * p + half].at[e]
        return pltpu.make_async_copy(src, wbuf.at[t % 2, pl.ds(half * hp, hp)], sems.at[t, half])

    @pl.when(s == 0)
    def _():
        copy(0, 0).start()
        copy(0, 1).start()

    for t in range(EL * pairs):
        @pl.when(s == t)
        def _(t=t):
            if t + 1 < EL * pairs:
                copy(t + 1, 0).start()
                copy(t + 1, 1).start()
            copy(t, 0).wait()
            copy(t, 1).wait()

    return s % 2


def expert_first_kernel(pairs, offs, xa_ref, ga_ref, *refs):
    pieces = refs[:2 * pairs]
    a1, a2, go_ref, at_ref, wbuf, sems = refs[2 * pairs:]
    e = pl.program_id(0)
    total = offs[e * (GRP + 1) + GRP]
    tiles = (total + (RT - 1)) // RT
    cur = fetch_weights(pieces, wbuf, sems, pairs)

    @pl.when(pl.program_id(1) == 0)
    def _():
        a1[...] = jnp.zeros_like(a1)
        a2[...] = jnp.zeros_like(a2)
        at_ref[0] = flip(xa_ref[0, :, D:DW])
        at_ref[1] = flip(ga_ref[0, :, D:DW])

    acc_u = jnp.zeros((AC, wbuf.shape[1]), F32)

    def step(t, carry):
        gu, gd = carry
        here = pl.ds(pl.multiple_of(t * RT, RT), RT)
        wu = wbuf[cur, :, 0:DW]
        wd = wbuf[cur, :, DW:2 * DW]
        pre = nt(xa_ref[0, here, :], wu)
        gact = nt(ga_ref[0, here, :], wd)
        act, slope = gelu_parts(pre)
        act = act.astype(BF)
        gp = (slope * gact).astype(BF)
        a1[0, here, :] += nn(act, wd)
        a2[0, here, :] += nn(gp, wu)
        return gu + nn(at_ref[0, :, here], gp), gd + nn(at_ref[1, :, here], act)

    gu, gd = lax.fori_loop(0, tiles, step, (acc_u, acc_u))
    go_ref[0, 0, 0] = jnp.transpose(gu).astype(BF)
    go_ref[0, 0, 1] = jnp.transpose(gd).astype(BF)


def expert_first(offs, xa, ga, pieces):
    pairs = len(pieces) // 2
    hp = pieces[0].shape[1]
    rows = pl.BlockSpec((1, ROWS, DW), lambda e, p, *_: (e, 0, 0))
    anyspace = pl.BlockSpec(memory_space=pl.ANY)
    return pl.pallas_call(
        functools.partial(expert_first_kernel, pairs),
        grid_spec=pltpu.PrefetchScalarGridSpec(
            num_scalar_prefetch=1,
            grid=(EL, pairs),
            in_specs=[rows, rows] + [anyspace] * len(pieces),
            out_specs=[rows, rows, pl.BlockSpec((1, 1, 2, 2 * hp, AC), lambda e, p, *_: (p, e, 0, 0, 0))],
            scratch_shapes=[pltpu.VMEM((2, AC, ROWS), BF), pltpu.VMEM((2, 2 * hp, 2 * DW), BF), pltpu.SemaphoreType.DMA((EL * pairs, 2))],
        ),
        out_shape=[
            jax.ShapeDtypeStruct((EL, ROWS, DW), F32),
            jax.ShapeDtypeStruct((EL, ROWS, DW), F32),
            jax.ShapeDtypeStruct((pairs, EL, 2, 2 * hp, AC), BF),
        ],
        compiler_params=params(2),
        cost_estimate=cost(56),
        name="expert_first",
    )(offs, xa, ga, *pieces)


def expert_last_kernel(offs, xa_ref, ga_ref, mk_ref, p1, p2, u1_ref, d2_ref, w0, w1, ob_ref, gb_ref, go_ref, gf_ref,
                       wbuf, sems):
    e = pl.program_id(0)
    total = offs[e * (GRP + 1) + GRP]
    tiles = (total + (RT - 1)) // RT
    cur = fetch_weights((w0, w1), wbuf, sems, 1)
    ob_ref[...] = jnp.zeros_like(ob_ref)
    gb_ref[...] = jnp.zeros_like(gb_ref)
    hb = wbuf.shape[1]

    def step(t, carry):
        gu, gd, gud, gdu = carry
        here = pl.ds(pl.multiple_of(t * RT, RT), RT)
        wu = wbuf[cur, :, 0:DW]
        wd = wbuf[cur, :, DW:2 * DW]
        x = xa_ref[0, here, :]
        g = ga_ref[0, here, :]
        pre = nt(x, wu)
        gact = nt(g, wd)
        act, slope = gelu_parts(pre)
        act = act.astype(BF)
        gp = (slope * gact).astype(BF)
        t1 = p1[0, here, :] + nn(act, wd)
        t2 = p2[0, here, :] + nn(gp, wu)
        mk = mk_ref[0, here, :].astype(F32)
        adt = (mk * t1[:, D:DW]).astype(BF)
        aut = (mk * t2[:, D:DW]).astype(BF)
        ob_ref[0, here, :] = (t1[:, 0:D] + nt(adt, d2_ref[0])).astype(BF)
        gb_ref[0, here, :] = (t2[:, 0:D] + nt(aut, u1_ref[0])).astype(BF)
        return (gu + nn(flip(x[:, D:DW]), gp), gd + nn(flip(g[:, D:DW]), act),
                gud + nn(flip(aut), x[:, 0:D]), gdu + nn(flip(adt), g[:, 0:D]))

    zero = jnp.zeros((AC, hb), F32)
    zed = jnp.zeros((AC, D), F32)
    gu, gd, gud, gdu = lax.fori_loop(0, tiles, step, (zero, zero, zed, zed))
    go_ref[0, 0] = jnp.transpose(gu).astype(BF)
    go_ref[0, 1] = jnp.transpose(gd).astype(BF)
    gf_ref[0, 0] = jnp.transpose(gud).astype(BF)
    gf_ref[0, 1] = jnp.transpose(gdu).astype(BF)


def expert_last(offs, xa, ga, mk, a1, a2, u1, d2, pieces):
    hp = pieces[0].shape[1]
    each = lambda *shape: pl.BlockSpec((1,) + shape, lambda e, p, *_: (e,) + (0,) * len(shape))
    anyspace = pl.BlockSpec(memory_space=pl.ANY)
    return pl.pallas_call(
        expert_last_kernel,
        grid_spec=pltpu.PrefetchScalarGridSpec(
            num_scalar_prefetch=1,
            grid=(EL, 1),
            in_specs=[each(ROWS, DW), each(ROWS, DW), each(ROWS, AC), each(ROWS, DW), each(ROWS, DW), each(D, AC), each(D, AC),
                      anyspace, anyspace],
            out_specs=[each(ROWS, D), each(ROWS, D), each(2, 2 * hp, AC), each(2, D, AC)],
            scratch_shapes=[pltpu.VMEM((2, 2 * hp, 2 * DW), BF), pltpu.SemaphoreType.DMA((EL, 2))],
        ),
        out_shape=[
            jax.ShapeDtypeStruct((EL, ROWS, D), BF),
            jax.ShapeDtypeStruct((EL, ROWS, D), BF),
            jax.ShapeDtypeStruct((EL, 2, 2 * hp, AC), BF),
            jax.ShapeDtypeStruct((EL, 2, D, AC), BF),
        ],
        compiler_params=params(2),
        cost_estimate=cost(34),
        name="expert_last",
    )(offs, xa, ga, mk, a1, a2, u1, d2, *pieces)


def combine_kernel(lo, n, offs, firsts, first_expert, ob, gb, slot_ref, gate_ref, *refs):
    b = pl.program_id(0)
    cot_refs, outs = refs[:GRP], refs[GRP:]
    y_ref, g_ref, cot_buf, cot_sem = outs[6:]
    fetch_blocks(b == 0, b, (([r.at[lo:lo + n] for r in cot_refs], cot_buf, cot_sem),))
    lanes = lax.broadcasted_iota(jnp.int32, (LP, WIN), 1)
    dlane = lax.broadcasted_iota(jnp.int32, (LP, AC), 1)
    scol = [jnp.transpose(slot_ref[0, e].astype(F32)) for e in range(EL)]
    gcol = [jnp.transpose(gate_ref[0, e]) for e in range(EL)]
    for i in range(n):
        y = jnp.zeros((LP, D), F32)
        g = jnp.zeros((LP, D), F32)
        dots = jnp.zeros((LP, AC), F32)
        cot = jnp.concatenate([cot_buf[b, i].astype(F32), jnp.zeros((LP - LEN, D), F32)], axis=0)
        for e in range(EL):
            first = jnp.minimum(firsts[(b * EL + e) * IMG + lo + i], CAP - 1)
            base = offs[e * (GRP + 1) + b]
            at = window(base, first, ROWS)
            here = pl.ds(at, WIN)
            slot = scol[e][0:LP, lo + i:lo + i + 1]
            pick = jnp.where(slot == (lanes + (at - base)).astype(F32), 1.0, 0.0).astype(BF)
            ye = nn(pick, ob[e, here, :])
            g = g + nn(pick, gb[e, here, :])
            y = y + gcol[e][0:LP, lo + i:lo + i + 1] * ye
            dot = jnp.sum(ye * cot, axis=-1, keepdims=True)
            dots = dots + jnp.where(dlane == first_expert[0] + e, dot, 0.0)
        y_ref[i] = y.astype(BF)
        g_ref[i, 0:LP] = g.astype(BF)
        full = jnp.transpose(jnp.concatenate([dots, jnp.zeros((SL - LP, AC), F32)], axis=0))[0:16, :]
        high = full.astype(BF)
        g_ref[i, LP:LG, 0:SL] = high
        g_ref[i, LP:LG, SL:2 * SL] = (full - high.astype(F32)).astype(BF)
        g_ref[i, LP:LG, 2 * SL:] = jnp.zeros((LG - LP, D - 2 * SL), BF)
    for v, mine, far, core in ((y_ref, outs[0], outs[1], outs[2]), (g_ref, outs[3], outs[4], outs[5])):
        for when, ref in ((0, mine), (1, far), (2, core), (3, core)):
            @pl.when(b == when)
            def _(ref=ref, v=v):
                if len(ref.shape) == 4:
                    ref[0] = v[...]
                else:
                    ref[...] = v[...]


def combine(lo, n, offs, firsts, first_expert, ob, gb, slots, gates, cot):
    block = lambda *shape: pl.BlockSpec((1,) + shape, lambda b, *_: (b,) + (0,) * len(shape))
    return pl.pallas_call(
        functools.partial(combine_kernel, lo, n),
        grid_spec=pltpu.PrefetchScalarGridSpec(
            num_scalar_prefetch=3,
            grid=(GRP,),
            in_specs=[whole((EL, ROWS, D)), whole((EL, ROWS, D)), block(EL, 8, SL), block(EL, 8, SL)] + [pl.BlockSpec(memory_space=pl.ANY)] * GRP,
            out_specs=[spec for rows in (LP, LG) for spec in (
                whole((n, rows, D)), whole((n, rows, D)), pl.BlockSpec((1, n, rows, D), lambda b, *_: (jnp.maximum(b - 2, 0), 0, 0, 0)))],
            scratch_shapes=[pltpu.VMEM((n, LP, D), BF), pltpu.VMEM((n, LG, D), BF), pltpu.VMEM((GRP, n, LEN, D), BF),
                            pltpu.SemaphoreType.DMA((GRP,))],
        ),
        out_shape=[jax.ShapeDtypeStruct(shape, BF) for rows in (LP, LG) for shape in ((n, rows, D), (n, rows, D), (2, n, rows, D))],
        compiler_params=params(1),
        cost_estimate=cost(6 * n),
        name="combine",
    )(offs, firsts, first_expert, ob, gb, slots, gates, *cot)


def bwd_kernel(lo, last, r, sets, live, order, x_ref, cot_ref, go_ref, gc_ref, gy_ref, pr_ref, mid_ref, qkv_ref, att_ref, x2_ref, ad_ref, g_ref,
               wq, wk, wv, wo, b4, a2t, rm, *refs):
    if last:
        pacc, _, ig_ref, mine_ref, other_ref, hid, gq, acc, flat = refs
    else:
        ig_ref, acc_ref, hid, gq, acc = refs
    i = pl.program_id(0) + lo
    mask = adapter_mask(LP, sets[i])
    alive = live[i].astype(F32)
    aq = ad_ref[0, :, 0:AC]
    ao = ad_ref[0, :, AC:2 * AC]
    ar = ad_ref[0, :, 2 * AC:3 * AC]

    @pl.when(i == lo)
    def _():
        acc[...] = pacc[...] if lo else jnp.zeros_like(acc)

    tr = flip
    gsum = go_ref[0].astype(F32) + gc_ref[0, 0].astype(F32) + gy_ref[0].astype(F32)
    dots = gsum[LP:LP + NE, 0:SL] + gsum[LP:LP + NE, SL:2 * SL]

    hid[...] = jnp.zeros((LP, D), F32)
    hid[0:LEN, :] = cot_ref[0].astype(F32) * alive
    gfin = hid[...]
    elane = lax.broadcasted_iota(jnp.int32, (LP, AC), 1)
    zrow = jnp.zeros((AC - NE, SL), F32)
    probs = jnp.transpose(jnp.concatenate([pr_ref[0], zrow], axis=0))[0:LP, :]
    gprobs = jnp.transpose(jnp.concatenate([dots, zrow], axis=0))[0:LP, :]
    gl = probs * (gprobs - jnp.sum(gprobs * probs, axis=-1, keepdims=True))
    gl = jnp.where(elane < NE, gl, 0.0).astype(BF)
    gar = (mask * nt(gl, rm[...])).astype(BF)
    gtwo = gsum[0:LP] + nt(gl, b4[:, 4 * AC:5 * AC]) + nt(gar, b4[:, 2 * AC:3 * AC])
    middle = mid_ref[0]
    unit2, inv2 = norm_parts(middle)
    gmid = gfin + norm_back(gtwo, unit2, inv2, g_ref[1:2, :])
    gbr = gmid.astype(BF)
    gao = (mask * nn(gbr, b4[:, 3 * AC:4 * AC])).astype(BF)
    gatt = (nt(gbr, wo[...]) + nt(gao, b4[:, AC:2 * AC])).astype(BF)
    gart = tr(gar)
    acc[:, 4 * D:5 * D] += nn(tr(gao), att_ref[0])
    acc[:, 5 * D:6 * D] += nn(tr(ao), gbr)
    acc[:, 6 * D:7 * D] += nn(gart, x2_ref[0])
    acc[:, 7 * D:] += nn(tr(ar), gl)

    lane = lax.broadcasted_iota(jnp.int32, (LP, 2 * HEAD), 1)
    keyok = lax.broadcasted_iota(jnp.int32, (LP, LP), 0) < LEN
    drow = lax.broadcasted_iota(jnp.int32, (2 * HEAD, LP), 0)
    scale = 1.0 / math.sqrt(HEAD)
    for h in range(HEADS // 2):
        at = h * 2 * HEAD
        q = qkv_ref[0, :, at:at + 2 * HEAD]
        k = qkv_ref[0, :, D + at:D + at + 2 * HEAD]
        v = qkv_ref[0, :, 2 * D + at:2 * D + at + 2 * HEAD]
        go = gatt[:, at:at + 2 * HEAD]
        kt = tr(k)
        dq, dk, dv = [], [], []
        for half in range(2):
            mine = (lane >= HEAD) if half else (lane < HEAD)
            s = nt(k, jnp.where(mine, q, jnp.zeros_like(q))) * scale
            s = jnp.where(keyok, s, -1e30)
            ex = jnp.exp(s - jnp.max(s, axis=0, keepdims=True))
            p = ex * (1.0 / jnp.sum(ex, axis=0, keepdims=True))
            dv.append(nn(p.astype(BF), go))
            dp = nt(v, jnp.where(mine, go, jnp.zeros_like(go)))
            gs = (p * (dp - jnp.sum(dp * p, axis=0, keepdims=True))).astype(BF)
            dk.append(nn(gs, q))
            dq.append(nn(kt, gs))
        dqt = jnp.where(drow < HEAD, dq[0], dq[1]) * scale
        gq[:, at:at + 2 * HEAD] = jnp.transpose(dqt).astype(BF)
        gq[:, D + at:D + at + 2 * HEAD] = (jnp.where(lane < HEAD, dk[0], dk[1]) * scale).astype(BF)
        gq[:, 2 * D + at:2 * D + at + 2 * HEAD] = jnp.where(lane < HEAD, dv[0], dv[1]).astype(BF)
    gqkv = gq[...]
    gaq = (mask * nn(gqkv, a2t[...])).astype(BF)
    hid[...] = jnp.zeros((LP, D), F32)
    hid[0:LEN, :] = x_ref[0].astype(F32)
    unit1, inv1 = norm_parts(hid[...])
    x1 = (unit1 * g_ref[0:1, :]).astype(BF)
    acc[:, 0:D] += nn(tr(gaq), x1)
    acc[:, D:4 * D] += nn(tr(aq), gqkv)
    gone = nt(gaq, b4[:, 0:AC])
    for j, w in enumerate((wq, wk, wv)):
        gone = gone + nt(gqkv[:, j * D:(j + 1) * D], w[...])
    ig = gmid + norm_back(gone, unit1, inv1, g_ref[0:1, :])
    ig_ref[0] = ig[0:LEN, :].astype(BF)

    @pl.when(pl.program_id(0) == pl.num_programs(0) - 1)
    def _():
        if not last:
            acc_ref[...] = acc[...]
            return
        for c in range(acc.shape[1] // AC):
            flat[c * AC:(c + 1) * AC, :] = jnp.transpose(acc[:, c * AC:(c + 1) * AC])
        half = mine_ref.shape[0]

        def place(p, carry):
            for ref, at in ((mine_ref, 0), (other_ref, half)):
                dev = order[at + p]
                row, base = 0, 0
                for w in (1, 3, 1, 1, 1):
                    here = pl.ds(pl.multiple_of(base + w * r * dev, 8), w * r)
                    ref[p, row:row + w * r, :] = flat[here, :].astype(BF)
                    row += w * r
                    base += w * D
                ref[p, row:row + NE, :] = flat[7 * D:7 * D + NE, :].astype(BF)
            return carry

        lax.fori_loop(0, half, place, 0)


def backward(lo, n, ndev, sets, live, order, block_in, cot, g, gc, gy, probs, mid, qkv, att, x2, ad, gains, wq, wk, wv, wo, b4, a2t,
             rm, prev):
    sq = whole((D, D))
    na = 7 * D + AC
    r = D // ndev
    last = lo > 0
    packed = (ndev // 2, 7 * r + NE, AC)

    def image(*shape):
        return pl.BlockSpec((1,) + shape, lambda i, *_: (i + lo,) + (0,) * len(shape))

    part = lambda *shape: pl.BlockSpec((1, 1) + shape, lambda i, *_: (0, i) + (0,) * len(shape))
    in_specs = [
        image(LEN, D), image(LEN, D), per_image((1, LG, D)), part(LG, D), per_image((1, LG, D)), image(NE, SL),
        image(LP, D), image(LP, 3 * D), image(LP, D), image(LP, D),
        image(LP, 3 * AC), whole((8, D)), sq, sq, sq, sq, sq, whole((3 * D, AC)), whole((AC, AC)),
    ]
    args = [block_in, cot, g, gc, gy, probs, mid, qkv, att, x2, ad, gains, wq, wk, wv, wo, b4, a2t, rm]
    scratch = [pltpu.VMEM((LP, D), F32), pltpu.VMEM((LP, 3 * D), BF), pltpu.VMEM((AC, na), F32)]
    alias = {}
    if last:
        in_specs += [whole((AC, na)), pl.BlockSpec(memory_space=pl.ANY)]
        args += [prev[1], prev[0]]
        alias = {3 + len(args) - 1: 0}
        scratch.append(pltpu.VMEM((na, AC), F32))
        tails = [packed, packed]
    else:
        tails = [(AC, na)]
    return pl.pallas_call(
        functools.partial(bwd_kernel, lo, last, r),
        grid_spec=pltpu.PrefetchScalarGridSpec(
            num_scalar_prefetch=3,
            grid=(n,),
            in_specs=in_specs,
            out_specs=[image(LEN, D)] + [whole(t) for t in tails],
            scratch_shapes=scratch,
        ),
        out_shape=[jax.ShapeDtypeStruct(block_in.shape, BF)] + [jax.ShapeDtypeStruct(t, BF if last else F32) for t in tails],
        input_output_aliases=alias,
        compiler_params=params(1),
        cost_estimate=cost(12 * n),
        name="backward",
    )(sets, live, order, *args)


def on_device(dpn, fsn, block_in, cotangent, image_live, image_set, expert_routes, expert_slots, gain_attn, gain_moe, w_qkv, w_out,
              w_router, w_up, w_down, qkv_first, qkv_second, out_first, out_second, router_first, router_second, up_first,
              up_second, down_first, down_second):
    ndev = dpn * fsn
    nx = 1 << ((fsn.bit_length() - 1) // 2)
    nz = fsn // nx
    ng = dpn // GRP
    r = D // ndev
    hs = w_up.shape[2]
    d = lax.axis_index("dp")
    q = d % GRP
    rings = [
        (nz, "fsdp", [(f, ((f // nx + 1) % nz) * nx + f % nx) for f in range(fsn)]),
        (nx, "fsdp", [(f, (f // nx) * nx + (f % nx + 1) % nx) for f in range(fsn)]),
        (ng, "dp", [(a, (a + GRP) % dpn) for a in range(dpn)]),
    ]

    def swap(v, bit):
        return lax.ppermute(v, "dp", [(a, a ^ bit) for a in range(dpn)])

    rel = [0, 2, 1, 3]

    tr = jnp.transpose
    small = jnp.concatenate(
        [
            qkv_first, out_first, router_first, tr(out_second),
            jnp.concatenate([w_router, gain_attn[:, None], gain_moe[:, None], jnp.zeros((r, AC - NE - 2), BF)], axis=1),
            jnp.zeros((r, AC), BF).at[0, 0:router_second.shape[0]].set(router_second),
        ],
        axis=1,
    )
    a2s = tr(qkv_second).reshape(3, r, AC)
    second = jnp.concatenate([a2s[0], a2s[1], a2s[2], jnp.zeros((r, 3 * AC), BF)], axis=1)
    front = jnp.stack([w_qkv[:, 0:D], w_qkv[:, D:2 * D], w_qkv[:, 2 * D:], w_out, small, second])
    front = lax.all_gather(front.reshape(6 * r, D), AXES, axis=0, tiled=True).reshape(ndev, 6, r, D)
    wq, wk, wv, wo, b4 = (front[:, j].reshape(D, D) for j in range(5))
    a2t = tr(front[:, 5, :, 0:3 * AC].reshape(ndev, r, 3, AC), (0, 2, 1, 3)).reshape(3 * D, AC)
    gains = jnp.concatenate(
        [b4[:, 4 * AC + NE].reshape(1, D), b4[:, 4 * AC + NE + 1].reshape(1, D), jnp.zeros((6, D), BF)], axis=0
    ).astype(F32)
    rm = front[:, 4, 0, 5 * AC:5 * AC + router_second.shape[0]].reshape(AC, NE)
    rm = jnp.pad(rm, ((0, 0), (0, AC - NE)))

    after = lambda v, *deps: lax.optimization_barrier((v,) + deps)[0]

    ef = jnp.concatenate([up_first, tr(down_second, (0, 2, 1))], axis=2).reshape(GRP, EL, r, 2 * AC)
    own = [lax.dynamic_index_in_dim(ef, q ^ j, 0, keepdims=False) for j in range(GRP)]
    sib_ef = swap(jnp.stack([own[1], own[3]]), 1)
    got_ef = swap(jnp.stack([own[2], sib_ef[1]]), 2)
    mine_ef = jnp.stack([own[0], sib_ef[0], got_ef[0], got_ef[1]])
    wpk = jnp.concatenate([tr(w_up, (0, 2, 1)), tr(up_second, (0, 2, 1)), tr(w_down, (0, 2, 1)), tr(down_first, (0, 2, 1))], axis=2)
    wpk = wpk.reshape(GRP, EL, hs, 2 * DW)
    own = [lax.dynamic_index_in_dim(wpk, q ^ j, 0, keepdims=False) for j in range(GRP)]
    sib = swap(jnp.stack([own[1], own[3]], axis=1), 1)
    near = jnp.stack([own[0], sib[:, 0]], axis=1).reshape(EL, 2 * hs, 2 * DW)
    send, _ = lax.optimization_barrier((jnp.stack([own[2], sib[:, 1]], axis=1), got_ef))
    got = swap(send, 2)
    far = got.reshape(EL, 2 * hs, 2 * DW)

    def hop(v, ring):
        return lax.ppermute(v, ring[1], ring[2])

    up = [[(u, ((u // nx + k) % nz) * nx + u % nx) for u in range(fsn)] for k in range(nz)]
    all_ef = jnp.concatenate([mine_ef] + [lax.ppermute(mine_ef, "fsdp", up[k]) for k in range(1, nz)])
    near, all_ef = lax.optimization_barrier((near, all_ef))
    for n, axis, perm in rings[1:]:
        rows = [all_ef]
        for _ in range(n - 1):
            rows.append(lax.ppermute(rows[-1], axis, perm))
        all_ef = jnp.concatenate(rows)
    near_x, all_ef = lax.optimization_barrier((near, all_ef))
    zn, xn, far = lax.optimization_barrier((hop(near, rings[0]), hop(near_x, rings[1]), far))
    z_row = [jnp.concatenate([near, far], axis=1), jnp.concatenate([zn, hop(far, rings[0])], axis=1)]
    x_row = [jnp.concatenate([xn, hop(far, rings[1])], axis=1)]
    z0, x0, block_in_late = lax.optimization_barrier((z_row[1], x_row[0], block_in))
    z_row[1], x_row[0] = z0, x0
    route = expert_routes.reshape(IMG, LEN, 2)
    slot = expert_slots.reshape(IMG, LEN, 2)
    ids = jnp.arange(NE, dtype=jnp.int32)[None, :, None, None]
    ok = (route[:, None] == ids) & (slot[:, None] >= 0) & (image_live[:, None, None, None] > 0)
    mine_slots = jnp.max(jnp.where(ok, slot[:, None], -1), axis=-1)
    mine_slots = jnp.pad(mine_slots, ((0, 8 - IMG), (0, 0), (0, SL - LEN)), constant_values=-1)
    mine_slots = tr(mine_slots, (1, 0, 2))

    def members(v):
        far = swap(v, 2)
        return [v, far, swap(v, 1), swap(far, 1)]

    def group(v):
        return jnp.stack(members(v))

    all_slots = lax.dynamic_slice_in_dim(group(mine_slots), q * EL, EL, axis=1)
    counts = jnp.max(all_slots, axis=(2, 3)) + 1
    steps = (counts + 15) // 16 * 16
    offs = jnp.concatenate([jnp.zeros((1, EL), jnp.int32), jnp.cumsum(steps, axis=0)], axis=0)
    offs = tr(offs).reshape(-1).astype(jnp.int32)
    firsts = jnp.min(jnp.where(all_slots >= 0, all_slots, CAP), axis=3)[:, :, 0:IMG].reshape(-1)
    all_sets = group(image_set).reshape(-1)
    cots = members(after(cotangent, got))

    f = lax.axis_index("fsdp")
    devs = jnp.arange(ndev, dtype=jnp.int32)
    dd, df = devs // fsn, devs % fsn
    gap = lambda mine, other, n: (mine - other) % n
    spot = (gap(d // GRP, dd // GRP, ng) * nx + gap(f % nx, df % nx, nx)) * nz + gap(f // nx, df // nx, nz)
    ef = jnp.take(all_ef, spot * GRP + ((dd % GRP) ^ q), axis=0)
    ef = tr(ef, (1, 0, 2, 3)).reshape(EL, D, 2 * AC)
    u1, d2 = ef[:, :, 0:AC], ef[:, :, AC:]

    offs, firsts, all_sets, block_in_late, *cots = lax.optimization_barrier((offs, firsts, all_sets, block_in_late, *cots))
    qkv, att, mid, x2, ad, probs = attention_forward(block_in_late, image_set, gains, wq, wk, wv, wo, b4, a2t, rm)
    for k in range(2, nz):
        z_row.append(hop(z_row[-1], rings[0]))
        x_row.append(hop(z_row[k - 1], rings[1]))
        if k == 2:
            z_row[k], x_row[k - 1], x2s = lax.optimization_barrier((z_row[k], x_row[k - 1], x2))
    x2s = members(x2s)
    gates = lax.dynamic_slice_in_dim(tr(group(jnp.pad(probs, ((0, 8 - IMG), (0, 0), (0, 0)))), (0, 2, 1, 3)), q * EL, EL, axis=1)

    xa, ga, mk = dispatch(offs, firsts, all_sets, all_slots, gates, x2s, cots, u1, d2)
    z_row[-1], x_row[-1], xa = lax.optimization_barrier((z_row[-1], x_row[-1], xa))
    x_row.append(hop(z_row[nz - 1], rings[1]))
    rows = [z_row, x_row]
    for _ in range(2, nx):
        rows.append([hop(v, rings[1]) for v in rows[-1]])
    held = [v for row in rows for v in row]
    rows = [held]
    for _ in range(1, ng):
        rows.append([hop(v, rings[2]) for v in rows[-1]])
    held = [v for row in rows for v in row]
    join = len(held) // 8
    pieces = [held[k] if join == 1 else jnp.concatenate(held[k * join:(k + 1) * join], axis=1) for k in range(8)]
    a1, a2, go = expert_first(offs, xa, ga, pieces[:6])
    go = [go[k] for k in range(3)]
    ob, gb, gl, gf = expert_last(offs, xa, ga, mk, a1, a2, u1, d2, pieces[6:])

    k = jnp.arange(ng * nx * nz, dtype=jnp.int32)
    kg, kx, kz = k // (nx * nz), k // nz % nx, k % nz
    column = (f // nx - kz) % nz * nx + (f % nx - kx) % nx
    rank = ((d // GRP - kg) % ng * GRP)[:, None] + (q ^ jnp.arange(GRP, dtype=jnp.int32))[None, :]
    spot = (rank * fsn + column[:, None]).reshape(-1)
    gf = jnp.take(gf.reshape(EL, 2, ndev, r, AC), spot, axis=2).reshape(EL, 2, ng * nx, nz * GRP * r, AC)
    simple = ng == 1 and nx == 2
    xback = [(v, u) for u, v in rings[1][2]]
    if simple:
        near_x = lax.ppermute(go[2], "fsdp", xback)
        near_x, ob = lax.optimization_barrier((near_x, ob))
        far_x = lax.ppermute(jnp.concatenate([gl, gf[:, :, 1]], axis=2), "fsdp", xback)

    fe = (q * EL).reshape(1)
    cut = 2
    parts = []
    for lo, n in ((0, cut), (cut, IMG - cut)):
        ym, yf, yp, gm, gfar, gp = combine(lo, n, offs, firsts, fe, ob, gb, all_slots, gates, cots)
        gc = swap(gp, 1)
        gs = (gfar.astype(F32) + gc[1].astype(F32)).astype(BF)
        gc, ob = lax.optimization_barrier((gc, ob))
        parts.append((lo, n, (ym, yf, yp), gm, gc, swap(gs, 2)))

    (lo, n, ya, ga1, gca, gya), (lo2, n2, yb, gb1, gcb, gyb) = parts
    spots = jnp.arange(ndev, dtype=jnp.int32)
    order = (q ^ jnp.array([0, 2, 1, 3], jnp.int32)[spots // fsn % GRP]) * fsn + (f + spots % fsn) % fsn
    order = (order if ng == 1 else spots).astype(jnp.int32)
    yca = swap(ya[2], 1)
    ycb = swap(yb[2], 1)
    add = lambda u, v: (u.astype(F32) + v.astype(F32)).astype(BF)
    ga1, gcb = lax.optimization_barrier((ga1, gcb))
    shared = (probs, mid, qkv, att, x2, ad, gains, wq, wk, wv, wo, b4, a2t, rm)
    first = backward(lo, n, ndev, image_set, image_live, order, block_in, cotangent, ga1, gca, gya, *shared, None)

    head, gyb, yca, ycb = lax.optimization_barrier((first[0], gyb, yca, ycb))
    ysend = jnp.concatenate([add(ya[1], yca[1]), add(yb[1], ycb[1])], axis=0)
    if simple:
        near_x, far_x, _ = lax.optimization_barrier((near_x, far_x, gyb))
        cut = GRP * hs
        s0 = add(go[0], near_x)
        s1 = add(go[1], far_x[:, :, 0:2 * cut])
        sf = add(gf[:, :, 0], far_x[:, :, 2 * cut:])
        hid = [s0[:, :, 0:cut], s0[:, :, cut:], s1[:, :, 0:cut], s1[:, :, cut:]]
        cols = [jnp.concatenate([hid[k], sf[:, :, k * GRP * r:(k + 1) * GRP * r]], axis=2) for k in range(nz)]
    else:
        cut = go[0].shape[2] * 4 // (ng * nx * nz)
        cols = []
        for k, v in enumerate(p for pair in go + [gl] for p in jnp.split(pair, pair.shape[2] // cut, axis=2)):
            at = k % nz * GRP * r
            cols.append(jnp.concatenate([v, gf[:, :, k // nz, at:at + GRP * r]], axis=2))
        for m, axis, perm in rings[2:0:-1]:
            back = [(v, u) for u, v in perm]
            part = len(cols) // m
            rows = [cols[k * part:(k + 1) * part] for k in range(m)]
            cols = rows[m - 1]
            for k in range(m - 2, -1, -1):
                cols = [add(lax.ppermute(v, axis, back), u) for v, u in zip(cols, rows[k])]
    down = [lax.ppermute(cols[k], "fsdp", [(u, ((u // nx - k) % nz) * nx + u % nx) for u in range(fsn)]) for k in range(1, nz)]
    yy = swap(ysend, 2)
    input_grad, mine, other = backward(lo2, n2, ndev, image_set, image_live, order, block_in, cotangent, gb1, gcb, gyb, *shared,
                                       (head, first[1]))
    mine, other, yy, *down = lax.optimization_barrier((mine, other, yy, *down))
    yya, yyb = yy[0:n], yy[n:]

    eg = (cols[0].astype(F32) + sum(v.astype(F32) for v in down)).astype(BF)
    eg = [jnp.concatenate([eg[:, :, j * hs:(j + 1) * hs], eg[:, :, GRP * hs + j * r:GRP * hs + (j + 1) * r]], axis=2) for j in range(GRP)]
    sib = swap(jnp.stack([eg[1], eg[3]]), 1)
    got = swap(jnp.stack([eg[2], sib[1]]), 2)
    got = jnp.concatenate([eg[0][None], sib[0:1], got], axis=0)
    at = jnp.stack([q ^ j for j in range(GRP)])
    eg = jnp.take(got, jnp.argsort(at), axis=0).reshape(NE, 2, hs + r, AC).astype(F32)
    ff = eg[:, :, hs:]
    eg = tr(eg[:, :, 0:hs], (1, 0, 3, 2))
    outs = []
    for at, m, y, yc, yy in ((lo, n, ya, yca, yya), (lo2, n2, yb, ycb, yyb)):
        total = mid[at:at + m] + y[0].astype(F32) + yc[0].astype(F32) + yy.astype(F32)
        outs.append(total[:, 0:LEN])
    block_out = (jnp.concatenate(outs, axis=0) * image_live.astype(F32)[:, None, None]).astype(BF)

    nrs = router_second.shape[0]
    if ng == 1:
        got = swap(other, 1)
        far = swap(add(mine[fsn:], got[fsn:]), 2)
        sm = add(add(mine[0:fsn], got[0:fsn]), far)
        total = sm[0].astype(F32)
        for k in range(1, fsn):
            perm = [(u, (u + k) % fsn) for u in range(fsn)]
            total = total + lax.ppermute(sm[k], "fsdp", perm).astype(F32)
        sm = total
    else:
        sm = jnp.concatenate([mine, other], axis=0)
        sm = lax.psum_scatter(sm, AXES, scatter_dimension=0, tiled=False).astype(F32)
    rs = tr(sm[7 * r:7 * r + NE]).reshape(-1)
    rs = lax.dynamic_slice_in_dim(rs, (d * fsn + f) * nrs, nrs)
    return (
        block_out,
        input_grad,
        sm[0:r],
        tr(sm[r:4 * r]),
        sm[4 * r:5 * r],
        tr(sm[5 * r:6 * r]),
        sm[6 * r:7 * r],
        rs,
        ff[:, 0],
        eg[0],
        eg[1],
        tr(ff[:, 1], (0, 2, 1)),
    )


def solution(mesh):
    dpn, fsn = mesh.shape["dp"], mesh.shape["fsdp"]
    both = ("dp", "fsdp")
    return jax.shard_map(
        functools.partial(on_device, dpn, fsn),
        mesh=mesh,
        in_specs=(
            P(both, None, None),
            P(both, None, None),
            P(both),
            P(both),
            P(both, None, None),
            P(both, None, None),
            P(both),
            P(both),
            P(both, None),
            P(both, None),
            P(both, None),
            P(None, None, both),
            P(None, None, both),
            P(both, None),
            P(None, both),
            P(both, None),
            P(None, both),
            P(both, None),
            P(both),
            P(None, both, None),
            P(None, None, both),
            P(None, None, both),
            P(None, None, both),
        ),
        out_specs=(
            P(both, None, None),
            P(both, None, None),
            P(both, None),
            P(None, both),
            P(both, None),
            P(None, both),
            P(both, None),
            P(both),
            P(None, both, None),
            P(None, None, both),
            P(None, None, both),
            P(None, None, both),
        ),
        check_vma=False,
    )
```

```python
import functools
import math

import jax
import jax.numpy as jnp
from jax import lax
from jax.experimental import pallas as pl
from jax.experimental.pallas import tpu as pltpu
from jax.sharding import PartitionSpec as P

D = 768
HEADS = 12
HEAD = 64
NE = 8
LEN = 197
LP = 208
SL = 256
AC = 128
RANK = 16
CAP = 384
IMG = 5
GRP = 4
EL = NE // GRP
ROWS = GRP * CAP
RT = 256
DW = D + AC
WIN = 256
NFIRST = 7
LG = LP + 16
EPS = 1e-06
F32 = jnp.float32
BF = jnp.bfloat16
AXES = ("dp", "fsdp")
VMEM = 60 * 1000 * 1024


def nn(a, b):
    return lax.dot_general(a, b, (((1,), (0,)), ((), ())), preferred_element_type=F32)


def nt(a, b):
    return lax.dot_general(a, b, (((1,), (1,)), ((), ())), preferred_element_type=F32)


def adapter_mask(rows, which):
    lane = lax.broadcasted_iota(jnp.int32, (rows, AC), 1)
    return jnp.where(lane // RANK == which, 1.0, 0.0).astype(F32)


def norm_parts(v):
    mean = jnp.mean(v, axis=-1, keepdims=True)
    cen = v - mean
    var = jnp.mean(cen * cen, axis=-1, keepdims=True)
    inv = lax.rsqrt(var + EPS)
    return cen * inv, inv


def norm_back(g, unit, inv, gain):
    s = g * gain
    return inv * (
        s
        - jnp.mean(s, axis=-1, keepdims=True)
        - unit * jnp.mean(s * unit, axis=-1, keepdims=True)
    )


def params(n):
    return pltpu.CompilerParams(dimension_semantics=("arbitrary",) * n, vmem_limit_bytes=VMEM)


def cost(us):
    return pl.CostEstimate(flops=int(us * 1.15e9), transcendentals=0, bytes_accessed=0)


def whole(shape):
    zeros = (0,) * len(shape)
    return pl.BlockSpec(shape, lambda *_: zeros, pipeline_mode=pl.Buffered(1))


def per_image(shape):
    rest = (0,) * (len(shape) - 1)
    return pl.BlockSpec(shape, lambda i, *_: (i,) + rest)


def fwd_kernel(sets, x_ref, g_ref, wq, wk, wv, wo, b4, a2t, rm, qkv_ref, att_ref, mid_ref, x2_ref, ad_ref, pr_ref, hid):
    mask = adapter_mask(LP, sets[pl.program_id(0)])
    hid[...] = jnp.zeros((LP, D), F32)
    hid[0:LEN, :] = x_ref[0].astype(F32)
    hidden = hid[...]
    unit, _ = norm_parts(hidden)
    x1 = (unit * g_ref[0:1, :]).astype(BF)
    aq = (mask * nn(x1, b4[:, 0:AC])).astype(BF)
    ad_ref[0, :, 0:AC] = aq
    for j, w in enumerate((wq, wk, wv)):
        part = nn(x1, w[...]) + nt(aq, a2t[j * D:(j + 1) * D, :])
        qkv_ref[0, :, j * D:(j + 1) * D] = part.astype(BF)
    lane = lax.broadcasted_iota(jnp.int32, (LP, 2 * HEAD), 1)
    keyok = lax.broadcasted_iota(jnp.int32, (LP, LP), 1) < LEN
    scale = 1.0 / math.sqrt(HEAD)
    for h in range(HEADS // 2):
        at = h * 2 * HEAD
        q = qkv_ref[0, :, at:at + 2 * HEAD]
        k = qkv_ref[0, :, D + at:D + at + 2 * HEAD]
        v = qkv_ref[0, :, 2 * D + at:2 * D + at + 2 * HEAD]
        outs = []
        for half in range(2):
            mine = (lane >= HEAD) if half else (lane < HEAD)
            s = nt(jnp.where(mine, q, jnp.zeros_like(q)), k) * scale
            s = jnp.where(keyok, s, -1e30)
            e = jnp.exp(s - jnp.max(s, axis=-1, keepdims=True))
            p = e * (1.0 / jnp.sum(e, axis=-1, keepdims=True))
            outs.append(nn(p.astype(BF), v))
        att_ref[0, :, at:at + 2 * HEAD] = jnp.where(lane < HEAD, outs[0], outs[1]).astype(BF)
    att = att_ref[0]
    ao = (mask * nn(att, b4[:, AC:2 * AC])).astype(BF)
    ad_ref[0, :, AC:2 * AC] = ao
    middle = hidden + nn(att, wo[...]) + nt(ao, b4[:, 3 * AC:4 * AC])
    mid_ref[0] = middle
    unit2, _ = norm_parts(middle)
    x2 = (unit2 * g_ref[1:2, :]).astype(BF)
    x2_ref[0] = x2
    ar = (mask * nn(x2, b4[:, 2 * AC:3 * AC])).astype(BF)
    ad_ref[0, :, 2 * AC:3 * AC] = ar
    logits = nn(x2, b4[:, 4 * AC:5 * AC]) + nn(ar, rm[...])
    elane = lax.broadcasted_iota(jnp.int32, (LP, AC), 1)
    logits = jnp.where(elane < NE, logits, -1e30)
    e = jnp.exp(logits - jnp.max(logits, axis=-1, keepdims=True))
    probs = e * (1.0 / jnp.sum(e, axis=-1, keepdims=True))
    padded = jnp.concatenate([probs, jnp.zeros((SL - LP, AC), F32)], axis=0)
    pr_ref[0] = jnp.transpose(padded)[0:NE, :]


def attention_forward(block_in, sets, gains, wq, wk, wv, wo, b4, a2t, rm):
    n = block_in.shape[0]
    sq = whole((D, D))
    return pl.pallas_call(
        fwd_kernel,
        grid_spec=pltpu.PrefetchScalarGridSpec(
            num_scalar_prefetch=1,
            grid=(n,),
            in_specs=[per_image((1, LEN, D)), whole((8, D)), sq, sq, sq, sq, sq, whole((3 * D, AC)), whole((AC, AC))],
            out_specs=[
                per_image((1, LP, 3 * D)),
                per_image((1, LP, D)),
                per_image((1, LP, D)),
                per_image((1, LP, D)),
                per_image((1, LP, 3 * AC)),
                per_image((1, NE, SL)),
            ],
            scratch_shapes=[pltpu.VMEM((LP, D), F32)],
        ),
        out_shape=[
            jax.ShapeDtypeStruct((n, LP, 3 * D), BF),
            jax.ShapeDtypeStruct((n, LP, D), BF),
            jax.ShapeDtypeStruct((n, LP, D), F32),
            jax.ShapeDtypeStruct((n, LP, D), BF),
            jax.ShapeDtypeStruct((n, LP, 3 * AC), BF),
            jax.ShapeDtypeStruct((n, NE, SL), F32),
        ],
        compiler_params=params(1),
        cost_estimate=cost(28),
        name="attention_forward",
    )(sets, block_in, gains, wq, wk, wv, wo, b4, a2t, rm)


def window(base, first, limit):
    at = jnp.minimum(base + first // 16 * 16, limit - WIN)
    return pl.multiple_of(at, 16)


def fetch_blocks(at_start, b, sets):
    def copies(k):
        return [pltpu.make_async_copy(refs[k], buf.at[k], sems.at[k]) for refs, buf, sems in sets]

    @pl.when(at_start)
    def _():
        for k in range(GRP):
            for c in copies(k):
                c.start()

    for k in range(GRP):
        @pl.when(b == k)
        def _(k=k):
            for c in copies(k):
                c.wait()


def dispatch_kernel(offs, firsts, sets, slot_ref, gate_ref, *refs):
    x2_refs, cot_refs = refs[0:GRP], refs[GRP:2 * GRP]
    u1_ref, d2_ref, xa_ref, ga_ref, mk_ref, acc, cpad, x2_buf, cot_buf, x2_sem, cot_sem = refs[2 * GRP:]
    e = pl.program_id(0)
    b = pl.program_id(1)

    @pl.when(e == 0)
    def _():
        fetch_blocks(b == 0, b, ((x2_refs, x2_buf, x2_sem), (cot_refs, cot_buf, cot_sem)))

    @pl.when(b == 0)
    def _():
        xa_ref[...] = jnp.zeros_like(xa_ref)
        ga_ref[...] = jnp.zeros_like(ga_ref)
        mk_ref[...] = jnp.zeros_like(mk_ref)

    acc[...] = jnp.zeros_like(acc)
    cpad[...] = jnp.zeros_like(cpad)
    gcol = jnp.transpose(gate_ref[0, 0])
    rows = lax.broadcasted_iota(jnp.int32, (WIN, LP), 0)
    for i in range(IMG):
        first = firsts[(b * EL + e) * IMG + i]

        @pl.when(first < CAP)
        def _():
            at = window(0, first, CAP)
            here = pl.ds(at, WIN)
            pick = jnp.where(rows + at == slot_ref[0, 0, i:i + 1, 0:LP], 1.0, 0.0).astype(BF)
            cpad[0:LEN, :] = cot_buf[b, i].astype(F32)
            gg = (cpad[...] * gcol[0:LP, i:i + 1]).astype(BF)
            acc[here, 0:D] += nn(pick, x2_buf[b, i])
            acc[here, D:2 * D] += nn(pick, gg)
            acc[here, 2 * D:] += nn(pick, adapter_mask(LP, sets[b * IMG + i]).astype(BF))

    mk = acc[:, 2 * D:]
    xs = acc[:, 0:D].astype(BF)
    gs = acc[:, D:2 * D].astype(BF)
    at = pl.multiple_of(offs[e * (GRP + 1) + b], 16)
    here = pl.ds(at, CAP)
    xa_ref[0, here, 0:D] = xs
    xa_ref[0, here, D:DW] = (mk * nn(xs, u1_ref[0])).astype(BF)
    ga_ref[0, here, 0:D] = gs
    ga_ref[0, here, D:DW] = (mk * nn(gs, d2_ref[0])).astype(BF)
    mk_ref[0, here, :] = mk.astype(BF)


def dispatch(offs, firsts, sets, slots, gates, x2, cot, u1, d2):
    return pl.pallas_call(
        dispatch_kernel,
        grid_spec=pltpu.PrefetchScalarGridSpec(
            num_scalar_prefetch=3,
            grid=(EL, GRP),
            in_specs=[
                pl.BlockSpec((1, 1, 8, SL), lambda e, b, *_: (b, e, 0, 0)),
                pl.BlockSpec((1, 1, 8, SL), lambda e, b, *_: (b, e, 0, 0)),
            ] + [pl.BlockSpec(memory_space=pl.ANY)] * (2 * GRP) + [
                pl.BlockSpec((1, D, AC), lambda e, b, *_: (e, 0, 0)),
                pl.BlockSpec((1, D, AC), lambda e, b, *_: (e, 0, 0)),
            ],
            out_specs=[
                pl.BlockSpec((1, ROWS, DW), lambda e, b, *_: (e, 0, 0)),
                pl.BlockSpec((1, ROWS, DW), lambda e, b, *_: (e, 0, 0)),
                pl.BlockSpec((1, ROWS, AC), lambda e, b, *_: (e, 0, 0)),
            ],
            scratch_shapes=[
                pltpu.VMEM((CAP, 2 * D + AC), F32), pltpu.VMEM((LP, D), F32), pltpu.VMEM((GRP, IMG, LP, D), BF),
                pltpu.VMEM((GRP, IMG, LEN, D), BF), pltpu.SemaphoreType.DMA((GRP,)), pltpu.SemaphoreType.DMA((GRP,)),
            ],
        ),
        out_shape=[
            jax.ShapeDtypeStruct((EL, ROWS, DW), BF),
            jax.ShapeDtypeStruct((EL, ROWS, DW), BF),
            jax.ShapeDtypeStruct((EL, ROWS, AC), BF),
        ],
        compiler_params=params(2),
        cost_estimate=cost(1),
        name="dispatch",
    )(offs, firsts, sets, slots, gates, *x2, *cot, u1, d2)


def flip(v):
    return jnp.transpose(v.astype(F32)).astype(BF)


def gelu_parts(pre):
    c0 = math.sqrt(2.0 / math.pi)
    sq = pre * pre
    th = jnp.tanh(c0 * pre * (1.0 + 0.044715 * sq))
    half = 0.5 * (1.0 + th)
    slope = half + 0.5 * pre * (1.0 - th * th) * (c0 * (1.0 + 3 * 0.044715 * sq))
    return pre * half, slope


def tile_products(x, g, xt, gt, wbuf, cur, width, put):
    wu = wbuf[cur, 0:width, 0:DW]
    wd = wbuf[cur, 0:width, DW:2 * DW]
    act, slope = gelu_parts(nt(x, wu))
    act = act.astype(BF)
    gp = (slope * nt(g, wd)).astype(BF)
    t1, t2 = nn(act, wd), nn(gp, wu)
    put(nn(xt, gp), nn(gt, act))
    return t1, t2


def tall_tiles(offs, e):
    total = offs[e * (GRP + 1) + GRP]
    tall = (total + RT - 1) // (2 * RT)
    return tall, (total > tall * 2 * RT).astype(jnp.int32)


def live_tiles(offs, e):
    tall, tail = tall_tiles(offs, e)
    return 2 * tall + tail


def over_tiles(offs, e, step):
    tall, tail = tall_tiles(offs, e)

    def one(t, carry):
        step(2 * t, 2)
        return carry

    lax.fori_loop(0, tall, one, 0)

    @pl.when(tail > 0)
    def _():
        step(2 * tall, 1)


def each_tile(limit, do):
    for t in range(ROWS // RT):
        @pl.when(t < limit)
        def _(t=t):
            do(t)


def unit_copies(units, wbuf, slot, sems, s, e):
    hu = units[0].shape[1]
    return [pltpu.make_async_copy(u.at[e], wbuf.at[slot, pl.ds(k * hu, hu)], sems.at[s, k]) for k, u in enumerate(units)]


def expert_first_kernel(offs, xa, ga, *refs):
    units = refs[:NFIRST]
    a1, a2, go_ref, gh_ref, xb, gb, s1, s2, at_ref, wbuf, gacc, wsem, isem, osem = refs[NFIRST:]
    chunks = [units[k:k + 2] for k in range(0, NFIRST, 2)]
    steps = len(chunks)
    e, p = pl.program_id(0), pl.program_id(1)
    s = e * steps + p
    full, short = 2 * units[0].shape[1], units[0].shape[1]

    def rows(t):
        return pl.ds(t * RT, RT)

    def incoming(v, t):
        return [pltpu.make_async_copy(src.at[v, rows(t)], dst.at[v, rows(t)], isem.at[v, t, k])
                for k, (src, dst) in enumerate(((xa, xb), (ga, gb)))]

    def outgoing(v, t):
        return [pltpu.make_async_copy(src.at[v, rows(t)], dst.at[v, rows(t)], osem.at[v, t, k])
                for k, (src, dst) in enumerate(((s1, a1), (s2, a2)))]

    def weights(k):
        return unit_copies(chunks[k % steps], wbuf, k % 2, wsem, k, k // steps)

    @pl.when(s == 0)
    def _():
        for c in weights(0):
            c.start()
        for v in range(EL):
            each_tile(live_tiles(offs, v), lambda t, v=v: [c.start() for c in incoming(v, t)])

    for k in range(EL * steps):
        @pl.when(s == k)
        def _(k=k):
            if k + 1 < EL * steps:
                for c in weights(k + 1):
                    c.start()
            if k % steps == 0:
                each_tile(live_tiles(offs, k // steps), lambda t: [c.wait() for c in incoming(k // steps, t)])
            for c in weights(k):
                c.wait()

    tiles = live_tiles(offs, e)
    cur = s % 2

    @pl.when(p == 0)
    def _():
        def turn(t, carry):
            here = pl.ds(pl.multiple_of(t * RT, RT), RT)
            at_ref[0, :, here] = flip(xb[e, here, D:DW])
            at_ref[1, :, here] = flip(gb[e, here, D:DW])
            s1[e, here, :] = jnp.zeros((RT, DW), F32)
            s2[e, here, :] = jnp.zeros((RT, DW), F32)
            return carry

        lax.fori_loop(0, tiles, turn, 0)

    def run(width, ref):
        gacc[:, :, 0:width] = jnp.zeros((2, AC, width), F32)

        def put(gu, gd):
            gacc[0, :, 0:width] += gu
            gacc[1, :, 0:width] += gd

        def step(t, height):
            here = pl.ds(pl.multiple_of(t * RT, RT), height * RT)
            t1, t2 = tile_products(xb[e, here, :], gb[e, here, :], at_ref[0, :, here], at_ref[1, :, here], wbuf, cur, width, put)
            s1[e, here, :] += t1
            s2[e, here, :] += t2

        over_tiles(offs, e, step)
        for k in range(2):
            ref[k] = jnp.transpose(gacc[k, :, 0:width]).astype(BF)

    @pl.when(p < steps - 1)
    def _():
        run(full, go_ref.at[0, 0])

    @pl.when(p == steps - 1)
    def _():
        run(short, gh_ref.at[0])
        for v in range(EL):
            @pl.when(e == v)
            def _(v=v):
                each_tile(tiles, lambda t: [c.start() for c in outgoing(v, t)])

    @pl.when(s == EL * steps - 1)
    def _():
        for v in range(EL):
            each_tile(live_tiles(offs, v), lambda t, v=v: [c.wait() for c in outgoing(v, t)])


def expert_first(offs, xa, ga, units):
    hu = units[0].shape[1]
    steps = (NFIRST + 1) // 2
    nt_ = ROWS // RT
    anyspace = pl.BlockSpec(memory_space=pl.ANY)
    return pl.pallas_call(
        expert_first_kernel,
        grid_spec=pltpu.PrefetchScalarGridSpec(
            num_scalar_prefetch=1,
            grid=(EL, steps),
            in_specs=[anyspace] * (2 + NFIRST),
            out_specs=[anyspace, anyspace,
                       pl.BlockSpec((1, 1, 2, 2 * hu, AC), lambda e, p, *_: (jnp.minimum(p, steps - 2), e, 0, 0, 0)),
                       pl.BlockSpec((1, 2, hu, AC), lambda e, p, *_: (e, 0, 0, 0))],
            scratch_shapes=[
                pltpu.VMEM((EL, ROWS, DW), BF), pltpu.VMEM((EL, ROWS, DW), BF), pltpu.VMEM((EL, ROWS, DW), F32),
                pltpu.VMEM((EL, ROWS, DW), F32), pltpu.VMEM((2, AC, ROWS), BF), pltpu.VMEM((2, 2 * hu, 2 * DW), BF),
                pltpu.VMEM((2, AC, 2 * hu), F32), pltpu.SemaphoreType.DMA((EL * steps, 2)), pltpu.SemaphoreType.DMA((EL, nt_, 2)),
                pltpu.SemaphoreType.DMA((EL, nt_, 2)),
            ],
        ),
        out_shape=[
            jax.ShapeDtypeStruct((EL, ROWS, DW), F32),
            jax.ShapeDtypeStruct((EL, ROWS, DW), F32),
            jax.ShapeDtypeStruct((steps - 1, EL, 2, 2 * hu, AC), BF),
            jax.ShapeDtypeStruct((EL, 2, hu, AC), BF),
        ],
        compiler_params=params(2),
        cost_estimate=cost(45),
        name="expert_first",
    )(offs, xa, ga, *units)


def expert_last_kernel(offs, mk_ref, u1_ref, d2_ref, xa, ga, a1, a2, w0, ob, gb, go_ref, gf_ref,
                       xs, gs, s1, s2, os, hs, wbuf, gacc, facc, wsem, isem, osem):
    e = pl.program_id(0)
    tiles = live_tiles(offs, e)

    def rows(t):
        return pl.ds(t * RT if isinstance(t, int) else pl.multiple_of(t * RT, RT), RT)

    def incoming(v, t):
        return [pltpu.make_async_copy(src.at[v, rows(t)], dst.at[v, rows(t)], isem.at[v, t, k])
                for k, (src, dst) in enumerate(((xa, xs), (ga, gs), (a1, s1), (a2, s2)))]

    def outgoing(v, t):
        return [pltpu.make_async_copy(src.at[v, rows(t)], dst.at[v, rows(t)], osem.at[v, t, k])
                for k, (src, dst) in enumerate(((os, ob), (hs, gb)))]

    def weights(v):
        return unit_copies((w0,), wbuf, v, wsem, v, v)

    @pl.when(e == 0)
    def _():
        for v in range(EL):
            for c in weights(v):
                c.start()
            each_tile(live_tiles(offs, v), lambda t, v=v: [c.start() for c in incoming(v, t)])

    gacc[...] = jnp.zeros_like(gacc)
    facc[...] = jnp.zeros_like(facc)
    for v in range(EL):
        @pl.when(e == v)
        def _(v=v):
            for c in weights(v):
                c.wait()

    def put(gu, gd):
        gacc[0] += gu
        gacc[1] += gd

    def step(t, height):
        here = pl.ds(pl.multiple_of(t * RT, RT), height * RT)
        for k in range(height):
            for c in incoming(e, t + k):
                c.wait()
        x = xs[e, here, :]
        g = gs[e, here, :]
        t1, t2 = tile_products(x, g, flip(x[:, D:DW]), flip(g[:, D:DW]), wbuf, e, wbuf.shape[1], put)
        t1 = s1[e, here, :] + t1
        t2 = s2[e, here, :] + t2
        mk = mk_ref[0, here, :].astype(F32)
        adt = (mk * t1[:, D:DW]).astype(BF)
        aut = (mk * t2[:, D:DW]).astype(BF)
        os[e, here, :] = (t1[:, 0:D] + nt(adt, d2_ref[0])).astype(BF)
        hs[e, here, :] = (t2[:, 0:D] + nt(aut, u1_ref[0])).astype(BF)
        for k in range(height):
            for c in outgoing(e, t + k):
                c.start()
        facc[0] += nn(flip(aut), x[:, 0:D])
        facc[1] += nn(flip(adt), g[:, 0:D])

    over_tiles(offs, e, step)
    @pl.when(tiles < ROWS // RT)
    def _():
        here = rows(tiles)
        os[e, here, :] = jnp.zeros((RT, D), BF)
        hs[e, here, :] = jnp.zeros((RT, D), BF)
        for c in outgoing(e, tiles):
            c.start()

    for j in range(2):
        go_ref[0, j] = jnp.transpose(gacc[j]).astype(BF)
        gf_ref[0, j] = jnp.transpose(facc[j]).astype(BF)

    @pl.when(e == EL - 1)
    def _():
        for v in range(EL):
            each_tile(live_tiles(offs, v) + 1, lambda t, v=v: [c.wait() for c in outgoing(v, t)])


def expert_last(offs, xa, ga, mk, a1, a2, u1, d2, units):
    hu = units[0].shape[1]
    nt_ = ROWS // RT
    each = lambda *shape: pl.BlockSpec((1,) + shape, lambda e, *_: (e,) + (0,) * len(shape))
    anyspace = pl.BlockSpec(memory_space=pl.ANY)
    return pl.pallas_call(
        expert_last_kernel,
        grid_spec=pltpu.PrefetchScalarGridSpec(
            num_scalar_prefetch=1,
            grid=(EL,),
            in_specs=[each(ROWS, AC), each(D, AC), each(D, AC)] + [anyspace] * 5,
            out_specs=[anyspace, anyspace, each(2, hu, AC), each(2, D, AC)],
            scratch_shapes=[
                pltpu.VMEM((EL, ROWS, DW), BF), pltpu.VMEM((EL, ROWS, DW), BF), pltpu.VMEM((EL, ROWS, DW), F32),
                pltpu.VMEM((EL, ROWS, DW), F32), pltpu.VMEM((EL, ROWS, D), BF), pltpu.VMEM((EL, ROWS, D), BF),
                pltpu.VMEM((EL, hu, 2 * DW), BF), pltpu.VMEM((2, AC, hu), F32), pltpu.VMEM((2, AC, D), F32),
                pltpu.SemaphoreType.DMA((EL, 1)), pltpu.SemaphoreType.DMA((EL, nt_, 4)), pltpu.SemaphoreType.DMA((EL, nt_, 2)),
            ],
        ),
        out_shape=[
            jax.ShapeDtypeStruct((EL, ROWS, D), BF),
            jax.ShapeDtypeStruct((EL, ROWS, D), BF),
            jax.ShapeDtypeStruct((EL, 2, hu, AC), BF),
            jax.ShapeDtypeStruct((EL, 2, D, AC), BF),
        ],
        compiler_params=params(1),
        cost_estimate=cost(18),
        name="expert_last",
    )(offs, mk, u1, d2, xa, ga, a1, a2, *units)


def combine_kernel(lo, n, offs, firsts, first_expert, ob, gb, slot_ref, gate_ref, *refs):
    b = pl.program_id(0)
    cot_refs, outs = refs[:GRP], refs[GRP:]
    y_ref, g_ref, cot_buf, cot_sem = outs[6:]
    fetch_blocks(b == 0, b, (([r.at[lo:lo + n] for r in cot_refs], cot_buf, cot_sem),))
    lanes = lax.broadcasted_iota(jnp.int32, (LP, WIN), 1)
    dlane = lax.broadcasted_iota(jnp.int32, (LP, AC), 1)
    scol = [jnp.transpose(slot_ref[0, e].astype(F32)) for e in range(EL)]
    gcol = [jnp.transpose(gate_ref[0, e]) for e in range(EL)]
    for i in range(n):
        y = jnp.zeros((LP, D), F32)
        g = jnp.zeros((LP, D), F32)
        dots = jnp.zeros((LP, AC), F32)
        cot = jnp.concatenate([cot_buf[b, i].astype(F32), jnp.zeros((LP - LEN, D), F32)], axis=0)
        for e in range(EL):
            first = firsts[(b * EL + e) * IMG + lo + i]
            first = jnp.where(first < CAP, first, 0)
            base = offs[e * (GRP + 1) + b]
            at = window(base, first, ROWS)
            here = pl.ds(at, WIN)
            slot = scol[e][0:LP, lo + i:lo + i + 1]
            pick = jnp.where(slot == (lanes + (at - base)).astype(F32), 1.0, 0.0).astype(BF)
            ye = nn(pick, ob[e, here, :])
            g = g + nn(pick, gb[e, here, :])
            y = y + gcol[e][0:LP, lo + i:lo + i + 1] * ye
            dot = jnp.sum(ye * cot, axis=-1, keepdims=True)
            dots = dots + jnp.where(dlane == first_expert[0] + e, dot, 0.0)
        y_ref[i] = y.astype(BF)
        g_ref[i, 0:LP] = g.astype(BF)
        full = jnp.transpose(jnp.concatenate([dots, jnp.zeros((SL - LP, AC), F32)], axis=0))[0:16, :]
        high = full.astype(BF)
        g_ref[i, LP:LG, 0:SL] = high
        g_ref[i, LP:LG, SL:2 * SL] = (full - high.astype(F32)).astype(BF)
        g_ref[i, LP:LG, 2 * SL:] = jnp.zeros((LG - LP, D - 2 * SL), BF)
    for v, mine, far, core in ((y_ref, outs[0], outs[1], outs[2]), (g_ref, outs[3], outs[4], outs[5])):
        for when, ref in ((0, mine), (1, far), (2, core), (3, core)):
            @pl.when(b == when)
            def _(ref=ref, v=v):
                if len(ref.shape) == 4:
                    ref[0] = v[...]
                else:
                    ref[...] = v[...]


def combine(lo, n, offs, firsts, first_expert, ob, gb, slots, gates, cot):
    block = lambda *shape: pl.BlockSpec((1,) + shape, lambda b, *_: (b,) + (0,) * len(shape))
    return pl.pallas_call(
        functools.partial(combine_kernel, lo, n),
        grid_spec=pltpu.PrefetchScalarGridSpec(
            num_scalar_prefetch=3,
            grid=(GRP,),
            in_specs=[whole((EL, ROWS, D)), whole((EL, ROWS, D)), block(EL, 8, SL), block(EL, 8, SL)] + [pl.BlockSpec(memory_space=pl.ANY)] * GRP,
            out_specs=[spec for rows in (LP, LG) for spec in (
                whole((n, rows, D)), whole((n, rows, D)), pl.BlockSpec((1, n, rows, D), lambda b, *_: (jnp.maximum(b - 2, 0), 0, 0, 0)))],
            scratch_shapes=[pltpu.VMEM((n, LP, D), BF), pltpu.VMEM((n, LG, D), BF), pltpu.VMEM((GRP, n, LEN, D), BF),
                            pltpu.SemaphoreType.DMA((GRP,))],
        ),
        out_shape=[jax.ShapeDtypeStruct(shape, BF) for rows in (LP, LG) for shape in ((n, rows, D), (n, rows, D), (2, n, rows, D))],
        compiler_params=params(1),
        cost_estimate=cost(6 * n),
        name="combine",
    )(offs, firsts, first_expert, ob, gb, slots, gates, *cot)


def bwd_kernel(lo, n, last, r, sets, live, order, go_ref, gc_ref, gy_ref, g_ref, wq, wk, wv, wo, b4, a2t, rm, *refs):
    sources, refs = refs[:8], refs[8:]
    if last:
        pacc, _, ig_ref, mine_ref, other_ref, *refs = refs
    else:
        ig_ref, acc_ref, *refs = refs
    xb, cb, pb, midb, qkvb, attb, x2b, adb, igb, hid, gin, gq, acc = refs[:13]
    flat = refs[13] if last else None
    sems, osem = refs[-2:]
    rows = n * LP
    loads = [pltpu.make_async_copy(src.at[lo:lo + n], dst, sems.at[k])
             for k, (src, dst) in enumerate(zip(sources, (xb, cb, pb, midb, qkvb, attb, x2b, adb)))]
    for c in loads:
        c.start()
    acc[...] = pacc[...] if last else jnp.zeros_like(acc)
    tr = flip
    flatten = lambda v: v.reshape(rows, v.shape[-1])
    stack = lambda f: jnp.concatenate([f(i) for i in range(n)], axis=0)
    mask = stack(lambda i: adapter_mask(LP, sets[lo + i]))
    zrow = jnp.zeros((AC - NE, SL), F32)
    gprobs = []
    for i in range(n):
        gsum = go_ref[i].astype(F32) + gc_ref[0, i].astype(F32) + gy_ref[i].astype(F32)
        gin[i * LP:(i + 1) * LP, :] = gsum[0:LP]
        dots = gsum[LP:LP + NE, 0:SL] + gsum[LP:LP + NE, SL:2 * SL]
        gprobs.append(jnp.transpose(jnp.concatenate([dots, zrow], axis=0))[0:LP, :])
    gprobs = jnp.concatenate(gprobs, axis=0)
    for c in loads:
        c.wait()

    def padded(buf, scale):
        hid[...] = jnp.zeros((rows, D), F32)
        for i in range(n):
            v = buf[i].astype(F32)
            hid[i * LP:i * LP + LEN, :] = v if scale is None else v * scale(i)
        return hid[...]

    aq = flatten(adb[:, :, 0:AC])
    ao = flatten(adb[:, :, AC:2 * AC])
    ar = flatten(adb[:, :, 2 * AC:3 * AC])
    att = flatten(attb[...])
    elane = lax.broadcasted_iota(jnp.int32, (rows, AC), 1)
    probs = stack(lambda i: jnp.transpose(jnp.concatenate([pb[i], zrow], axis=0))[0:LP, :])
    gl = probs * (gprobs - jnp.sum(gprobs * probs, axis=-1, keepdims=True))
    gl = jnp.where(elane < NE, gl, 0.0).astype(BF)
    gar = (mask * nt(gl, rm[...])).astype(BF)
    gtwo = gin[...] + nt(gl, b4[:, 4 * AC:5 * AC]) + nt(gar, b4[:, 2 * AC:3 * AC])
    unit2, inv2 = norm_parts(flatten(midb[...]))
    gin[...] = padded(cb, lambda i: live[lo + i].astype(F32)) + norm_back(gtwo, unit2, inv2, g_ref[1:2, :])
    gbr = gin[...].astype(BF)
    gao = (mask * nn(gbr, b4[:, 3 * AC:4 * AC])).astype(BF)
    gatt = (nt(gbr, wo[...]) + nt(gao, b4[:, AC:2 * AC])).astype(BF)
    acc[:, 4 * D:5 * D] += nn(tr(gao), att)
    acc[:, 5 * D:6 * D] += nn(tr(ao), gbr)
    acc[:, 6 * D:7 * D] += nn(tr(gar), flatten(x2b[...]))
    acc[:, 7 * D:] += nn(tr(ar), gl)
    attb[...] = gatt.reshape(n, LP, D)

    lane = lax.broadcasted_iota(jnp.int32, (LP, 2 * HEAD), 1)
    keyok = lax.broadcasted_iota(jnp.int32, (LP, LP), 0) < LEN
    drow = lax.broadcasted_iota(jnp.int32, (2 * HEAD, LP), 0)
    scale = 1.0 / math.sqrt(HEAD)

    def image(i, carry):
        for h in range(HEADS // 2):
            at = h * 2 * HEAD
            q = qkvb[i, :, at:at + 2 * HEAD]
            k = qkvb[i, :, D + at:D + at + 2 * HEAD]
            v = qkvb[i, :, 2 * D + at:2 * D + at + 2 * HEAD]
            go = attb[i, :, at:at + 2 * HEAD]
            kt = tr(k)
            dq, dk, dv = [], [], []
            for half in range(2):
                mine = (lane >= HEAD) if half else (lane < HEAD)
                s = nt(k, jnp.where(mine, q, jnp.zeros_like(q))) * scale
                s = jnp.where(keyok, s, -1e30)
                ex = jnp.exp(s - jnp.max(s, axis=0, keepdims=True))
                p = ex * (1.0 / jnp.sum(ex, axis=0, keepdims=True))
                dv.append(nn(p.astype(BF), go))
                dp = nt(v, jnp.where(mine, go, jnp.zeros_like(go)))
                gs = (p * (dp - jnp.sum(dp * p, axis=0, keepdims=True))).astype(BF)
                dk.append(nn(gs, q))
                dq.append(nn(kt, gs))
            dqt = jnp.where(drow < HEAD, dq[0], dq[1]) * scale
            gq[i, :, at:at + 2 * HEAD] = jnp.transpose(dqt).astype(BF)
            gq[i, :, D + at:D + at + 2 * HEAD] = (jnp.where(lane < HEAD, dk[0], dk[1]) * scale).astype(BF)
            gq[i, :, 2 * D + at:2 * D + at + 2 * HEAD] = jnp.where(lane < HEAD, dv[0], dv[1]).astype(BF)
        return carry

    lax.fori_loop(0, n, image, 0)
    gqkv = flatten(gq[...])
    gaq = (mask * nn(gqkv, a2t[...])).astype(BF)
    unit1, inv1 = norm_parts(padded(xb, None))
    x1 = (unit1 * g_ref[0:1, :]).astype(BF)
    acc[:, 0:D] += nn(tr(gaq), x1)
    acc[:, D:4 * D] += nn(tr(aq), gqkv)
    gone = nt(gaq, b4[:, 0:AC])
    for j, w in enumerate((wq, wk, wv)):
        gone = gone + nt(gqkv[:, j * D:(j + 1) * D], w[...])
    hid[...] = gin[...] + norm_back(gone, unit1, inv1, g_ref[0:1, :])
    for i in range(n):
        igb[i] = hid[i * LP:i * LP + LEN, :].astype(BF)
    out = pltpu.make_async_copy(igb, ig_ref.at[lo:lo + n], osem.at[0])
    out.start()
    if last:
        for c in range(acc.shape[1] // AC):
            flat[c * AC:(c + 1) * AC, :] = jnp.transpose(acc[:, c * AC:(c + 1) * AC])
        half = mine_ref.shape[0]

        def place(p, carry):
            for ref, at in ((mine_ref, 0), (other_ref, half)):
                dev = order[at + p]
                row, base = 0, 0
                for w in (1, 3, 1, 1, 1):
                    here = pl.ds(base + w * r * dev, w * r)
                    if r % 8 == 0:
                        here = pl.ds(pl.multiple_of(base + w * r * dev, 8), w * r)
                    ref[p, row:row + w * r, :] = flat[here, :].astype(BF)
                    row += w * r
                    base += w * D
                ref[p, row:row + NE, :] = flat[7 * D:7 * D + NE, :].astype(BF)
            return carry

        lax.fori_loop(0, half, place, 0)
    else:
        acc_ref[...] = acc[...]
    out.wait()


def backward(lo, n, ndev, sets, live, order, block_in, cot, g, gc, gy, probs, mid, qkv, att, x2, ad, gains, wq, wk, wv, wo, b4, a2t,
             rm, prev):
    sq = whole((D, D))
    na = 7 * D + AC
    r = D // ndev
    last = lo > 0
    packed = (ndev // 2, 7 * r + NE, AC)
    anyspace = pl.BlockSpec(memory_space=pl.ANY)
    part = pl.BlockSpec((1, n, LG, D), lambda i, *_: (0, 0, 0, 0))
    in_specs = [whole((n, LG, D)), part, whole((n, LG, D)), whole((8, D)), sq, sq, sq, sq, sq, whole((3 * D, AC)), whole((AC, AC))]
    in_specs += [anyspace] * 8
    args = [g, gc, gy, gains, wq, wk, wv, wo, b4, a2t, rm, block_in, cot, probs, mid, qkv, att, x2, ad]
    rows = n * LP
    scratch = [
        pltpu.VMEM((n, LEN, D), BF), pltpu.VMEM((n, LEN, D), BF), pltpu.VMEM((n, NE, SL), F32), pltpu.VMEM((n, LP, D), F32),
        pltpu.VMEM((n, LP, 3 * D), BF), pltpu.VMEM((n, LP, D), BF), pltpu.VMEM((n, LP, D), BF), pltpu.VMEM((n, LP, 3 * AC), BF),
        pltpu.VMEM((n, LEN, D), BF), pltpu.VMEM((rows, D), F32), pltpu.VMEM((rows, D), F32), pltpu.VMEM((n, LP, 3 * D), BF),
        pltpu.VMEM((AC, na), F32),
    ]
    alias = {}
    if last:
        in_specs += [whole((AC, na)), anyspace]
        args += [prev[1], prev[0]]
        alias = {3 + len(args) - 1: 0}
        scratch.append(pltpu.VMEM((na, AC), F32))
        tails = [packed, packed]
    else:
        tails = [(AC, na)]
    scratch += [pltpu.SemaphoreType.DMA((8,)), pltpu.SemaphoreType.DMA((1,))]
    return pl.pallas_call(
        functools.partial(bwd_kernel, lo, n, last, r),
        grid_spec=pltpu.PrefetchScalarGridSpec(
            num_scalar_prefetch=3,
            grid=(1,),
            in_specs=in_specs,
            out_specs=[anyspace] + [whole(t) for t in tails],
            scratch_shapes=scratch,
        ),
        out_shape=[jax.ShapeDtypeStruct(block_in.shape, BF)] + [jax.ShapeDtypeStruct(t, BF if last else F32) for t in tails],
        input_output_aliases=alias,
        compiler_params=params(1),
        cost_estimate=cost(12 * n),
        name="backward",
    )(sets, live, order, *args)


def on_device(dpn, fsn, block_in, cotangent, image_live, image_set, expert_routes, expert_slots, gain_attn, gain_moe, w_qkv, w_out,
              w_router, w_up, w_down, qkv_first, qkv_second, out_first, out_second, router_first, router_second, up_first,
              up_second, down_first, down_second):
    ndev = dpn * fsn
    nx = 1 << ((fsn.bit_length() - 1) // 2)
    nz = fsn // nx
    ng = dpn // GRP
    r = D // ndev
    hs = w_up.shape[2]
    d = lax.axis_index("dp")
    q = d % GRP
    rings = [
        (nz, "fsdp", [(f, ((f // nx + 1) % nz) * nx + f % nx) for f in range(fsn)]),
        (nx, "fsdp", [(f, (f // nx) * nx + (f % nx + 1) % nx) for f in range(fsn)]),
        (ng, "dp", [(a, (a + GRP) % dpn) for a in range(dpn)]),
    ]

    def swap(v, bit):
        return lax.ppermute(v, "dp", [(a, a ^ bit) for a in range(dpn)])

    rel = [0, 2, 1, 3]

    tr = jnp.transpose
    small = jnp.concatenate(
        [
            qkv_first, out_first, router_first, tr(out_second),
            jnp.concatenate([w_router, gain_attn[:, None], gain_moe[:, None], jnp.zeros((r, AC - NE - 2), BF)], axis=1),
            jnp.zeros((r, AC), BF).at[0, 0:router_second.shape[0]].set(router_second),
        ],
        axis=1,
    )
    a2s = tr(qkv_second).reshape(3, r, AC)
    second = jnp.concatenate([a2s[0], a2s[1], a2s[2], jnp.zeros((r, 3 * AC), BF)], axis=1)
    front = jnp.stack([w_qkv[:, 0:D], w_qkv[:, D:2 * D], w_qkv[:, 2 * D:], w_out, small, second])
    front = lax.all_gather(front.reshape(6 * r, D), AXES, axis=0, tiled=True).reshape(ndev, 6, r, D)
    wq, wk, wv, wo, b4 = (front[:, j].reshape(D, D) for j in range(5))
    a2t = tr(front[:, 5, :, 0:3 * AC].reshape(ndev, r, 3, AC), (0, 2, 1, 3)).reshape(3 * D, AC)
    gains = jnp.concatenate(
        [b4[:, 4 * AC + NE].reshape(1, D), b4[:, 4 * AC + NE + 1].reshape(1, D), jnp.zeros((6, D), BF)], axis=0
    ).astype(F32)
    rm = front[:, 4, 0, 5 * AC:5 * AC + router_second.shape[0]].reshape(AC, NE)
    rm = jnp.pad(rm, ((0, 0), (0, AC - NE)))

    after = lambda v, *deps: lax.optimization_barrier((v,) + deps)[0]

    ef = jnp.concatenate([up_first, tr(down_second, (0, 2, 1))], axis=2).reshape(GRP, EL, r, 2 * AC)
    own = [lax.dynamic_index_in_dim(ef, q ^ j, 0, keepdims=False) for j in range(GRP)]
    sib_ef = swap(jnp.stack([own[1], own[3]]), 1)
    got_ef = swap(jnp.stack([own[2], sib_ef[1]]), 2)
    mine_ef = jnp.stack([own[0], sib_ef[0], got_ef[0], got_ef[1]])
    wpk = jnp.concatenate([tr(w_up, (0, 2, 1)), tr(up_second, (0, 2, 1)), tr(w_down, (0, 2, 1)), tr(down_first, (0, 2, 1))], axis=2)
    wpk = wpk.reshape(GRP, EL, hs, 2 * DW)
    own = [lax.dynamic_index_in_dim(wpk, q ^ j, 0, keepdims=False) for j in range(GRP)]
    sib = swap(jnp.stack([own[1], own[3]], axis=1), 1)
    near = jnp.stack([own[0], sib[:, 0]], axis=1).reshape(EL, 2 * hs, 2 * DW)
    send, _ = lax.optimization_barrier((jnp.stack([own[2], sib[:, 1]], axis=1), got_ef))
    got = swap(send, 2)
    far = got.reshape(EL, 2 * hs, 2 * DW)

    def hop(v, ring):
        return lax.ppermute(v, ring[1], ring[2])

    up = [[(u, ((u // nx + k) % nz) * nx + u % nx) for u in range(fsn)] for k in range(nz)]
    all_ef = jnp.concatenate([mine_ef] + [lax.ppermute(mine_ef, "fsdp", up[k]) for k in range(1, nz)])
    near, all_ef = lax.optimization_barrier((near, all_ef))
    for n, axis, perm in rings[1:]:
        rows = [all_ef]
        for _ in range(n - 1):
            rows.append(lax.ppermute(rows[-1], axis, perm))
        all_ef = jnp.concatenate(rows)
    near_x, all_ef = lax.optimization_barrier((near, all_ef))
    zn, xn, far = lax.optimization_barrier((hop(near, rings[0]), hop(near_x, rings[1]), far))
    z_row = [jnp.concatenate([near, far], axis=1), jnp.concatenate([zn, hop(far, rings[0])], axis=1)]
    x_row = [jnp.concatenate([xn, hop(far, rings[1])], axis=1)]
    z0, x0, block_in_late = lax.optimization_barrier((z_row[1], x_row[0], block_in))
    z_row[1], x_row[0] = z0, x0
    route = expert_routes.reshape(IMG, LEN, 2)
    slot = expert_slots.reshape(IMG, LEN, 2)
    ids = jnp.arange(NE, dtype=jnp.int32)[None, :, None, None]
    ok = (route[:, None] == ids) & (slot[:, None] >= 0) & (image_live[:, None, None, None] > 0)
    mine_slots = jnp.max(jnp.where(ok, slot[:, None], -1), axis=-1)
    mine_slots = jnp.pad(mine_slots, ((0, 8 - IMG), (0, 0), (0, SL - LEN)), constant_values=-1)
    mine_slots = tr(mine_slots, (1, 0, 2))

    def members(v):
        far = swap(v, 2)
        return [v, far, swap(v, 1), swap(far, 1)]

    def group(v):
        return jnp.stack(members(v))

    all_slots = lax.dynamic_slice_in_dim(group(mine_slots), q * EL, EL, axis=1)
    counts = jnp.max(all_slots, axis=(2, 3)) + 1
    steps = (counts + 15) // 16 * 16
    offs = jnp.concatenate([jnp.zeros((1, EL), jnp.int32), jnp.cumsum(steps, axis=0)], axis=0)
    offs = tr(offs).reshape(-1).astype(jnp.int32)
    firsts = jnp.min(jnp.where(all_slots >= 0, all_slots, CAP), axis=3)[:, :, 0:IMG].reshape(-1)
    all_sets = group(image_set).reshape(-1)
    cots = members(after(cotangent, got))

    f = lax.axis_index("fsdp")
    devs = jnp.arange(ndev, dtype=jnp.int32)
    dd, df = devs // fsn, devs % fsn
    gap = lambda mine, other, n: (mine - other) % n
    spot = (gap(d // GRP, dd // GRP, ng) * nx + gap(f % nx, df % nx, nx)) * nz + gap(f // nx, df // nx, nz)
    ef = jnp.take(all_ef, spot * GRP + ((dd % GRP) ^ q), axis=0)
    ef = tr(ef, (1, 0, 2, 3)).reshape(EL, D, 2 * AC)
    u1, d2 = ef[:, :, 0:AC], ef[:, :, AC:]

    offs, firsts, all_sets, block_in_late, *cots = lax.optimization_barrier((offs, firsts, all_sets, block_in_late, *cots))
    qkv, att, mid, x2, ad, probs = attention_forward(block_in_late, image_set, gains, wq, wk, wv, wo, b4, a2t, rm)
    for k in range(2, nz):
        z_row.append(hop(z_row[-1], rings[0]))
        x_row.append(hop(z_row[k - 1], rings[1]))
        if k == 2:
            z_row[k], x_row[k - 1], x2s = lax.optimization_barrier((z_row[k], x_row[k - 1], x2))
    x2s = members(x2s)
    gates = lax.dynamic_slice_in_dim(tr(group(jnp.pad(probs, ((0, 8 - IMG), (0, 0), (0, 0)))), (0, 2, 1, 3)), q * EL, EL, axis=1)

    xa, ga, mk = dispatch(offs, firsts, all_sets, all_slots, gates, x2s, cots, u1, d2)
    z_row[-1], x_row[-1], xa = lax.optimization_barrier((z_row[-1], x_row[-1], xa))
    x_row.append(hop(z_row[nz - 1], rings[1]))
    rows = [z_row, x_row]
    for _ in range(2, nx):
        rows.append([hop(v, rings[1]) for v in rows[-1]])
    held = [v for row in rows for v in row]
    rows = [held]
    for _ in range(1, ng):
        rows.append([hop(v, rings[2]) for v in rows[-1]])
    held = [v for row in rows for v in row]
    join = len(held) // 8
    units = [held[k] if join == 1 else jnp.concatenate(held[k * join:(k + 1) * join], axis=1) for k in range(8)]
    a1, a2, go, gh = expert_first(offs, xa, ga, units[:NFIRST])
    go = [go[k] for k in range(3)]
    ob, gb, gl, gf = expert_last(offs, xa, ga, mk, a1, a2, u1, d2, units[NFIRST:])

    k = jnp.arange(ng * nx * nz, dtype=jnp.int32)
    kg, kx, kz = k // (nx * nz), k // nz % nx, k % nz
    column = (f // nx - kz) % nz * nx + (f % nx - kx) % nx
    rank = ((d // GRP - kg) % ng * GRP)[:, None] + (q ^ jnp.arange(GRP, dtype=jnp.int32))[None, :]
    spot = (rank * fsn + column[:, None]).reshape(-1)
    gf = jnp.take(gf.reshape(EL, 2, ndev, r, AC), spot, axis=2).reshape(EL, 2, ng * nx, nz * GRP * r, AC)
    simple = ng == 1 and nx == 2
    xback = [(v, u) for u, v in rings[1][2]]
    if simple:
        near_x = lax.ppermute(go[2], "fsdp", xback)
        near_x, ob = lax.optimization_barrier((near_x, ob))
        far_send = jnp.concatenate([gh, gl, gf[:, :, 1]], axis=2)
        far_x = lax.ppermute(far_send, "fsdp", xback)
    else:
        far_send = gf

    fe = (q * EL).reshape(1)
    cut = 2
    parts = []
    for lo, n in ((0, cut), (cut, IMG - cut)):
        ym, yf, yp, gm, gfar, gp = combine(lo, n, offs, firsts, fe, ob, gb, all_slots, gates, cots)
        if parts:
            gp, gy = lax.optimization_barrier((gp, parts[-1][-1]))
            parts[-1] = parts[-1][:-1] + (gy,)
        gc = swap(gp, 1)
        gs = (gfar.astype(F32) + gc[1].astype(F32)).astype(BF)
        gc, gs, ob, far_send = lax.optimization_barrier((gc, gs, ob, far_send))
        parts.append((lo, n, (ym, yf, yp), gm, gc, swap(gs, 2)))

    (lo, n, ya, ga1, gca, gya), (lo2, n2, yb, gb1, gcb, gyb) = parts
    spots = jnp.arange(ndev, dtype=jnp.int32)
    order = (q ^ jnp.array([0, 2, 1, 3], jnp.int32)[spots // fsn % GRP]) * fsn + (f + spots % fsn) % fsn
    order = (order if ng == 1 else spots).astype(jnp.int32)
    yca = swap(ya[2], 1)
    ycb = swap(yb[2], 1)
    add = lambda u, v: (u.astype(F32) + v.astype(F32)).astype(BF)
    ga1, gcb = lax.optimization_barrier((ga1, gcb))
    shared = (probs, mid, qkv, att, x2, ad, gains, wq, wk, wv, wo, b4, a2t, rm)
    first = backward(lo, n, ndev, image_set, image_live, order, block_in, cotangent, ga1, gca, gya, *shared, None)

    head, gyb, yca, ycb = lax.optimization_barrier((first[0], gyb, yca, ycb))
    ysend = jnp.concatenate([add(ya[1], yca[1]), add(yb[1], ycb[1])], axis=0)
    if simple:
        near_x, far_x, _ = lax.optimization_barrier((near_x, far_x, gyb))
        cut = GRP * hs
        s0 = add(go[0], near_x)
        s1 = add(go[1], far_x[:, :, 0:2 * cut])
        sf = add(gf[:, :, 0], far_x[:, :, 2 * cut:])
        hid = [s0[:, :, 0:cut], s0[:, :, cut:], s1[:, :, 0:cut], s1[:, :, cut:]]
        cols = [jnp.concatenate([hid[k], sf[:, :, k * GRP * r:(k + 1) * GRP * r]], axis=2) for k in range(nz)]
    else:
        cut = go[0].shape[2] * 4 // (ng * nx * nz)
        cols = []
        for k, v in enumerate(p for pair in go + [jnp.concatenate([gh, gl], axis=2)] for p in jnp.split(pair, pair.shape[2] // cut, axis=2)):
            at = k % nz * GRP * r
            cols.append(jnp.concatenate([v, gf[:, :, k // nz, at:at + GRP * r]], axis=2))
        for m, axis, perm in rings[2:0:-1]:
            back = [(v, u) for u, v in perm]
            part = len(cols) // m
            rows = [cols[k * part:(k + 1) * part] for k in range(m)]
            cols = rows[m - 1]
            for k in range(m - 2, -1, -1):
                cols = [add(lax.ppermute(v, axis, back), u) for v, u in zip(cols, rows[k])]
    down = [lax.ppermute(cols[k], "fsdp", [(u, ((u // nx - k) % nz) * nx + u % nx) for u in range(fsn)]) for k in range(1, nz)]
    yy = swap(ysend, 2)
    input_grad, mine, other = backward(lo2, n2, ndev, image_set, image_live, order, block_in, cotangent, gb1, gcb, gyb, *shared,
                                       (head, first[1]))
    mine, other, yy, *down = lax.optimization_barrier((mine, other, yy, *down))
    got_small = swap(other, 1) if ng == 1 else other
    got_small, yy, mid, own_cols, *down = lax.optimization_barrier((got_small, yy, mid, cols[0], *down))
    yya, yyb = yy[0:n], yy[n:]

    eg = (own_cols.astype(F32) + sum(v.astype(F32) for v in down)).astype(BF)
    eg = [jnp.concatenate([eg[:, :, j * hs:(j + 1) * hs], eg[:, :, GRP * hs + j * r:GRP * hs + (j + 1) * r]], axis=2) for j in range(GRP)]
    sib = swap(jnp.stack([eg[1], eg[3]]), 1)
    got = swap(jnp.stack([eg[2], sib[1]]), 2)
    got = jnp.concatenate([eg[0][None], sib[0:1], got], axis=0)
    at = jnp.stack([q ^ j for j in range(GRP)])
    eg = jnp.take(got, jnp.argsort(at), axis=0).reshape(NE, 2, hs + r, AC).astype(F32)
    ff = eg[:, :, hs:]
    eg = tr(eg[:, :, 0:hs], (1, 0, 3, 2))
    outs = []
    for at, m, y, yc, yy in ((lo, n, ya, yca, yya), (lo2, n2, yb, ycb, yyb)):
        total = mid[at:at + m] + y[0].astype(F32) + yc[0].astype(F32) + yy.astype(F32)
        outs.append(total[:, 0:LEN])
    block_out = (jnp.concatenate(outs, axis=0) * image_live.astype(F32)[:, None, None]).astype(BF)

    nrs = router_second.shape[0]
    if ng == 1:
        far = swap(add(mine[fsn:], got_small[fsn:]), 2)
        sm = add(add(mine[0:fsn], got_small[0:fsn]), far)
        total = sm[0].astype(F32)
        for k in range(1, fsn):
            perm = [(u, (u + k) % fsn) for u in range(fsn)]
            total = total + lax.ppermute(sm[k], "fsdp", perm).astype(F32)
        sm = total
    else:
        sm = jnp.concatenate([mine, other], axis=0)
        sm = lax.psum_scatter(sm, AXES, scatter_dimension=0, tiled=False).astype(F32)
    rs = tr(sm[7 * r:7 * r + NE]).reshape(-1)
    rs = lax.dynamic_slice_in_dim(rs, (d * fsn + f) * nrs, nrs)
    return (
        block_out,
        input_grad,
        sm[0:r],
        tr(sm[r:4 * r]),
        sm[4 * r:5 * r],
        tr(sm[5 * r:6 * r]),
        sm[6 * r:7 * r],
        rs,
        ff[:, 0],
        eg[0],
        eg[1],
        tr(ff[:, 1], (0, 2, 1)),
    )


def solution(mesh):
    dpn, fsn = mesh.shape["dp"], mesh.shape["fsdp"]
    both = ("dp", "fsdp")
    return jax.shard_map(
        functools.partial(on_device, dpn, fsn),
        mesh=mesh,
        in_specs=(
            P(both, None, None),
            P(both, None, None),
            P(both),
            P(both),
            P(both, None, None),
            P(both, None, None),
            P(both),
            P(both),
            P(both, None),
            P(both, None),
            P(both, None),
            P(None, None, both),
            P(None, None, both),
            P(both, None),
            P(None, both),
            P(both, None),
            P(None, both),
            P(both, None),
            P(both),
            P(None, both, None),
            P(None, None, both),
            P(None, None, both),
            P(None, None, both),
        ),
        out_specs=(
            P(both, None, None),
            P(both, None, None),
            P(both, None),
            P(None, both),
            P(both, None),
            P(None, both),
            P(both, None),
            P(both),
            P(None, both, None),
            P(None, None, both),
            P(None, None, both),
            P(None, None, both),
        ),
        check_vma=False,
    )
```

```python
import functools
import math

import jax
import jax.numpy as jnp
from jax import lax
from jax.experimental import pallas as pl
from jax.experimental.pallas import tpu as pltpu
from jax.sharding import PartitionSpec as P

D = 768
HEADS = 12
HEAD = 64
NE = 8
LEN = 197
LP = 208
SL = 256
AC = 128
RANK = 16
CAP = 384
IMG = 5
GRP = 4
EL = NE // GRP
ROWS = GRP * CAP
RT = 256
DW = D + AC
WIN = 256
NFIRST = 7
LG = LP + 16
EPS = 1e-06
F32 = jnp.float32
BF = jnp.bfloat16
AXES = ("dp", "fsdp")
VMEM = 60 * 1000 * 1024


def nn(a, b):
    return lax.dot_general(a, b, (((1,), (0,)), ((), ())), preferred_element_type=F32)


def nt(a, b):
    return lax.dot_general(a, b, (((1,), (1,)), ((), ())), preferred_element_type=F32)


def adapter_mask(rows, which):
    lane = lax.broadcasted_iota(jnp.int32, (rows, AC), 1)
    return jnp.where(lane // RANK == which, 1.0, 0.0).astype(F32)


def norm_parts(v):
    mean = jnp.mean(v, axis=-1, keepdims=True)
    cen = v - mean
    var = jnp.mean(cen * cen, axis=-1, keepdims=True)
    inv = lax.rsqrt(var + EPS)
    return cen * inv, inv


def norm_back(g, unit, inv, gain):
    s = g * gain
    return inv * (
        s
        - jnp.mean(s, axis=-1, keepdims=True)
        - unit * jnp.mean(s * unit, axis=-1, keepdims=True)
    )


def params(n):
    return pltpu.CompilerParams(dimension_semantics=("arbitrary",) * n, vmem_limit_bytes=VMEM)


def cost(us):
    return pl.CostEstimate(flops=int(us * 1.15e9), transcendentals=0, bytes_accessed=0)


def whole(shape):
    zeros = (0,) * len(shape)
    return pl.BlockSpec(shape, lambda *_: zeros, pipeline_mode=pl.Buffered(1))


def per_image(shape):
    rest = (0,) * (len(shape) - 1)
    return pl.BlockSpec(shape, lambda i, *_: (i,) + rest)


def fwd_kernel(sets, x_ref, g_ref, wq, wk, wv, wo, b4, a2t, rm, qkv_ref, att_ref, mid_ref, x2_ref, ad_ref, pr_ref, hid):
    mask = adapter_mask(LP, sets[pl.program_id(0)])
    hid[...] = jnp.zeros((LP, D), F32)
    hid[0:LEN, :] = x_ref[0].astype(F32)
    hidden = hid[...]
    unit, _ = norm_parts(hidden)
    x1 = (unit * g_ref[0:1, :]).astype(BF)
    aq = (mask * nn(x1, b4[:, 0:AC])).astype(BF)
    ad_ref[0, :, 0:AC] = aq
    for j, w in enumerate((wq, wk, wv)):
        part = nn(x1, w[...]) + nt(aq, a2t[j * D:(j + 1) * D, :])
        qkv_ref[0, :, j * D:(j + 1) * D] = part.astype(BF)
    lane = lax.broadcasted_iota(jnp.int32, (LP, 2 * HEAD), 1)
    keyok = lax.broadcasted_iota(jnp.int32, (LP, LP), 1) < LEN
    scale = 1.0 / math.sqrt(HEAD)
    for h in range(HEADS // 2):
        at = h * 2 * HEAD
        q = qkv_ref[0, :, at:at + 2 * HEAD]
        k = qkv_ref[0, :, D + at:D + at + 2 * HEAD]
        v = qkv_ref[0, :, 2 * D + at:2 * D + at + 2 * HEAD]
        outs = []
        for half in range(2):
            mine = (lane >= HEAD) if half else (lane < HEAD)
            s = nt(jnp.where(mine, q, jnp.zeros_like(q)), k) * scale
            s = jnp.where(keyok, s, -1e30)
            e = jnp.exp(s - jnp.max(s, axis=-1, keepdims=True))
            p = e * (1.0 / jnp.sum(e, axis=-1, keepdims=True))
            outs.append(nn(p.astype(BF), v))
        att_ref[0, :, at:at + 2 * HEAD] = jnp.where(lane < HEAD, outs[0], outs[1]).astype(BF)
    att = att_ref[0]
    ao = (mask * nn(att, b4[:, AC:2 * AC])).astype(BF)
    ad_ref[0, :, AC:2 * AC] = ao
    middle = hidden + nn(att, wo[...]) + nt(ao, b4[:, 3 * AC:4 * AC])
    mid_ref[0] = middle
    unit2, _ = norm_parts(middle)
    x2 = (unit2 * g_ref[1:2, :]).astype(BF)
    x2_ref[0] = x2
    ar = (mask * nn(x2, b4[:, 2 * AC:3 * AC])).astype(BF)
    ad_ref[0, :, 2 * AC:3 * AC] = ar
    logits = nn(x2, b4[:, 4 * AC:5 * AC]) + nn(ar, rm[...])
    elane = lax.broadcasted_iota(jnp.int32, (LP, AC), 1)
    logits = jnp.where(elane < NE, logits, -1e30)
    e = jnp.exp(logits - jnp.max(logits, axis=-1, keepdims=True))
    probs = e * (1.0 / jnp.sum(e, axis=-1, keepdims=True))
    padded = jnp.concatenate([probs, jnp.zeros((SL - LP, AC), F32)], axis=0)
    pr_ref[0] = jnp.transpose(padded)[0:NE, :]


def attention_forward(block_in, sets, gains, wq, wk, wv, wo, b4, a2t, rm):
    n = block_in.shape[0]
    sq = whole((D, D))
    return pl.pallas_call(
        fwd_kernel,
        grid_spec=pltpu.PrefetchScalarGridSpec(
            num_scalar_prefetch=1,
            grid=(n,),
            in_specs=[per_image((1, LEN, D)), whole((8, D)), sq, sq, sq, sq, sq, whole((3 * D, AC)), whole((AC, AC))],
            out_specs=[
                per_image((1, LP, 3 * D)),
                per_image((1, LP, D)),
                per_image((1, LP, D)),
                per_image((1, LP, D)),
                per_image((1, LP, 3 * AC)),
                per_image((1, NE, SL)),
            ],
            scratch_shapes=[pltpu.VMEM((LP, D), F32)],
        ),
        out_shape=[
            jax.ShapeDtypeStruct((n, LP, 3 * D), BF),
            jax.ShapeDtypeStruct((n, LP, D), BF),
            jax.ShapeDtypeStruct((n, LP, D), F32),
            jax.ShapeDtypeStruct((n, LP, D), BF),
            jax.ShapeDtypeStruct((n, LP, 3 * AC), BF),
            jax.ShapeDtypeStruct((n, NE, SL), F32),
        ],
        compiler_params=params(1),
        cost_estimate=cost(28),
        name="attention_forward",
    )(sets, block_in, gains, wq, wk, wv, wo, b4, a2t, rm)


def window(base, first, limit):
    at = jnp.minimum(base + first // 16 * 16, limit - WIN)
    return pl.multiple_of(at, 16)


def fetch_blocks(at_start, b, sets):
    def copies(k):
        return [pltpu.make_async_copy(refs[k], buf.at[k], sems.at[k]) for refs, buf, sems in sets]

    @pl.when(at_start)
    def _():
        for k in range(GRP):
            for c in copies(k):
                c.start()

    for k in range(GRP):
        @pl.when(b == k)
        def _(k=k):
            for c in copies(k):
                c.wait()


def dispatch_kernel(offs, firsts, sets, slot_ref, gate_ref, *refs):
    x2_refs, cot_refs = refs[0:GRP], refs[GRP:2 * GRP]
    u1_ref, d2_ref, xa_ref, ga_ref, mk_ref, acc, cpad, x2_buf, cot_buf, x2_sem, cot_sem = refs[2 * GRP:]
    e = pl.program_id(0)
    b = pl.program_id(1)

    @pl.when(e == 0)
    def _():
        fetch_blocks(b == 0, b, ((x2_refs, x2_buf, x2_sem), (cot_refs, cot_buf, cot_sem)))

    @pl.when(b == 0)
    def _():
        xa_ref[...] = jnp.zeros_like(xa_ref)
        ga_ref[...] = jnp.zeros_like(ga_ref)
        mk_ref[...] = jnp.zeros_like(mk_ref)

    acc[...] = jnp.zeros_like(acc)
    cpad[...] = jnp.zeros_like(cpad)
    gcol = jnp.transpose(gate_ref[0, 0])
    rows = lax.broadcasted_iota(jnp.int32, (WIN, LP), 0)
    for i in range(IMG):
        first = firsts[(b * EL + e) * IMG + i]

        @pl.when(first < CAP)
        def _():
            at = window(0, first, CAP)
            here = pl.ds(at, WIN)
            pick = jnp.where(rows + at == slot_ref[0, 0, i:i + 1, 0:LP], 1.0, 0.0).astype(BF)
            cpad[0:LEN, :] = cot_buf[b, i].astype(F32)
            gg = (cpad[...] * gcol[0:LP, i:i + 1]).astype(BF)
            acc[here, 0:D] += nn(pick, x2_buf[b, i])
            acc[here, D:2 * D] += nn(pick, gg)
            acc[here, 2 * D:] += nn(pick, adapter_mask(LP, sets[b * IMG + i]).astype(BF))

    mk = acc[:, 2 * D:]
    xs = acc[:, 0:D].astype(BF)
    gs = acc[:, D:2 * D].astype(BF)
    at = pl.multiple_of(offs[e * (GRP + 1) + b], 16)
    here = pl.ds(at, CAP)
    xa_ref[0, here, 0:D] = xs
    xa_ref[0, here, D:DW] = (mk * nn(xs, u1_ref[0])).astype(BF)
    ga_ref[0, here, 0:D] = gs
    ga_ref[0, here, D:DW] = (mk * nn(gs, d2_ref[0])).astype(BF)
    mk_ref[0, here, :] = mk.astype(BF)


def dispatch(offs, firsts, sets, slots, gates, x2, cot, u1, d2):
    return pl.pallas_call(
        dispatch_kernel,
        grid_spec=pltpu.PrefetchScalarGridSpec(
            num_scalar_prefetch=3,
            grid=(EL, GRP),
            in_specs=[
                pl.BlockSpec((1, 1, 8, SL), lambda e, b, *_: (b, e, 0, 0)),
                pl.BlockSpec((1, 1, 8, SL), lambda e, b, *_: (b, e, 0, 0)),
            ] + [pl.BlockSpec(memory_space=pl.ANY)] * (2 * GRP) + [
                pl.BlockSpec((1, D, AC), lambda e, b, *_: (e, 0, 0)),
                pl.BlockSpec((1, D, AC), lambda e, b, *_: (e, 0, 0)),
            ],
            out_specs=[
                pl.BlockSpec((1, ROWS, DW), lambda e, b, *_: (e, 0, 0)),
                pl.BlockSpec((1, ROWS, DW), lambda e, b, *_: (e, 0, 0)),
                pl.BlockSpec((1, ROWS, AC), lambda e, b, *_: (e, 0, 0)),
            ],
            scratch_shapes=[
                pltpu.VMEM((CAP, 2 * D + AC), F32), pltpu.VMEM((LP, D), F32), pltpu.VMEM((GRP, IMG, LP, D), BF),
                pltpu.VMEM((GRP, IMG, LEN, D), BF), pltpu.SemaphoreType.DMA((GRP,)), pltpu.SemaphoreType.DMA((GRP,)),
            ],
        ),
        out_shape=[
            jax.ShapeDtypeStruct((EL, ROWS, DW), BF),
            jax.ShapeDtypeStruct((EL, ROWS, DW), BF),
            jax.ShapeDtypeStruct((EL, ROWS, AC), BF),
        ],
        compiler_params=params(2),
        cost_estimate=cost(1),
        name="dispatch",
    )(offs, firsts, sets, slots, gates, *x2, *cot, u1, d2)


def flip(v):
    return jnp.transpose(v.astype(F32)).astype(BF)


def gelu_parts(pre):
    c0 = math.sqrt(2.0 / math.pi)
    sq = pre * pre
    th = jnp.tanh(c0 * pre * (1.0 + 0.044715 * sq))
    half = 0.5 * (1.0 + th)
    slope = half + 0.5 * pre * (1.0 - th * th) * (c0 * (1.0 + 3 * 0.044715 * sq))
    return pre * half, slope


def tile_products(x, g, xt, gt, wbuf, cur, width, put):
    wu = wbuf[cur, 0:width, 0:DW]
    wd = wbuf[cur, 0:width, DW:2 * DW]
    act, slope = gelu_parts(nt(x, wu))
    act = act.astype(BF)
    gp = (slope * nt(g, wd)).astype(BF)
    t1, t2 = nn(act, wd), nn(gp, wu)
    put(nn(xt, gp), nn(gt, act))
    return t1, t2


def tall_tiles(offs, e):
    total = offs[e * (GRP + 1) + GRP]
    tall = (total + RT - 1) // (2 * RT)
    return tall, (total > tall * 2 * RT).astype(jnp.int32)


def live_tiles(offs, e):
    tall, tail = tall_tiles(offs, e)
    return 2 * tall + tail


def over_tiles(offs, e, step):
    tall, tail = tall_tiles(offs, e)

    def one(t, carry):
        step(2 * t, 2)
        return carry

    lax.fori_loop(0, tall, one, 0)

    @pl.when(tail > 0)
    def _():
        step(2 * tall, 1)


def each_tile(limit, do):
    for t in range(ROWS // RT):
        @pl.when(t < limit)
        def _(t=t):
            do(t)


def unit_copies(units, wbuf, slot, sems, s, e):
    hu = units[0].shape[1]
    return [pltpu.make_async_copy(u.at[e], wbuf.at[slot, pl.ds(k * hu, hu)], sems.at[s, k]) for k, u in enumerate(units)]


def expert_some_kernel(nu, offs, xa, ga, *refs):
    units, refs = refs[:nu], refs[nu:]
    steps, odd = (nu + 1) // 2, nu % 2
    a1, a2, go_ref, *refs = refs
    gh_ref = refs.pop(0) if odd else None
    xb, gb, s1, s2, b1, b2, at_ref, wbuf, gacc, wsem, isem, osem = refs
    chunks = [units[k:k + 2] for k in range(0, nu, 2)]
    e, p = pl.program_id(0), pl.program_id(1)
    s = e * steps + p
    full, short = 2 * units[0].shape[1], units[0].shape[1]

    def rows(t):
        return pl.ds(t * RT, RT)

    def incoming(v, t):
        pairs = [(xa, xb), (ga, gb)]
        return [pltpu.make_async_copy(src.at[v, rows(t)], dst.at[v, rows(t)], isem.at[v, t, k]) for k, (src, dst) in enumerate(pairs)]

    def outgoing(v, t):
        return [pltpu.make_async_copy(src.at[v, rows(t)], dst.at[v, rows(t)], osem.at[v, t, k])
                for k, (src, dst) in enumerate(((b1, a1), (b2, a2)))]

    def weights(k):
        return unit_copies(chunks[k % steps], wbuf, k % 2, wsem, k, k // steps)

    @pl.when(s == 0)
    def _():
        for c in weights(0):
            c.start()
        for v in range(EL):
            each_tile(live_tiles(offs, v), lambda t, v=v: [c.start() for c in incoming(v, t)])

    for k in range(EL * steps):
        @pl.when(s == k)
        def _(k=k):
            if k + 1 < EL * steps:
                for c in weights(k + 1):
                    c.start()
            if k % steps == 0:
                each_tile(live_tiles(offs, k // steps), lambda t: [c.wait() for c in incoming(k // steps, t)])
            for c in weights(k):
                c.wait()

    tiles = live_tiles(offs, e)
    cur = s % 2

    @pl.when(p == 0)
    def _():
        def turn(t, carry):
            here = pl.ds(pl.multiple_of(t * RT, RT), RT)
            at_ref[0, :, here] = flip(xb[e, here, D:DW])
            at_ref[1, :, here] = flip(gb[e, here, D:DW])
            s1[e, here, :] = jnp.zeros((RT, DW), F32)
            s2[e, here, :] = jnp.zeros((RT, DW), F32)
            return carry

        lax.fori_loop(0, tiles, turn, 0)

    def run(width, ref, done):
        gacc[:, :, 0:width] = jnp.zeros((2, AC, width), F32)

        def put(gu, gd):
            gacc[0, :, 0:width] += gu
            gacc[1, :, 0:width] += gd

        def step(t, height):
            here = pl.ds(pl.multiple_of(t * RT, RT), height * RT)
            t1, t2 = tile_products(xb[e, here, :], gb[e, here, :], at_ref[0, :, here], at_ref[1, :, here], wbuf, cur, width, put)
            if done:
                b1[e, here, :] = (s1[e, here, :] + t1).astype(BF)
                b2[e, here, :] = (s2[e, here, :] + t2).astype(BF)
            else:
                s1[e, here, :] += t1
                s2[e, here, :] += t2

        over_tiles(offs, e, step)
        for k in range(2):
            ref[k] = jnp.transpose(gacc[k, :, 0:width]).astype(BF)

    @pl.when(p < steps - 1)
    def _():
        run(full, go_ref.at[0, 0], False)

    @pl.when(p == steps - 1)
    def _():
        run(short, gh_ref.at[0], True)

    @pl.when(p == steps - 1)
    def _():
        for v in range(EL):
            @pl.when(e == v)
            def _(v=v):
                each_tile(tiles, lambda t: [c.start() for c in outgoing(v, t)])

    @pl.when(s == EL * steps - 1)
    def _():
        for v in range(EL):
            each_tile(live_tiles(offs, v), lambda t, v=v: [c.wait() for c in outgoing(v, t)])


def expert_some(offs, xa, ga, units):
    hu, nu = units[0].shape[1], len(units)
    steps, odd = (nu + 1) // 2, nu % 2
    nt_ = ROWS // RT
    anyspace = pl.BlockSpec(memory_space=pl.ANY)
    short_spec = [pl.BlockSpec((1, 2, hu, AC), lambda e, p, *_: (e, 0, 0, 0))] * odd
    short_shape = [jax.ShapeDtypeStruct((EL, 2, hu, AC), BF)] * odd
    return pl.pallas_call(
        functools.partial(expert_some_kernel, nu),
        grid_spec=pltpu.PrefetchScalarGridSpec(
            num_scalar_prefetch=1,
            grid=(EL, steps),
            in_specs=[anyspace] * (2 + nu),
            out_specs=[anyspace, anyspace,
                       pl.BlockSpec((1, 1, 2, 2 * hu, AC), lambda e, p, *_: (jnp.minimum(p, steps - 1 - odd), e, 0, 0, 0))] + short_spec,
            scratch_shapes=[
                pltpu.VMEM((EL, ROWS, DW), BF), pltpu.VMEM((EL, ROWS, DW), BF), pltpu.VMEM((EL, ROWS, DW), F32),
                pltpu.VMEM((EL, ROWS, DW), F32), pltpu.VMEM((EL, ROWS, DW), BF), pltpu.VMEM((EL, ROWS, DW), BF), pltpu.VMEM((2, AC, ROWS), BF), pltpu.VMEM((2, 2 * hu, 2 * DW), BF),
                pltpu.VMEM((2, AC, 2 * hu), F32), pltpu.SemaphoreType.DMA((EL * steps, 2)), pltpu.SemaphoreType.DMA((EL, nt_, 4)),
                pltpu.SemaphoreType.DMA((EL, nt_, 2)),
            ],
        ),
        out_shape=[
            jax.ShapeDtypeStruct((EL, ROWS, DW), BF),
            jax.ShapeDtypeStruct((EL, ROWS, DW), BF),
            jax.ShapeDtypeStruct((steps - odd, EL, 2, 2 * hu, AC), BF),
        ] + short_shape,
        compiler_params=params(2),
        cost_estimate=cost(9 * nu),
        name="expert_some",
    )(offs, xa, ga, *units)


def expert_last_kernel(offs, mk_ref, u1_ref, d2_ref, xa, ga, a1, a2, w0, w1, ob, gb, go_ref, gf_ref,
                       xs, gs, s1, s2, os, hs, wbuf, gacc, facc, wsem, isem, osem):
    e = pl.program_id(0)
    tiles = live_tiles(offs, e)

    def rows(t):
        return pl.ds(t * RT if isinstance(t, int) else pl.multiple_of(t * RT, RT), RT)

    def incoming(v, t):
        return [pltpu.make_async_copy(src.at[v, rows(t)], dst.at[v, rows(t)], isem.at[v, t, k])
                for k, (src, dst) in enumerate(((xa, xs), (ga, gs), (a1, s1), (a2, s2)))]

    def outgoing(v, t):
        return [pltpu.make_async_copy(src.at[v, rows(t)], dst.at[v, rows(t)], osem.at[v, t, k])
                for k, (src, dst) in enumerate(((os, ob), (hs, gb)))]

    def weights(v):
        return unit_copies(((w0, w1)[v],), wbuf, v, wsem, v, 0)

    @pl.when(e == 0)
    def _():
        for v in range(EL):
            for c in weights(v):
                c.start()
            each_tile(live_tiles(offs, v), lambda t, v=v: [c.start() for c in incoming(v, t)])

    gacc[...] = jnp.zeros_like(gacc)
    facc[...] = jnp.zeros_like(facc)
    for v in range(EL):
        @pl.when(e == v)
        def _(v=v):
            for c in weights(v):
                c.wait()

    def put(gu, gd):
        gacc[0] += gu
        gacc[1] += gd

    def step(t, height):
        here = pl.ds(pl.multiple_of(t * RT, RT), height * RT)
        for k in range(height):
            for c in incoming(e, t + k):
                c.wait()
        x = xs[e, here, :]
        g = gs[e, here, :]
        t1, t2 = tile_products(x, g, flip(x[:, D:DW]), flip(g[:, D:DW]), wbuf, e, wbuf.shape[1], put)
        t1 = s1[e, here, :].astype(F32) + t1
        t2 = s2[e, here, :].astype(F32) + t2
        mk = mk_ref[0, here, :].astype(F32)
        adt = (mk * t1[:, D:DW]).astype(BF)
        aut = (mk * t2[:, D:DW]).astype(BF)
        os[e, here, :] = (t1[:, 0:D] + nt(adt, d2_ref[0])).astype(BF)
        hs[e, here, :] = (t2[:, 0:D] + nt(aut, u1_ref[0])).astype(BF)
        for k in range(height):
            for c in outgoing(e, t + k):
                c.start()
        facc[0] += nn(flip(aut), x[:, 0:D])
        facc[1] += nn(flip(adt), g[:, 0:D])

    over_tiles(offs, e, step)
    @pl.when(tiles < ROWS // RT)
    def _():
        here = rows(tiles)
        os[e, here, :] = jnp.zeros((RT, D), BF)
        hs[e, here, :] = jnp.zeros((RT, D), BF)
        for c in outgoing(e, tiles):
            c.start()

    for j in range(2):
        go_ref[0, j] = jnp.transpose(gacc[j]).astype(BF)
        gf_ref[0, j] = jnp.transpose(facc[j]).astype(BF)

    @pl.when(e == EL - 1)
    def _():
        for v in range(EL):
            each_tile(live_tiles(offs, v) + 1, lambda t, v=v: [c.wait() for c in outgoing(v, t)])


def expert_last(offs, xa, ga, mk, a1, a2, u1, d2, units):
    hu = units[0].shape[1]
    nt_ = ROWS // RT
    each = lambda *shape: pl.BlockSpec((1,) + shape, lambda e, *_: (e,) + (0,) * len(shape))
    anyspace = pl.BlockSpec(memory_space=pl.ANY)
    return pl.pallas_call(
        expert_last_kernel,
        grid_spec=pltpu.PrefetchScalarGridSpec(
            num_scalar_prefetch=1,
            grid=(EL,),
            in_specs=[each(ROWS, AC), each(D, AC), each(D, AC)] + [anyspace] * 6,
            out_specs=[anyspace, anyspace, each(2, hu, AC), each(2, D, AC)],
            scratch_shapes=[
                pltpu.VMEM((EL, ROWS, DW), BF), pltpu.VMEM((EL, ROWS, DW), BF), pltpu.VMEM((EL, ROWS, DW), BF),
                pltpu.VMEM((EL, ROWS, DW), BF), pltpu.VMEM((EL, ROWS, D), BF), pltpu.VMEM((EL, ROWS, D), BF),
                pltpu.VMEM((EL, hu, 2 * DW), BF), pltpu.VMEM((2, AC, hu), F32), pltpu.VMEM((2, AC, D), F32),
                pltpu.SemaphoreType.DMA((EL, 1)), pltpu.SemaphoreType.DMA((EL, nt_, 4)), pltpu.SemaphoreType.DMA((EL, nt_, 2)),
            ],
        ),
        out_shape=[
            jax.ShapeDtypeStruct((EL, ROWS, D), BF),
            jax.ShapeDtypeStruct((EL, ROWS, D), BF),
            jax.ShapeDtypeStruct((EL, 2, hu, AC), BF),
            jax.ShapeDtypeStruct((EL, 2, D, AC), BF),
        ],
        compiler_params=params(1),
        cost_estimate=cost(18),
        name="expert_last",
    )(offs, mk, u1, d2, xa, ga, a1, a2, *units)


def combine_kernel(lo, n, offs, firsts, first_expert, ob, gb, slot_ref, gate_ref, *refs):
    b = pl.program_id(0)
    cot_refs, outs = refs[:GRP], refs[GRP:]
    y_ref, g_ref, cot_buf, cot_sem = outs[6:]
    fetch_blocks(b == 0, b, (([r.at[lo:lo + n] for r in cot_refs], cot_buf, cot_sem),))
    lanes = lax.broadcasted_iota(jnp.int32, (LP, WIN), 1)
    dlane = lax.broadcasted_iota(jnp.int32, (LP, AC), 1)
    scol = [jnp.transpose(slot_ref[0, e].astype(F32)) for e in range(EL)]
    gcol = [jnp.transpose(gate_ref[0, e]) for e in range(EL)]
    for i in range(n):
        y = jnp.zeros((LP, D), F32)
        g = jnp.zeros((LP, D), F32)
        dots = jnp.zeros((LP, AC), F32)
        cot = jnp.concatenate([cot_buf[b, i].astype(F32), jnp.zeros((LP - LEN, D), F32)], axis=0)
        for e in range(EL):
            first = firsts[(b * EL + e) * IMG + lo + i]
            first = jnp.where(first < CAP, first, 0)
            base = offs[e * (GRP + 1) + b]
            at = window(base, first, ROWS)
            here = pl.ds(at, WIN)
            slot = scol[e][0:LP, lo + i:lo + i + 1]
            pick = jnp.where(slot == (lanes + (at - base)).astype(F32), 1.0, 0.0).astype(BF)
            ye = nn(pick, ob[e, here, :])
            g = g + nn(pick, gb[e, here, :])
            y = y + gcol[e][0:LP, lo + i:lo + i + 1] * ye
            dot = jnp.sum(ye * cot, axis=-1, keepdims=True)
            dots = dots + jnp.where(dlane == first_expert[0] + e, dot, 0.0)
        y_ref[i] = y.astype(BF)
        g_ref[i, 0:LP] = g.astype(BF)
        full = jnp.transpose(jnp.concatenate([dots, jnp.zeros((SL - LP, AC), F32)], axis=0))[0:16, :]
        high = full.astype(BF)
        g_ref[i, LP:LG, 0:SL] = high
        g_ref[i, LP:LG, SL:2 * SL] = (full - high.astype(F32)).astype(BF)
        g_ref[i, LP:LG, 2 * SL:] = jnp.zeros((LG - LP, D - 2 * SL), BF)
    for v, mine, far, core in ((y_ref, outs[0], outs[1], outs[2]), (g_ref, outs[3], outs[4], outs[5])):
        for when, ref in ((0, mine), (1, far), (2, core), (3, core)):
            @pl.when(b == when)
            def _(ref=ref, v=v):
                if len(ref.shape) == 4:
                    ref[0] = v[...]
                else:
                    ref[...] = v[...]


def combine(lo, n, offs, firsts, first_expert, ob, gb, slots, gates, cot):
    block = lambda *shape: pl.BlockSpec((1,) + shape, lambda b, *_: (b,) + (0,) * len(shape))
    return pl.pallas_call(
        functools.partial(combine_kernel, lo, n),
        grid_spec=pltpu.PrefetchScalarGridSpec(
            num_scalar_prefetch=3,
            grid=(GRP,),
            in_specs=[whole((EL, ROWS, D)), whole((EL, ROWS, D)), block(EL, 8, SL), block(EL, 8, SL)] + [pl.BlockSpec(memory_space=pl.ANY)] * GRP,
            out_specs=[spec for rows in (LP, LG) for spec in (
                whole((n, rows, D)), whole((n, rows, D)), pl.BlockSpec((1, n, rows, D), lambda b, *_: (jnp.maximum(b - 2, 0), 0, 0, 0)))],
            scratch_shapes=[pltpu.VMEM((n, LP, D), BF), pltpu.VMEM((n, LG, D), BF), pltpu.VMEM((GRP, n, LEN, D), BF),
                            pltpu.SemaphoreType.DMA((GRP,))],
        ),
        out_shape=[jax.ShapeDtypeStruct(shape, BF) for rows in (LP, LG) for shape in ((n, rows, D), (n, rows, D), (2, n, rows, D))],
        compiler_params=params(1),
        cost_estimate=cost(6 * n),
        name="combine",
    )(offs, firsts, first_expert, ob, gb, slots, gates, *cot)


def bwd_kernel(lo, n, last, r, sets, live, order, go_ref, gc_ref, gy_ref, g_ref, rm, *refs):
    sources, frozen, refs = refs[:8], refs[8:14], refs[14:]
    if last:
        pacc, _, ig_ref, mine_ref, other_ref, *refs = refs
    else:
        ig_ref, acc_ref, *refs = refs
    xb, cb, pb, midb, qkvb, attb, x2b, adb, igb, hid, gin, gq, acc, b4, wo, wq, wk, wv, a2t = refs[:19]
    flat = refs[19] if last else None
    sems, osem = refs[-2:]
    rows = n * LP
    loads = [pltpu.make_async_copy(src.at[lo:lo + n], dst, sems.at[k])
             for k, (src, dst) in enumerate(zip(sources, (xb, cb, pb, midb, qkvb, attb, x2b, adb)))]
    held = [pltpu.make_async_copy(src, dst, sems.at[8 + k]) for k, (src, dst) in enumerate(zip(frozen, (b4, wo, wq, wk, wv, a2t)))]
    for c in held[:1] + loads + held[1:]:
        c.start()
    acc[...] = pacc[...] if last else jnp.zeros_like(acc)
    tr = flip
    flatten = lambda v: v.reshape(rows, v.shape[-1])
    stack = lambda f: jnp.concatenate([f(i) for i in range(n)], axis=0)
    mask = stack(lambda i: adapter_mask(LP, sets[lo + i]))
    zrow = jnp.zeros((AC - NE, SL), F32)
    gprobs = []
    for i in range(n):
        gsum = go_ref[i].astype(F32) + gc_ref[0, i].astype(F32) + gy_ref[i].astype(F32)
        gin[i * LP:(i + 1) * LP, :] = gsum[0:LP]
        dots = gsum[LP:LP + NE, 0:SL] + gsum[LP:LP + NE, SL:2 * SL]
        gprobs.append(jnp.transpose(jnp.concatenate([dots, zrow], axis=0))[0:LP, :])
    gprobs = jnp.concatenate(gprobs, axis=0)
    for c in held[:1] + loads:
        c.wait()

    def padded(buf, scale):
        hid[...] = jnp.zeros((rows, D), F32)
        for i in range(n):
            v = buf[i].astype(F32)
            hid[i * LP:i * LP + LEN, :] = v if scale is None else v * scale(i)
        return hid[...]

    aq = flatten(adb[:, :, 0:AC])
    ao = flatten(adb[:, :, AC:2 * AC])
    ar = flatten(adb[:, :, 2 * AC:3 * AC])
    att = flatten(attb[...])
    elane = lax.broadcasted_iota(jnp.int32, (rows, AC), 1)
    probs = stack(lambda i: jnp.transpose(jnp.concatenate([pb[i], zrow], axis=0))[0:LP, :])
    gl = probs * (gprobs - jnp.sum(gprobs * probs, axis=-1, keepdims=True))
    gl = jnp.where(elane < NE, gl, 0.0).astype(BF)
    gar = (mask * nt(gl, rm[...])).astype(BF)
    gtwo = gin[...] + nt(gl, b4[:, 4 * AC:5 * AC]) + nt(gar, b4[:, 2 * AC:3 * AC])
    unit2, inv2 = norm_parts(flatten(midb[...]))
    gin[...] = padded(cb, lambda i: live[lo + i].astype(F32)) + norm_back(gtwo, unit2, inv2, g_ref[1:2, :])
    gbr = gin[...].astype(BF)
    gao = (mask * nn(gbr, b4[:, 3 * AC:4 * AC])).astype(BF)
    held[1].wait()
    gatt = (nt(gbr, wo[...]) + nt(gao, b4[:, AC:2 * AC])).astype(BF)
    acc[:, 4 * D:5 * D] += nn(tr(gao), att)
    acc[:, 5 * D:6 * D] += nn(tr(ao), gbr)
    acc[:, 6 * D:7 * D] += nn(tr(gar), flatten(x2b[...]))
    acc[:, 7 * D:] += nn(tr(ar), gl)
    attb[...] = gatt.reshape(n, LP, D)

    lane = lax.broadcasted_iota(jnp.int32, (LP, 2 * HEAD), 1)
    keyok = lax.broadcasted_iota(jnp.int32, (LP, LP), 0) < LEN
    drow = lax.broadcasted_iota(jnp.int32, (2 * HEAD, LP), 0)
    scale = 1.0 / math.sqrt(HEAD)

    def image(i, carry):
        for h in range(HEADS // 2):
            at = h * 2 * HEAD
            q = qkvb[i, :, at:at + 2 * HEAD]
            k = qkvb[i, :, D + at:D + at + 2 * HEAD]
            v = qkvb[i, :, 2 * D + at:2 * D + at + 2 * HEAD]
            go = attb[i, :, at:at + 2 * HEAD]
            kt = tr(k)
            dq, dk, dv = [], [], []
            for half in range(2):
                mine = (lane >= HEAD) if half else (lane < HEAD)
                s = nt(k, jnp.where(mine, q, jnp.zeros_like(q))) * scale
                s = jnp.where(keyok, s, -1e30)
                ex = jnp.exp(s - jnp.max(s, axis=0, keepdims=True))
                p = ex * (1.0 / jnp.sum(ex, axis=0, keepdims=True))
                dv.append(nn(p.astype(BF), go))
                dp = nt(v, jnp.where(mine, go, jnp.zeros_like(go)))
                gs = (p * (dp - jnp.sum(dp * p, axis=0, keepdims=True))).astype(BF)
                dk.append(nn(gs, q))
                dq.append(nn(kt, gs))
            dqt = jnp.where(drow < HEAD, dq[0], dq[1]) * scale
            gq[i, :, at:at + 2 * HEAD] = jnp.transpose(dqt).astype(BF)
            gq[i, :, D + at:D + at + 2 * HEAD] = (jnp.where(lane < HEAD, dk[0], dk[1]) * scale).astype(BF)
            gq[i, :, 2 * D + at:2 * D + at + 2 * HEAD] = jnp.where(lane < HEAD, dv[0], dv[1]).astype(BF)
        return carry

    lax.fori_loop(0, n, image, 0)
    for c in held[2:]:
        c.wait()
    gqkv = flatten(gq[...])
    gaq = (mask * nn(gqkv, a2t[...])).astype(BF)
    unit1, inv1 = norm_parts(padded(xb, None))
    x1 = (unit1 * g_ref[0:1, :]).astype(BF)
    acc[:, 0:D] += nn(tr(gaq), x1)
    acc[:, D:4 * D] += nn(tr(aq), gqkv)
    gone = nt(gaq, b4[:, 0:AC])
    for j, w in enumerate((wq, wk, wv)):
        gone = gone + nt(gqkv[:, j * D:(j + 1) * D], w[...])
    hid[...] = gin[...] + norm_back(gone, unit1, inv1, g_ref[0:1, :])
    for i in range(n):
        igb[i] = hid[i * LP:i * LP + LEN, :].astype(BF)
    out = pltpu.make_async_copy(igb, ig_ref.at[lo:lo + n], osem.at[0])
    out.start()
    if last:
        for c in range(acc.shape[1] // AC):
            flat[c * AC:(c + 1) * AC, :] = jnp.transpose(acc[:, c * AC:(c + 1) * AC])
        half = mine_ref.shape[0]

        def place(p, carry):
            for ref, at in ((mine_ref, 0), (other_ref, half)):
                dev = order[at + p]
                row, base = 0, 0
                for w in (1, 3, 1, 1, 1):
                    here = pl.ds(base + w * r * dev, w * r)
                    if r % 8 == 0:
                        here = pl.ds(pl.multiple_of(base + w * r * dev, 8), w * r)
                    ref[p, row:row + w * r, :] = flat[here, :].astype(BF)
                    row += w * r
                    base += w * D
                ref[p, row:row + NE, :] = flat[7 * D:7 * D + NE, :].astype(BF)
            return carry

        lax.fori_loop(0, half, place, 0)
    else:
        acc_ref[...] = acc[...]
    out.wait()


def backward(lo, n, ndev, sets, live, order, block_in, cot, g, gc, gy, probs, mid, qkv, att, x2, ad, gains, wq, wk, wv, wo, b4, a2t,
             rm, prev):
    na = 7 * D + AC
    r = D // ndev
    last = lo > 0
    packed = (ndev // 2, 7 * r + NE, AC)
    anyspace = pl.BlockSpec(memory_space=pl.ANY)
    part = pl.BlockSpec((1, n, LG, D), lambda i, *_: (0, 0, 0, 0))
    in_specs = [whole((n, LG, D)), part, whole((n, LG, D)), whole((8, D)), whole((AC, AC))]
    in_specs += [anyspace] * 14
    args = [g, gc, gy, gains, rm, block_in, cot, probs, mid, qkv, att, x2, ad, b4, wo, wq, wk, wv, a2t]
    rows = n * LP
    scratch = [
        pltpu.VMEM((n, LEN, D), BF), pltpu.VMEM((n, LEN, D), BF), pltpu.VMEM((n, NE, SL), F32), pltpu.VMEM((n, LP, D), F32),
        pltpu.VMEM((n, LP, 3 * D), BF), pltpu.VMEM((n, LP, D), BF), pltpu.VMEM((n, LP, D), BF), pltpu.VMEM((n, LP, 3 * AC), BF),
        pltpu.VMEM((n, LEN, D), BF), pltpu.VMEM((rows, D), F32), pltpu.VMEM((rows, D), F32), pltpu.VMEM((n, LP, 3 * D), BF),
        pltpu.VMEM((AC, na), F32),
    ] + [pltpu.VMEM((D, D), BF)] * 5 + [pltpu.VMEM((3 * D, AC), BF)]
    alias = {}
    if last:
        in_specs += [whole((AC, na)), anyspace]
        args += [prev[1], prev[0]]
        alias = {3 + len(args) - 1: 0}
        scratch.append(pltpu.VMEM((na, AC), F32))
        tails = [packed, packed]
    else:
        tails = [(AC, na)]
    scratch += [pltpu.SemaphoreType.DMA((14,)), pltpu.SemaphoreType.DMA((1,))]
    return pl.pallas_call(
        functools.partial(bwd_kernel, lo, n, last, r),
        grid_spec=pltpu.PrefetchScalarGridSpec(
            num_scalar_prefetch=3,
            grid=(1,),
            in_specs=in_specs,
            out_specs=[anyspace] + [whole(t) for t in tails],
            scratch_shapes=scratch,
        ),
        out_shape=[jax.ShapeDtypeStruct(block_in.shape, BF)] + [jax.ShapeDtypeStruct(t, BF if last else F32) for t in tails],
        input_output_aliases=alias,
        compiler_params=params(1),
        cost_estimate=cost(12 * n),
        name="backward",
    )(sets, live, order, *args)


def on_device(dpn, fsn, block_in, cotangent, image_live, image_set, expert_routes, expert_slots, gain_attn, gain_moe, w_qkv, w_out,
              w_router, w_up, w_down, qkv_first, qkv_second, out_first, out_second, router_first, router_second, up_first,
              up_second, down_first, down_second):
    ndev = dpn * fsn
    nx = 1 << ((fsn.bit_length() - 1) // 2)
    nz = fsn // nx
    ng = dpn // GRP
    r = D // ndev
    hs = w_up.shape[2]
    d = lax.axis_index("dp")
    q = d % GRP
    rings = [
        (nz, "fsdp", [(f, ((f // nx + 1) % nz) * nx + f % nx) for f in range(fsn)]),
        (nx, "fsdp", [(f, (f // nx) * nx + (f % nx + 1) % nx) for f in range(fsn)]),
        (ng, "dp", [(a, (a + GRP) % dpn) for a in range(dpn)]),
    ]

    def swap(v, bit):
        return lax.ppermute(v, "dp", [(a, a ^ bit) for a in range(dpn)])

    rel = [0, 2, 1, 3]

    tr = jnp.transpose
    small = jnp.concatenate(
        [
            qkv_first, out_first, router_first, tr(out_second),
            jnp.concatenate([w_router, gain_attn[:, None], gain_moe[:, None], jnp.zeros((r, AC - NE - 2), BF)], axis=1),
            jnp.zeros((r, AC), BF).at[0, 0:router_second.shape[0]].set(router_second),
        ],
        axis=1,
    )
    a2s = tr(qkv_second).reshape(3, r, AC)
    second = jnp.concatenate([a2s[0], a2s[1], a2s[2], jnp.zeros((r, 3 * AC), BF)], axis=1)
    front = jnp.stack([w_qkv[:, 0:D], w_qkv[:, D:2 * D], w_qkv[:, 2 * D:], w_out, small, second])
    front = lax.all_gather(front.reshape(6 * r, D), AXES, axis=0, tiled=True).reshape(ndev, 6, r, D)
    wq, wk, wv, wo, b4 = (front[:, j].reshape(D, D) for j in range(5))
    a2t = tr(front[:, 5, :, 0:3 * AC].reshape(ndev, r, 3, AC), (0, 2, 1, 3)).reshape(3 * D, AC)
    gains = jnp.concatenate(
        [b4[:, 4 * AC + NE].reshape(1, D), b4[:, 4 * AC + NE + 1].reshape(1, D), jnp.zeros((6, D), BF)], axis=0
    ).astype(F32)
    rm = front[:, 4, 0, 5 * AC:5 * AC + router_second.shape[0]].reshape(AC, NE)
    rm = jnp.pad(rm, ((0, 0), (0, AC - NE)))

    after = lambda v, *deps: lax.optimization_barrier((v,) + deps)[0]

    ef = jnp.concatenate([up_first, tr(down_second, (0, 2, 1))], axis=2).reshape(GRP, EL, r, 2 * AC)
    own = [lax.dynamic_index_in_dim(ef, q ^ j, 0, keepdims=False) for j in range(GRP)]
    sib_ef = swap(jnp.stack([own[1], own[3]]), 1)
    got_ef = swap(jnp.stack([own[2], sib_ef[1]]), 2)
    mine_ef = jnp.stack([own[0], sib_ef[0], got_ef[0], got_ef[1]])
    wpk = jnp.concatenate([tr(w_up, (0, 2, 1)), tr(up_second, (0, 2, 1)), tr(w_down, (0, 2, 1)), tr(down_first, (0, 2, 1))], axis=2)
    wpk = wpk.reshape(GRP, EL, hs, 2 * DW)
    own = [lax.dynamic_index_in_dim(wpk, q ^ j, 0, keepdims=False) for j in range(GRP)]
    sib = swap(jnp.stack([own[1], own[3]], axis=1), 1)
    near = jnp.stack([own[0], sib[:, 0]], axis=1).reshape(EL, 2 * hs, 2 * DW)
    send, _ = lax.optimization_barrier((jnp.stack([own[2], sib[:, 1]], axis=1), got_ef))
    got = swap(send, 2)
    far = got.reshape(EL, 2 * hs, 2 * DW)

    def hop(v, ring):
        return lax.ppermute(v, ring[1], ring[2])

    up = [[(u, ((u // nx + k) % nz) * nx + u % nx) for u in range(fsn)] for k in range(nz)]
    all_ef = jnp.concatenate([mine_ef] + [lax.ppermute(mine_ef, "fsdp", up[k]) for k in range(1, nz)])
    near, all_ef = lax.optimization_barrier((near, all_ef))
    for n, axis, perm in rings[1:]:
        rows = [all_ef]
        for _ in range(n - 1):
            rows.append(lax.ppermute(rows[-1], axis, perm))
        all_ef = jnp.concatenate(rows)
    near_x, all_ef = lax.optimization_barrier((near, all_ef))
    zn, xn, far = lax.optimization_barrier((hop(near, rings[0]), hop(near_x, rings[1]), far))
    z_row = [jnp.concatenate([near, far], axis=1), jnp.concatenate([zn, hop(far, rings[0])], axis=1)]
    x_row = [jnp.concatenate([xn, hop(far, rings[1])], axis=1)]
    z0, x0, block_in_late = lax.optimization_barrier((z_row[1], x_row[0], block_in))
    z_row[1], x_row[0] = z0, x0
    route = expert_routes.reshape(IMG, LEN, 2)
    slot = expert_slots.reshape(IMG, LEN, 2)
    ids = jnp.arange(NE, dtype=jnp.int32)[None, :, None, None]
    ok = (route[:, None] == ids) & (slot[:, None] >= 0) & (image_live[:, None, None, None] > 0)
    mine_slots = jnp.max(jnp.where(ok, slot[:, None], -1), axis=-1)
    mine_slots = jnp.pad(mine_slots, ((0, 8 - IMG), (0, 0), (0, SL - LEN)), constant_values=-1)
    mine_slots = tr(mine_slots, (1, 0, 2))

    def members(v):
        far = swap(v, 2)
        return [v, far, swap(v, 1), swap(far, 1)]

    def group(v):
        return jnp.stack(members(v))

    all_slots = lax.dynamic_slice_in_dim(group(mine_slots), q * EL, EL, axis=1)
    counts = jnp.max(all_slots, axis=(2, 3)) + 1
    steps = (counts + 15) // 16 * 16
    offs = jnp.concatenate([jnp.zeros((1, EL), jnp.int32), jnp.cumsum(steps, axis=0)], axis=0)
    offs = tr(offs).reshape(-1).astype(jnp.int32)
    firsts = jnp.min(jnp.where(all_slots >= 0, all_slots, CAP), axis=3)[:, :, 0:IMG].reshape(-1)
    all_sets = group(image_set).reshape(-1)
    cots = members(after(cotangent, got))

    f = lax.axis_index("fsdp")
    devs = jnp.arange(ndev, dtype=jnp.int32)
    dd, df = devs // fsn, devs % fsn
    gap = lambda mine, other, n: (mine - other) % n
    spot = (gap(d // GRP, dd // GRP, ng) * nx + gap(f % nx, df % nx, nx)) * nz + gap(f // nx, df // nx, nz)
    ef = jnp.take(all_ef, spot * GRP + ((dd % GRP) ^ q), axis=0)
    ef = tr(ef, (1, 0, 2, 3)).reshape(EL, D, 2 * AC)
    u1, d2 = ef[:, :, 0:AC], ef[:, :, AC:]

    offs, firsts, all_sets, block_in_late, *cots = lax.optimization_barrier((offs, firsts, all_sets, block_in_late, *cots))
    qkv, att, mid, x2, ad, probs = attention_forward(block_in_late, image_set, gains, wq, wk, wv, wo, b4, a2t, rm)
    for k in range(2, nz):
        z_row.append(hop(z_row[-1], rings[0]))
        x_row.append(hop(z_row[k - 1], rings[1]))
        if k + 1 < nz:
            z_row[k], x_row[k - 1] = lax.optimization_barrier((z_row[k], x_row[k - 1]))
    x2y = swap(x2, 2)
    x2y, *_ = lax.optimization_barrier((x2y, z_row[min(2, nz - 1)], x_row[1]))
    x2s = [x2, x2y, swap(x2, 1), swap(x2y, 1)]
    gates = lax.dynamic_slice_in_dim(tr(group(jnp.pad(probs, ((0, 8 - IMG), (0, 0), (0, 0)))), (0, 2, 1, 3)), q * EL, EL, axis=1)

    xa, ga, mk = dispatch(offs, firsts, all_sets, all_slots, gates, x2s, cots, u1, d2)
    def parts_of(rows):
        held = [v for row in rows for v in row]
        join = (ng * nx * nz) // 8
        if join <= 1:
            return held
        return [jnp.concatenate(held[k:k + join], axis=1) for k in range(0, len(held), join)]

    early = ng == 1 and nx == 2 and nz == 4
    if early:
        z_row[-1], x_row[-1], xa = lax.optimization_barrier((z_row[-1], x_row[-1], xa))
        tail = [hop(z_row[-1][0:1], rings[1]), hop(x_row[-1][1:2], rings[0])]
        a1, a2, go, gh = expert_some(offs, xa, ga, z_row + x_row)
        go = [go[k] for k in range(3)]
    else:
        x_row.append(hop(z_row[nz - 1], rings[1]))
        rows = [z_row, x_row]
        for _ in range(2, nx):
            rows.append([hop(v, rings[1]) for v in rows[-1]])
        held = [v for row in rows for v in row]
        rows = [held]
        for _ in range(1, ng):
            rows.append([hop(v, rings[2]) for v in rows[-1]])
        units = parts_of(rows)
        a1, a2, go, gh = expert_some(offs, xa, ga, units[:7])
        go = [go[k] for k in range(3)]
        tail = [units[7][0:1], units[7][1:2]]
    ob, gb, gl, gf = expert_last(offs, xa, ga, mk, a1, a2, u1, d2, tail)

    k = jnp.arange(ng * nx * nz, dtype=jnp.int32)
    kg, kx, kz = k // (nx * nz), k // nz % nx, k % nz
    column = (f // nx - kz) % nz * nx + (f % nx - kx) % nx
    rank = ((d // GRP - kg) % ng * GRP)[:, None] + (q ^ jnp.arange(GRP, dtype=jnp.int32))[None, :]
    spot = (rank * fsn + column[:, None]).reshape(-1)
    gf = jnp.take(gf.reshape(EL, 2, ndev, r, AC), spot, axis=2).reshape(EL, 2, ng * nx, nz * GRP * r, AC)
    simple = ng == 1 and nx == 2
    xback = [(v, u) for u, v in rings[1][2]]
    if simple:
        near_x = lax.ppermute(go[2], "fsdp", xback)
        near_x, ob = lax.optimization_barrier((near_x, ob))
        far_send = jnp.concatenate([gh, gl, gf[:, :, 1]], axis=2)
        far_x = lax.ppermute(far_send, "fsdp", xback)
    else:
        far_send = gf

    fe = (q * EL).reshape(1)
    cut = 2
    parts = []
    for lo, n in ((0, cut), (cut, IMG - cut)):
        ym, yf, yp, gm, gfar, gp = combine(lo, n, offs, firsts, fe, ob, gb, all_slots, gates, cots)
        if parts:
            gp, gy = lax.optimization_barrier((gp, parts[-1][-1]))
            parts[-1] = parts[-1][:-1] + (gy,)
        gc = swap(gp, 1)
        gs = (gfar.astype(F32) + gc[1].astype(F32)).astype(BF)
        gc, gs, ob, far_send = lax.optimization_barrier((gc, gs, ob, far_send))
        parts.append((lo, n, (ym, yf, yp), gm, gc, swap(gs, 2)))

    (lo, n, ya, ga1, gca, gya), (lo2, n2, yb, gb1, gcb, gyb) = parts
    spots = jnp.arange(ndev, dtype=jnp.int32)
    order = (q ^ jnp.array([0, 2, 1, 3], jnp.int32)[spots // fsn % GRP]) * fsn + (f + spots % fsn) % fsn
    order = (order if ng == 1 else spots).astype(jnp.int32)
    yca = swap(ya[2], 1)
    ycb = swap(yb[2], 1)
    add = lambda u, v: (u.astype(F32) + v.astype(F32)).astype(BF)
    ga1, gcb = lax.optimization_barrier((ga1, gcb))
    shared = (probs, mid, qkv, att, x2, ad, gains, wq, wk, wv, wo, b4, a2t, rm)
    first = backward(lo, n, ndev, image_set, image_live, order, block_in, cotangent, ga1, gca, gya, *shared, None)

    head, gyb, yca, ycb = lax.optimization_barrier((first[0], gyb, yca, ycb))
    ysend = jnp.concatenate([add(ya[1], yca[1]), add(yb[1], ycb[1])], axis=0)
    if simple:
        near_x, far_x, _ = lax.optimization_barrier((near_x, far_x, gyb))
        cut = GRP * hs
        s0 = add(go[0], near_x)
        s1 = add(go[1], far_x[:, :, 0:2 * cut])
        sf = add(gf[:, :, 0], far_x[:, :, 2 * cut:])
        hid = [s0[:, :, 0:cut], s0[:, :, cut:], s1[:, :, 0:cut], s1[:, :, cut:]]
        cols = [jnp.concatenate([hid[k], sf[:, :, k * GRP * r:(k + 1) * GRP * r]], axis=2) for k in range(nz)]
    else:
        cut = go[0].shape[2] * 4 // (ng * nx * nz)
        cols = []
        for k, v in enumerate(p for pair in go + [jnp.concatenate([gh, gl], axis=2)] for p in jnp.split(pair, pair.shape[2] // cut, axis=2)):
            at = k % nz * GRP * r
            cols.append(jnp.concatenate([v, gf[:, :, k // nz, at:at + GRP * r]], axis=2))
        for m, axis, perm in rings[2:0:-1]:
            back = [(v, u) for u, v in perm]
            part = len(cols) // m
            rows = [cols[k * part:(k + 1) * part] for k in range(m)]
            cols = rows[m - 1]
            for k in range(m - 2, -1, -1):
                cols = [add(lax.ppermute(v, axis, back), u) for v, u in zip(cols, rows[k])]
    down = [lax.ppermute(cols[k], "fsdp", [(u, ((u // nx - k) % nz) * nx + u % nx) for u in range(fsn)]) for k in range(1, nz)]
    yy = swap(ysend, 2)
    input_grad, mine, other = backward(lo2, n2, ndev, image_set, image_live, order, block_in, cotangent, gb1, gcb, gyb, *shared,
                                       (head, first[1]))
    mine, other, yy, *down = lax.optimization_barrier((mine, other, yy, *down))
    got_small = swap(other, 1) if ng == 1 else other
    got_small, yy, mid, own_cols, *down = lax.optimization_barrier((got_small, yy, mid, cols[0], *down))
    yya, yyb = yy[0:n], yy[n:]

    eg = (own_cols.astype(F32) + sum(v.astype(F32) for v in down)).astype(BF)
    eg = [jnp.concatenate([eg[:, :, j * hs:(j + 1) * hs], eg[:, :, GRP * hs + j * r:GRP * hs + (j + 1) * r]], axis=2) for j in range(GRP)]
    sib = swap(jnp.stack([eg[1], eg[3]]), 1)
    got = swap(jnp.stack([eg[2], sib[1]]), 2)
    got = jnp.concatenate([eg[0][None], sib[0:1], got], axis=0)
    at = jnp.stack([q ^ j for j in range(GRP)])
    eg = jnp.take(got, jnp.argsort(at), axis=0).reshape(NE, 2, hs + r, AC).astype(F32)
    ff = eg[:, :, hs:]
    eg = tr(eg[:, :, 0:hs], (1, 0, 3, 2))
    outs = []
    for at, m, y, yc, yy in ((lo, n, ya, yca, yya), (lo2, n2, yb, ycb, yyb)):
        total = mid[at:at + m] + y[0].astype(F32) + yc[0].astype(F32) + yy.astype(F32)
        outs.append(total[:, 0:LEN])
    block_out = (jnp.concatenate(outs, axis=0) * image_live.astype(F32)[:, None, None]).astype(BF)

    nrs = router_second.shape[0]
    if ng == 1:
        far = swap(add(mine[fsn:], got_small[fsn:]), 2)
        sm = add(add(mine[0:fsn], got_small[0:fsn]), far)
        total = sm[0].astype(F32)
        for k in range(1, fsn):
            perm = [(u, (u + k) % fsn) for u in range(fsn)]
            total = total + lax.ppermute(sm[k], "fsdp", perm).astype(F32)
        sm = total
    else:
        sm = jnp.concatenate([mine, other], axis=0)
        sm = lax.psum_scatter(sm, AXES, scatter_dimension=0, tiled=False).astype(F32)
    rs = tr(sm[7 * r:7 * r + NE]).reshape(-1)
    rs = lax.dynamic_slice_in_dim(rs, (d * fsn + f) * nrs, nrs)
    return (
        block_out,
        input_grad,
        sm[0:r],
        tr(sm[r:4 * r]),
        sm[4 * r:5 * r],
        tr(sm[5 * r:6 * r]),
        sm[6 * r:7 * r],
        rs,
        ff[:, 0],
        eg[0],
        eg[1],
        tr(ff[:, 1], (0, 2, 1)),
    )


def solution(mesh):
    dpn, fsn = mesh.shape["dp"], mesh.shape["fsdp"]
    both = ("dp", "fsdp")
    return jax.shard_map(
        functools.partial(on_device, dpn, fsn),
        mesh=mesh,
        in_specs=(
            P(both, None, None),
            P(both, None, None),
            P(both),
            P(both),
            P(both, None, None),
            P(both, None, None),
            P(both),
            P(both),
            P(both, None),
            P(both, None),
            P(both, None),
            P(None, None, both),
            P(None, None, both),
            P(both, None),
            P(None, both),
            P(both, None),
            P(None, both),
            P(both, None),
            P(both),
            P(None, both, None),
            P(None, None, both),
            P(None, None, both),
            P(None, None, both),
        ),
        out_specs=(
            P(both, None, None),
            P(both, None, None),
            P(both, None),
            P(None, both),
            P(both, None),
            P(None, both),
            P(both, None),
            P(both),
            P(None, both, None),
            P(None, None, both),
            P(None, None, both),
            P(None, None, both),
        ),
        check_vma=False,
    )
```

```python
import functools
import math

import jax
import jax.numpy as jnp
from jax import lax
from jax.experimental import pallas as pl
from jax.experimental.pallas import tpu as pltpu
from jax.sharding import PartitionSpec as P

D = 768
HEADS = 12
HEAD = 64
NE = 8
LEN = 197
LP = 208
SL = 256
AC = 128
RANK = 16
CAP = 384
IMG = 5
GRP = 4
EL = NE // GRP
ROWS = GRP * CAP
RT = 256
DW = D + AC
WIN = 256
NFIRST = 7
LG = LP + 16
EPS = 1e-06
F32 = jnp.float32
BF = jnp.bfloat16
AXES = ("dp", "fsdp")
VMEM = 60 * 1000 * 1024


def nn(a, b):
    return lax.dot_general(a, b, (((1,), (0,)), ((), ())), preferred_element_type=F32)


def nt(a, b):
    return lax.dot_general(a, b, (((1,), (1,)), ((), ())), preferred_element_type=F32)


def adapter_mask(rows, which):
    lane = lax.broadcasted_iota(jnp.int32, (rows, AC), 1)
    return jnp.where(lane // RANK == which, 1.0, 0.0).astype(F32)


def norm_parts(v):
    mean = jnp.mean(v, axis=-1, keepdims=True)
    cen = v - mean
    var = jnp.mean(cen * cen, axis=-1, keepdims=True)
    inv = lax.rsqrt(var + EPS)
    return cen * inv, inv


def norm_back(g, unit, inv, gain):
    s = g * gain
    return inv * (
        s
        - jnp.mean(s, axis=-1, keepdims=True)
        - unit * jnp.mean(s * unit, axis=-1, keepdims=True)
    )


def params(n):
    return pltpu.CompilerParams(dimension_semantics=("arbitrary",) * n, vmem_limit_bytes=VMEM)


def cost(us):
    return pl.CostEstimate(flops=int(us * 1.15e9), transcendentals=0, bytes_accessed=0)


def whole(shape):
    zeros = (0,) * len(shape)
    return pl.BlockSpec(shape, lambda *_: zeros, pipeline_mode=pl.Buffered(1))


def per_image(shape):
    rest = (0,) * (len(shape) - 1)
    return pl.BlockSpec(shape, lambda i, *_: (i,) + rest)


def fwd_kernel(sets, x_ref, g_ref, wq, wk, wv, wo, b4, a2t, rm, qkv_ref, att_ref, mid_ref, x2_ref, ad_ref, pr_ref, hid):
    mask = adapter_mask(LP, sets[pl.program_id(0)])
    hid[...] = jnp.zeros((LP, D), F32)
    hid[0:LEN, :] = x_ref[0].astype(F32)
    hidden = hid[...]
    unit, _ = norm_parts(hidden)
    x1 = (unit * g_ref[0:1, :]).astype(BF)
    aq = (mask * nn(x1, b4[:, 0:AC])).astype(BF)
    ad_ref[0, :, 0:AC] = aq
    for j, w in enumerate((wq, wk, wv)):
        part = nn(x1, w[...]) + nt(aq, a2t[j * D:(j + 1) * D, :])
        qkv_ref[0, :, j * D:(j + 1) * D] = part.astype(BF)
    lane = lax.broadcasted_iota(jnp.int32, (LP, 2 * HEAD), 1)
    keyok = lax.broadcasted_iota(jnp.int32, (LP, LP), 1) < LEN
    scale = 1.0 / math.sqrt(HEAD)
    for h in range(HEADS // 2):
        at = h * 2 * HEAD
        q = qkv_ref[0, :, at:at + 2 * HEAD]
        k = qkv_ref[0, :, D + at:D + at + 2 * HEAD]
        v = qkv_ref[0, :, 2 * D + at:2 * D + at + 2 * HEAD]
        outs = []
        for half in range(2):
            mine = (lane >= HEAD) if half else (lane < HEAD)
            s = nt(jnp.where(mine, q, jnp.zeros_like(q)), k) * scale
            s = jnp.where(keyok, s, -1e30)
            e = jnp.exp(s - jnp.max(s, axis=-1, keepdims=True))
            p = e * (1.0 / jnp.sum(e, axis=-1, keepdims=True))
            outs.append(nn(p.astype(BF), v))
        att_ref[0, :, at:at + 2 * HEAD] = jnp.where(lane < HEAD, outs[0], outs[1]).astype(BF)
    att = att_ref[0]
    ao = (mask * nn(att, b4[:, AC:2 * AC])).astype(BF)
    ad_ref[0, :, AC:2 * AC] = ao
    middle = hidden + nn(att, wo[...]) + nt(ao, b4[:, 3 * AC:4 * AC])
    mid_ref[0] = middle
    unit2, _ = norm_parts(middle)
    x2 = (unit2 * g_ref[1:2, :]).astype(BF)
    x2_ref[0] = x2
    ar = (mask * nn(x2, b4[:, 2 * AC:3 * AC])).astype(BF)
    ad_ref[0, :, 2 * AC:3 * AC] = ar
    logits = nn(x2, b4[:, 4 * AC:5 * AC]) + nn(ar, rm[...])
    elane = lax.broadcasted_iota(jnp.int32, (LP, AC), 1)
    logits = jnp.where(elane < NE, logits, -1e30)
    e = jnp.exp(logits - jnp.max(logits, axis=-1, keepdims=True))
    probs = e * (1.0 / jnp.sum(e, axis=-1, keepdims=True))
    padded = jnp.concatenate([probs, jnp.zeros((SL - LP, AC), F32)], axis=0)
    pr_ref[0] = jnp.transpose(padded)[0:NE, :]


def attention_forward(block_in, sets, gains, wq, wk, wv, wo, b4, a2t, rm):
    n = block_in.shape[0]
    sq = whole((D, D))
    return pl.pallas_call(
        fwd_kernel,
        grid_spec=pltpu.PrefetchScalarGridSpec(
            num_scalar_prefetch=1,
            grid=(n,),
            in_specs=[per_image((1, LEN, D)), whole((8, D)), sq, sq, sq, sq, sq, whole((3 * D, AC)), whole((AC, AC))],
            out_specs=[
                per_image((1, LP, 3 * D)),
                per_image((1, LP, D)),
                per_image((1, LP, D)),
                per_image((1, LP, D)),
                per_image((1, LP, 3 * AC)),
                per_image((1, NE, SL)),
            ],
            scratch_shapes=[pltpu.VMEM((LP, D), F32)],
        ),
        out_shape=[
            jax.ShapeDtypeStruct((n, LP, 3 * D), BF),
            jax.ShapeDtypeStruct((n, LP, D), BF),
            jax.ShapeDtypeStruct((n, LP, D), F32),
            jax.ShapeDtypeStruct((n, LP, D), BF),
            jax.ShapeDtypeStruct((n, LP, 3 * AC), BF),
            jax.ShapeDtypeStruct((n, NE, SL), F32),
        ],
        compiler_params=params(1),
        cost_estimate=cost(28),
        name="attention_forward",
    )(sets, block_in, gains, wq, wk, wv, wo, b4, a2t, rm)


def window(base, first, limit):
    at = jnp.minimum(base + first // 16 * 16, limit - WIN)
    return pl.multiple_of(at, 16)


def fetch_blocks(at_start, b, sets):
    def copies(k):
        return [pltpu.make_async_copy(refs[k], buf.at[k], sems.at[k]) for refs, buf, sems in sets]

    @pl.when(at_start)
    def _():
        for k in range(GRP):
            for c in copies(k):
                c.start()

    for k in range(GRP):
        @pl.when(b == k)
        def _(k=k):
            for c in copies(k):
                c.wait()


def dispatch_kernel(offs, firsts, sets, slot_ref, gate_ref, *refs):
    x2_refs, cot_refs = refs[0:GRP], refs[GRP:2 * GRP]
    u1_ref, d2_ref, xa_ref, ga_ref, mk_ref, acc, cpad, x2_buf, cot_buf, x2_sem, cot_sem = refs[2 * GRP:]
    e = pl.program_id(0)
    b = pl.program_id(1)

    @pl.when(e == 0)
    def _():
        fetch_blocks(b == 0, b, ((x2_refs, x2_buf, x2_sem), (cot_refs, cot_buf, cot_sem)))

    @pl.when(b == 0)
    def _():
        xa_ref[...] = jnp.zeros_like(xa_ref)
        ga_ref[...] = jnp.zeros_like(ga_ref)
        mk_ref[...] = jnp.zeros_like(mk_ref)

    acc[...] = jnp.zeros_like(acc)
    cpad[...] = jnp.zeros_like(cpad)
    gcol = jnp.transpose(gate_ref[0, 0])
    rows = lax.broadcasted_iota(jnp.int32, (WIN, LP), 0)
    for i in range(IMG):
        first = firsts[(b * EL + e) * IMG + i]

        @pl.when(first < CAP)
        def _():
            at = window(0, first, CAP)
            here = pl.ds(at, WIN)
            pick = jnp.where(rows + at == slot_ref[0, 0, i:i + 1, 0:LP], 1.0, 0.0).astype(BF)
            cpad[0:LEN, :] = cot_buf[b, i].astype(F32)
            gg = (cpad[...] * gcol[0:LP, i:i + 1]).astype(BF)
            acc[here, 0:D] += nn(pick, x2_buf[b, i])
            acc[here, D:2 * D] += nn(pick, gg)
            acc[here, 2 * D:] += nn(pick, adapter_mask(LP, sets[b * IMG + i]).astype(BF))

    mk = acc[:, 2 * D:]
    xs = acc[:, 0:D].astype(BF)
    gs = acc[:, D:2 * D].astype(BF)
    at = pl.multiple_of(offs[e * (GRP + 1) + b], 16)
    here = pl.ds(at, CAP)
    xa_ref[0, here, 0:D] = xs
    xa_ref[0, here, D:DW] = (mk * nn(xs, u1_ref[0])).astype(BF)
    ga_ref[0, here, 0:D] = gs
    ga_ref[0, here, D:DW] = (mk * nn(gs, d2_ref[0])).astype(BF)
    mk_ref[0, here, :] = mk.astype(BF)


def dispatch(offs, firsts, sets, slots, gates, x2, cot, u1, d2):
    return pl.pallas_call(
        dispatch_kernel,
        grid_spec=pltpu.PrefetchScalarGridSpec(
            num_scalar_prefetch=3,
            grid=(EL, GRP),
            in_specs=[
                pl.BlockSpec((1, 1, 8, SL), lambda e, b, *_: (b, e, 0, 0)),
                pl.BlockSpec((1, 1, 8, SL), lambda e, b, *_: (b, e, 0, 0)),
            ] + [pl.BlockSpec(memory_space=pl.ANY)] * (2 * GRP) + [
                pl.BlockSpec((1, D, AC), lambda e, b, *_: (e, 0, 0)),
                pl.BlockSpec((1, D, AC), lambda e, b, *_: (e, 0, 0)),
            ],
            out_specs=[
                pl.BlockSpec((1, ROWS, DW), lambda e, b, *_: (e, 0, 0)),
                pl.BlockSpec((1, ROWS, DW), lambda e, b, *_: (e, 0, 0)),
                pl.BlockSpec((1, ROWS, AC), lambda e, b, *_: (e, 0, 0)),
            ],
            scratch_shapes=[
                pltpu.VMEM((CAP, 2 * D + AC), F32), pltpu.VMEM((LP, D), F32), pltpu.VMEM((GRP, IMG, LP, D), BF),
                pltpu.VMEM((GRP, IMG, LEN, D), BF), pltpu.SemaphoreType.DMA((GRP,)), pltpu.SemaphoreType.DMA((GRP,)),
            ],
        ),
        out_shape=[
            jax.ShapeDtypeStruct((EL, ROWS, DW), BF),
            jax.ShapeDtypeStruct((EL, ROWS, DW), BF),
            jax.ShapeDtypeStruct((EL, ROWS, AC), BF),
        ],
        compiler_params=params(2),
        cost_estimate=cost(1),
        name="dispatch",
    )(offs, firsts, sets, slots, gates, *x2, *cot, u1, d2)


def flip(v):
    return jnp.transpose(v.astype(F32)).astype(BF)


def gelu_parts(pre):
    c0 = math.sqrt(2.0 / math.pi)
    sq = pre * pre
    th = jnp.tanh(c0 * pre * (1.0 + 0.044715 * sq))
    half = 0.5 * (1.0 + th)
    slope = half + 0.5 * pre * (1.0 - th * th) * (c0 * (1.0 + 3 * 0.044715 * sq))
    return pre * half, slope


def tile_products(x, g, xt, gt, wbuf, cur, width, put):
    wu = wbuf[cur, 0:width, 0:DW]
    wd = wbuf[cur, 0:width, DW:2 * DW]
    act, slope = gelu_parts(nt(x, wu))
    act = act.astype(BF)
    gp = (slope * nt(g, wd)).astype(BF)
    t1, t2 = nn(act, wd), nn(gp, wu)
    put(nn(xt, gp), nn(gt, act))
    return t1, t2


def tall_tiles(offs, e):
    total = offs[e * (GRP + 1) + GRP]
    tall = (total + RT - 1) // (2 * RT)
    return tall, (total > tall * 2 * RT).astype(jnp.int32)


def live_tiles(offs, e):
    tall, tail = tall_tiles(offs, e)
    return 2 * tall + tail


def over_tiles(offs, e, step):
    tall, tail = tall_tiles(offs, e)

    def one(t, carry):
        step(2 * t, 2)
        return carry

    lax.fori_loop(0, tall, one, 0)

    @pl.when(tail > 0)
    def _():
        step(2 * tall, 1)


def each_tile(limit, do):
    for t in range(ROWS // RT):
        @pl.when(t < limit)
        def _(t=t):
            do(t)


def unit_copies(units, wbuf, slot, sems, s, e):
    hu = units[0].shape[1]
    return [pltpu.make_async_copy(u.at[e], wbuf.at[slot, pl.ds(k * hu, hu)], sems.at[s, k]) for k, u in enumerate(units)]


def expert_some_kernel(nu, offs, xa, ga, *refs):
    units, refs = refs[:nu], refs[nu:]
    steps, odd = (nu + 1) // 2, nu % 2
    a1, a2, go_ref, *refs = refs
    gh_ref = refs.pop(0) if odd else None
    xb, gb, s1, s2, b1, b2, at_ref, wbuf, gacc, wsem, isem, osem = refs
    chunks = [units[k:k + 2] for k in range(0, nu, 2)]
    e, p = pl.program_id(0), pl.program_id(1)
    s = e * steps + p
    full, short = 2 * units[0].shape[1], units[0].shape[1]

    def rows(t):
        return pl.ds(t * RT, RT)

    def incoming(v, t):
        pairs = [(xa, xb), (ga, gb)]
        return [pltpu.make_async_copy(src.at[v, rows(t)], dst.at[v, rows(t)], isem.at[v, t, k]) for k, (src, dst) in enumerate(pairs)]

    def outgoing(v, t):
        return [pltpu.make_async_copy(src.at[v, rows(t)], dst.at[v, rows(t)], osem.at[v, t, k])
                for k, (src, dst) in enumerate(((b1, a1), (b2, a2)))]

    def weights(k):
        return unit_copies(chunks[k % steps], wbuf, k % 2, wsem, k, k // steps)

    @pl.when(s == 0)
    def _():
        for c in weights(0):
            c.start()
        for v in range(EL):
            each_tile(live_tiles(offs, v), lambda t, v=v: [c.start() for c in incoming(v, t)])

    for k in range(EL * steps):
        @pl.when(s == k)
        def _(k=k):
            if k + 1 < EL * steps:
                for c in weights(k + 1):
                    c.start()
            if k % steps == 0:
                each_tile(live_tiles(offs, k // steps), lambda t: [c.wait() for c in incoming(k // steps, t)])
            for c in weights(k):
                c.wait()

    tiles = live_tiles(offs, e)
    cur = s % 2

    @pl.when(p == 0)
    def _():
        def turn(t, carry):
            here = pl.ds(pl.multiple_of(t * RT, RT), RT)
            at_ref[0, :, here] = flip(xb[e, here, D:DW])
            at_ref[1, :, here] = flip(gb[e, here, D:DW])
            s1[e, here, :] = jnp.zeros((RT, DW), F32)
            s2[e, here, :] = jnp.zeros((RT, DW), F32)
            return carry

        lax.fori_loop(0, tiles, turn, 0)

    def run(width, ref, done):
        gacc[:, :, 0:width] = jnp.zeros((2, AC, width), F32)

        def put(gu, gd):
            gacc[0, :, 0:width] += gu
            gacc[1, :, 0:width] += gd

        def step(t, height):
            here = pl.ds(pl.multiple_of(t * RT, RT), height * RT)
            t1, t2 = tile_products(xb[e, here, :], gb[e, here, :], at_ref[0, :, here], at_ref[1, :, here], wbuf, cur, width, put)
            if done:
                b1[e, here, :] = (s1[e, here, :] + t1).astype(BF)
                b2[e, here, :] = (s2[e, here, :] + t2).astype(BF)
            else:
                s1[e, here, :] += t1
                s2[e, here, :] += t2

        over_tiles(offs, e, step)
        for k in range(2):
            ref[k] = jnp.transpose(gacc[k, :, 0:width]).astype(BF)

    @pl.when(p < steps - 1)
    def _():
        run(full, go_ref.at[0, 0], False)

    @pl.when(p == steps - 1)
    def _():
        run(short, gh_ref.at[0], True)

    @pl.when(p == steps - 1)
    def _():
        for v in range(EL):
            @pl.when(e == v)
            def _(v=v):
                each_tile(tiles, lambda t: [c.start() for c in outgoing(v, t)])

    @pl.when(s == EL * steps - 1)
    def _():
        for v in range(EL):
            each_tile(live_tiles(offs, v), lambda t, v=v: [c.wait() for c in outgoing(v, t)])


def expert_some(offs, xa, ga, units):
    hu, nu = units[0].shape[1], len(units)
    steps, odd = (nu + 1) // 2, nu % 2
    nt_ = ROWS // RT
    anyspace = pl.BlockSpec(memory_space=pl.ANY)
    short_spec = [pl.BlockSpec((1, 2, hu, AC), lambda e, p, *_: (e, 0, 0, 0))] * odd
    short_shape = [jax.ShapeDtypeStruct((EL, 2, hu, AC), BF)] * odd
    return pl.pallas_call(
        functools.partial(expert_some_kernel, nu),
        grid_spec=pltpu.PrefetchScalarGridSpec(
            num_scalar_prefetch=1,
            grid=(EL, steps),
            in_specs=[anyspace] * (2 + nu),
            out_specs=[anyspace, anyspace,
                       pl.BlockSpec((1, 1, 2, 2 * hu, AC), lambda e, p, *_: (jnp.minimum(p, steps - 1 - odd), e, 0, 0, 0))] + short_spec,
            scratch_shapes=[
                pltpu.VMEM((EL, ROWS, DW), BF), pltpu.VMEM((EL, ROWS, DW), BF), pltpu.VMEM((EL, ROWS, DW), F32),
                pltpu.VMEM((EL, ROWS, DW), F32), pltpu.VMEM((EL, ROWS, DW), BF), pltpu.VMEM((EL, ROWS, DW), BF), pltpu.VMEM((2, AC, ROWS), BF), pltpu.VMEM((2, 2 * hu, 2 * DW), BF),
                pltpu.VMEM((2, AC, 2 * hu), F32), pltpu.SemaphoreType.DMA((EL * steps, 2)), pltpu.SemaphoreType.DMA((EL, nt_, 4)),
                pltpu.SemaphoreType.DMA((EL, nt_, 2)),
            ],
        ),
        out_shape=[
            jax.ShapeDtypeStruct((EL, ROWS, DW), BF),
            jax.ShapeDtypeStruct((EL, ROWS, DW), BF),
            jax.ShapeDtypeStruct((steps - odd, EL, 2, 2 * hu, AC), BF),
        ] + short_shape,
        compiler_params=params(2),
        cost_estimate=cost(9 * nu),
        name="expert_some",
    )(offs, xa, ga, *units)


def expert_last_kernel(offs, mk_ref, u1_ref, d2_ref, xa, ga, a1, a2, w0, w1, ob, gb, go_ref, gf_ref,
                       xs, gs, s1, s2, os, hs, wbuf, gacc, facc, wsem, isem, osem):
    e = pl.program_id(0)
    tiles = live_tiles(offs, e)

    def rows(t):
        return pl.ds(t * RT if isinstance(t, int) else pl.multiple_of(t * RT, RT), RT)

    def incoming(v, t):
        return [pltpu.make_async_copy(src.at[v, rows(t)], dst.at[v, rows(t)], isem.at[v, t, k])
                for k, (src, dst) in enumerate(((xa, xs), (ga, gs), (a1, s1), (a2, s2)))]

    def outgoing(v, t):
        return [pltpu.make_async_copy(src.at[v, rows(t)], dst.at[v, rows(t)], osem.at[v, t, k])
                for k, (src, dst) in enumerate(((os, ob), (hs, gb)))]

    def weights(v):
        return unit_copies(((w0, w1)[v],), wbuf, v, wsem, v, 0)

    @pl.when(e == 0)
    def _():
        for v in range(EL):
            for c in weights(v):
                c.start()
            each_tile(live_tiles(offs, v), lambda t, v=v: [c.start() for c in incoming(v, t)])

    gacc[...] = jnp.zeros_like(gacc)
    facc[...] = jnp.zeros_like(facc)
    for v in range(EL):
        @pl.when(e == v)
        def _(v=v):
            for c in weights(v):
                c.wait()

    def put(gu, gd):
        gacc[0] += gu
        gacc[1] += gd

    def step(t, height):
        here = pl.ds(pl.multiple_of(t * RT, RT), height * RT)
        for k in range(height):
            for c in incoming(e, t + k):
                c.wait()
        x = xs[e, here, :]
        g = gs[e, here, :]
        t1, t2 = tile_products(x, g, flip(x[:, D:DW]), flip(g[:, D:DW]), wbuf, e, wbuf.shape[1], put)
        t1 = s1[e, here, :].astype(F32) + t1
        t2 = s2[e, here, :].astype(F32) + t2
        mk = mk_ref[0, here, :].astype(F32)
        adt = (mk * t1[:, D:DW]).astype(BF)
        aut = (mk * t2[:, D:DW]).astype(BF)
        os[e, here, :] = (t1[:, 0:D] + nt(adt, d2_ref[0])).astype(BF)
        hs[e, here, :] = (t2[:, 0:D] + nt(aut, u1_ref[0])).astype(BF)
        for k in range(height):
            for c in outgoing(e, t + k):
                c.start()
        facc[0] += nn(flip(aut), x[:, 0:D])
        facc[1] += nn(flip(adt), g[:, 0:D])

    over_tiles(offs, e, step)
    @pl.when(tiles < ROWS // RT)
    def _():
        here = rows(tiles)
        os[e, here, :] = jnp.zeros((RT, D), BF)
        hs[e, here, :] = jnp.zeros((RT, D), BF)
        for c in outgoing(e, tiles):
            c.start()

    for j in range(2):
        go_ref[0, j] = jnp.transpose(gacc[j]).astype(BF)
        gf_ref[0, j] = jnp.transpose(facc[j]).astype(BF)

    @pl.when(e == EL - 1)
    def _():
        for v in range(EL):
            each_tile(live_tiles(offs, v) + 1, lambda t, v=v: [c.wait() for c in outgoing(v, t)])


def expert_last(offs, xa, ga, mk, a1, a2, u1, d2, units):
    hu = units[0].shape[1]
    nt_ = ROWS // RT
    each = lambda *shape: pl.BlockSpec((1,) + shape, lambda e, *_: (e,) + (0,) * len(shape))
    anyspace = pl.BlockSpec(memory_space=pl.ANY)
    return pl.pallas_call(
        expert_last_kernel,
        grid_spec=pltpu.PrefetchScalarGridSpec(
            num_scalar_prefetch=1,
            grid=(EL,),
            in_specs=[each(ROWS, AC), each(D, AC), each(D, AC)] + [anyspace] * 6,
            out_specs=[anyspace, anyspace, each(2, hu, AC), each(2, D, AC)],
            scratch_shapes=[
                pltpu.VMEM((EL, ROWS, DW), BF), pltpu.VMEM((EL, ROWS, DW), BF), pltpu.VMEM((EL, ROWS, DW), BF),
                pltpu.VMEM((EL, ROWS, DW), BF), pltpu.VMEM((EL, ROWS, D), BF), pltpu.VMEM((EL, ROWS, D), BF),
                pltpu.VMEM((EL, hu, 2 * DW), BF), pltpu.VMEM((2, AC, hu), F32), pltpu.VMEM((2, AC, D), F32),
                pltpu.SemaphoreType.DMA((EL, 1)), pltpu.SemaphoreType.DMA((EL, nt_, 4)), pltpu.SemaphoreType.DMA((EL, nt_, 2)),
            ],
        ),
        out_shape=[
            jax.ShapeDtypeStruct((EL, ROWS, D), BF),
            jax.ShapeDtypeStruct((EL, ROWS, D), BF),
            jax.ShapeDtypeStruct((EL, 2, hu, AC), BF),
            jax.ShapeDtypeStruct((EL, 2, D, AC), BF),
        ],
        compiler_params=params(1),
        cost_estimate=cost(18),
        name="expert_last",
    )(offs, mk, u1, d2, xa, ga, a1, a2, *units)


def combine_kernel(lo, n, offs, firsts, first_expert, ob, gb, slot_ref, gate_ref, *refs):
    b = pl.program_id(0)
    cot_refs, outs = refs[:GRP], refs[GRP:]
    y_ref, g_ref, cot_buf, cot_sem = outs[6:]
    fetch_blocks(b == 0, b, (([r.at[lo:lo + n] for r in cot_refs], cot_buf, cot_sem),))
    lanes = lax.broadcasted_iota(jnp.int32, (LP, WIN), 1)
    dlane = lax.broadcasted_iota(jnp.int32, (LP, AC), 1)
    scol = [jnp.transpose(slot_ref[0, e].astype(F32)) for e in range(EL)]
    gcol = [jnp.transpose(gate_ref[0, e]) for e in range(EL)]
    for i in range(n):
        y = jnp.zeros((LP, D), F32)
        g = jnp.zeros((LP, D), F32)
        dots = jnp.zeros((LP, AC), F32)
        cot = jnp.concatenate([cot_buf[b, i].astype(F32), jnp.zeros((LP - LEN, D), F32)], axis=0)
        for e in range(EL):
            first = firsts[(b * EL + e) * IMG + lo + i]
            first = jnp.where(first < CAP, first, 0)
            base = offs[e * (GRP + 1) + b]
            at = window(base, first, ROWS)
            here = pl.ds(at, WIN)
            slot = scol[e][0:LP, lo + i:lo + i + 1]
            pick = jnp.where(slot == (lanes + (at - base)).astype(F32), 1.0, 0.0).astype(BF)
            ye = nn(pick, ob[e, here, :])
            g = g + nn(pick, gb[e, here, :])
            y = y + gcol[e][0:LP, lo + i:lo + i + 1] * ye
            dot = jnp.sum(ye * cot, axis=-1, keepdims=True)
            dots = dots + jnp.where(dlane == first_expert[0] + e, dot, 0.0)
        y_ref[i] = y.astype(BF)
        g_ref[i, 0:LP] = g.astype(BF)
        full = jnp.transpose(jnp.concatenate([dots, jnp.zeros((SL - LP, AC), F32)], axis=0))[0:16, :]
        high = full.astype(BF)
        g_ref[i, LP:LG, 0:SL] = high
        g_ref[i, LP:LG, SL:2 * SL] = (full - high.astype(F32)).astype(BF)
        g_ref[i, LP:LG, 2 * SL:] = jnp.zeros((LG - LP, D - 2 * SL), BF)
    for v, mine, far, core in ((y_ref, outs[0], outs[1], outs[2]), (g_ref, outs[3], outs[4], outs[5])):
        for when, ref in ((0, mine), (1, far), (2, core), (3, core)):
            @pl.when(b == when)
            def _(ref=ref, v=v):
                if len(ref.shape) == 4:
                    ref[0] = v[...]
                else:
                    ref[...] = v[...]


def combine(lo, n, offs, firsts, first_expert, ob, gb, slots, gates, cot):
    block = lambda *shape: pl.BlockSpec((1,) + shape, lambda b, *_: (b,) + (0,) * len(shape))
    return pl.pallas_call(
        functools.partial(combine_kernel, lo, n),
        grid_spec=pltpu.PrefetchScalarGridSpec(
            num_scalar_prefetch=3,
            grid=(GRP,),
            in_specs=[whole((EL, ROWS, D)), whole((EL, ROWS, D)), block(EL, 8, SL), block(EL, 8, SL)] + [pl.BlockSpec(memory_space=pl.ANY)] * GRP,
            out_specs=[spec for rows in (LP, LG) for spec in (
                whole((n, rows, D)), whole((n, rows, D)), pl.BlockSpec((1, n, rows, D), lambda b, *_: (jnp.maximum(b - 2, 0), 0, 0, 0)))],
            scratch_shapes=[pltpu.VMEM((n, LP, D), BF), pltpu.VMEM((n, LG, D), BF), pltpu.VMEM((GRP, n, LEN, D), BF),
                            pltpu.SemaphoreType.DMA((GRP,))],
        ),
        out_shape=[jax.ShapeDtypeStruct(shape, BF) for rows in (LP, LG) for shape in ((n, rows, D), (n, rows, D), (2, n, rows, D))],
        compiler_params=params(1),
        cost_estimate=cost(6 * n),
        name="combine",
    )(offs, firsts, first_expert, ob, gb, slots, gates, *cot)


def bwd_kernel(lo, n, last, r, sets, live, order, go_ref, gc_ref, gy_ref, g_ref, rm, *refs):
    sources, frozen, refs = refs[:8], refs[8:14], refs[14:]
    if last:
        pacc, _, ig_ref, mine_ref, other_ref, *refs = refs
    else:
        ig_ref, acc_ref, *refs = refs
    xb, cb, pb, midb, qkvb, attb, x2b, adb, igb, hid, gin, gq, acc, b4, wo, wq, wk, wv, a2t = refs[:19]
    flat = refs[19] if last else None
    sems, osem = refs[-2:]
    rows = n * LP
    loads = [pltpu.make_async_copy(src.at[lo:lo + n], dst, sems.at[k])
             for k, (src, dst) in enumerate(zip(sources, (xb, cb, pb, midb, qkvb, attb, x2b, adb)))]
    held = [pltpu.make_async_copy(src, dst, sems.at[8 + k]) for k, (src, dst) in enumerate(zip(frozen, (b4, wo, wq, wk, wv, a2t)))]
    for c in held[:1] + loads + held[1:]:
        c.start()
    acc[...] = pacc[...] if last else jnp.zeros_like(acc)
    tr = flip
    flatten = lambda v: v.reshape(rows, v.shape[-1])
    stack = lambda f: jnp.concatenate([f(i) for i in range(n)], axis=0)
    mask = stack(lambda i: adapter_mask(LP, sets[lo + i]))
    zrow = jnp.zeros((AC - NE, SL), F32)
    gprobs = []
    for i in range(n):
        gsum = go_ref[i].astype(F32) + gc_ref[0, i].astype(F32) + gy_ref[i].astype(F32)
        gin[i * LP:(i + 1) * LP, :] = gsum[0:LP]
        dots = gsum[LP:LP + NE, 0:SL] + gsum[LP:LP + NE, SL:2 * SL]
        gprobs.append(jnp.transpose(jnp.concatenate([dots, zrow], axis=0))[0:LP, :])
    gprobs = jnp.concatenate(gprobs, axis=0)
    for c in held[:1] + loads:
        c.wait()

    def padded(buf, scale):
        hid[...] = jnp.zeros((rows, D), F32)
        for i in range(n):
            v = buf[i].astype(F32)
            hid[i * LP:i * LP + LEN, :] = v if scale is None else v * scale(i)
        return hid[...]

    aq = flatten(adb[:, :, 0:AC])
    ao = flatten(adb[:, :, AC:2 * AC])
    ar = flatten(adb[:, :, 2 * AC:3 * AC])
    att = flatten(attb[...])
    elane = lax.broadcasted_iota(jnp.int32, (rows, AC), 1)
    probs = stack(lambda i: jnp.transpose(jnp.concatenate([pb[i], zrow], axis=0))[0:LP, :])
    gl = probs * (gprobs - jnp.sum(gprobs * probs, axis=-1, keepdims=True))
    gl = jnp.where(elane < NE, gl, 0.0).astype(BF)
    gar = (mask * nt(gl, rm[...])).astype(BF)
    gtwo = gin[...] + nt(gl, b4[:, 4 * AC:5 * AC]) + nt(gar, b4[:, 2 * AC:3 * AC])
    unit2, inv2 = norm_parts(flatten(midb[...]))
    gin[...] = padded(cb, lambda i: live[lo + i].astype(F32)) + norm_back(gtwo, unit2, inv2, g_ref[1:2, :])
    gbr = gin[...].astype(BF)
    gao = (mask * nn(gbr, b4[:, 3 * AC:4 * AC])).astype(BF)
    held[1].wait()
    gatt = (nt(gbr, wo[...]) + nt(gao, b4[:, AC:2 * AC])).astype(BF)
    acc[:, 4 * D:5 * D] += nn(tr(gao), att)
    acc[:, 5 * D:6 * D] += nn(tr(ao), gbr)
    acc[:, 6 * D:7 * D] += nn(tr(gar), flatten(x2b[...]))
    acc[:, 7 * D:] += nn(tr(ar), gl)
    attb[...] = gatt.reshape(n, LP, D)

    lane = lax.broadcasted_iota(jnp.int32, (LP, 2 * HEAD), 1)
    keyok = lax.broadcasted_iota(jnp.int32, (LP, LP), 0) < LEN
    drow = lax.broadcasted_iota(jnp.int32, (2 * HEAD, LP), 0)
    scale = 1.0 / math.sqrt(HEAD)

    def image(i, carry):
        for h in range(HEADS // 2):
            at = h * 2 * HEAD
            q = qkvb[i, :, at:at + 2 * HEAD]
            k = qkvb[i, :, D + at:D + at + 2 * HEAD]
            v = qkvb[i, :, 2 * D + at:2 * D + at + 2 * HEAD]
            go = attb[i, :, at:at + 2 * HEAD]
            kt = tr(k)
            dq, dk, dv = [], [], []
            for half in range(2):
                mine = (lane >= HEAD) if half else (lane < HEAD)
                s = nt(k, jnp.where(mine, q, jnp.zeros_like(q))) * scale
                s = jnp.where(keyok, s, -1e30)
                ex = jnp.exp(s - jnp.max(s, axis=0, keepdims=True))
                p = ex * (1.0 / jnp.sum(ex, axis=0, keepdims=True))
                dv.append(nn(p.astype(BF), go))
                dp = nt(v, jnp.where(mine, go, jnp.zeros_like(go)))
                gs = (p * (dp - jnp.sum(dp * p, axis=0, keepdims=True))).astype(BF)
                dk.append(nn(gs, q))
                dq.append(nn(kt, gs))
            dqt = jnp.where(drow < HEAD, dq[0], dq[1]) * scale
            gq[i, :, at:at + 2 * HEAD] = jnp.transpose(dqt).astype(BF)
            gq[i, :, D + at:D + at + 2 * HEAD] = (jnp.where(lane < HEAD, dk[0], dk[1]) * scale).astype(BF)
            gq[i, :, 2 * D + at:2 * D + at + 2 * HEAD] = jnp.where(lane < HEAD, dv[0], dv[1]).astype(BF)
        return carry

    lax.fori_loop(0, n, image, 0)
    for c in held[2:]:
        c.wait()
    gqkv = flatten(gq[...])
    gaq = (mask * nn(gqkv, a2t[...])).astype(BF)
    unit1, inv1 = norm_parts(padded(xb, None))
    x1 = (unit1 * g_ref[0:1, :]).astype(BF)
    acc[:, 0:D] += nn(tr(gaq), x1)
    acc[:, D:4 * D] += nn(tr(aq), gqkv)
    gone = nt(gaq, b4[:, 0:AC])
    for j, w in enumerate((wq, wk, wv)):
        gone = gone + nt(gqkv[:, j * D:(j + 1) * D], w[...])
    hid[...] = gin[...] + norm_back(gone, unit1, inv1, g_ref[0:1, :])
    for i in range(n):
        igb[i] = hid[i * LP:i * LP + LEN, :].astype(BF)
    out = pltpu.make_async_copy(igb, ig_ref.at[lo:lo + n], osem.at[0])
    out.start()
    if last:
        for c in range(acc.shape[1] // AC):
            flat[c * AC:(c + 1) * AC, :] = jnp.transpose(acc[:, c * AC:(c + 1) * AC])
        half = mine_ref.shape[0]

        def place(p, carry):
            for ref, at in ((mine_ref, 0), (other_ref, half)):
                dev = order[at + p]
                row, base = 0, 0
                for w in (1, 3, 1, 1, 1):
                    here = pl.ds(base + w * r * dev, w * r)
                    if r % 8 == 0:
                        here = pl.ds(pl.multiple_of(base + w * r * dev, 8), w * r)
                    ref[p, row:row + w * r, :] = flat[here, :].astype(BF)
                    row += w * r
                    base += w * D
                ref[p, row:row + NE, :] = flat[7 * D:7 * D + NE, :].astype(BF)
            return carry

        lax.fori_loop(0, half, place, 0)
    else:
        acc_ref[...] = acc[...]
    out.wait()


def backward(lo, n, ndev, sets, live, order, block_in, cot, g, gc, gy, probs, mid, qkv, att, x2, ad, gains, wq, wk, wv, wo, b4, a2t,
             rm, prev):
    na = 7 * D + AC
    r = D // ndev
    last = lo > 0
    packed = (ndev // 2, 7 * r + NE, AC)
    anyspace = pl.BlockSpec(memory_space=pl.ANY)
    part = pl.BlockSpec((1, n, LG, D), lambda i, *_: (0, 0, 0, 0))
    in_specs = [whole((n, LG, D)), part, whole((n, LG, D)), whole((8, D)), whole((AC, AC))]
    in_specs += [anyspace] * 14
    args = [g, gc, gy, gains, rm, block_in, cot, probs, mid, qkv, att, x2, ad, b4, wo, wq, wk, wv, a2t]
    rows = n * LP
    scratch = [
        pltpu.VMEM((n, LEN, D), BF), pltpu.VMEM((n, LEN, D), BF), pltpu.VMEM((n, NE, SL), F32), pltpu.VMEM((n, LP, D), F32),
        pltpu.VMEM((n, LP, 3 * D), BF), pltpu.VMEM((n, LP, D), BF), pltpu.VMEM((n, LP, D), BF), pltpu.VMEM((n, LP, 3 * AC), BF),
        pltpu.VMEM((n, LEN, D), BF), pltpu.VMEM((rows, D), F32), pltpu.VMEM((rows, D), F32), pltpu.VMEM((n, LP, 3 * D), BF),
        pltpu.VMEM((AC, na), F32),
    ] + [pltpu.VMEM((D, D), BF)] * 5 + [pltpu.VMEM((3 * D, AC), BF)]
    alias = {}
    if last:
        in_specs += [whole((AC, na)), anyspace]
        args += [prev[1], prev[0]]
        alias = {3 + len(args) - 1: 0}
        scratch.append(pltpu.VMEM((na, AC), F32))
        tails = [packed, packed]
    else:
        tails = [(AC, na)]
    scratch += [pltpu.SemaphoreType.DMA((14,)), pltpu.SemaphoreType.DMA((1,))]
    return pl.pallas_call(
        functools.partial(bwd_kernel, lo, n, last, r),
        grid_spec=pltpu.PrefetchScalarGridSpec(
            num_scalar_prefetch=3,
            grid=(1,),
            in_specs=in_specs,
            out_specs=[anyspace] + [whole(t) for t in tails],
            scratch_shapes=scratch,
        ),
        out_shape=[jax.ShapeDtypeStruct(block_in.shape, BF)] + [jax.ShapeDtypeStruct(t, BF if last else F32) for t in tails],
        input_output_aliases=alias,
        compiler_params=params(1),
        cost_estimate=cost(12 * n),
        name="backward",
    )(sets, live, order, *args)


def on_device(dpn, fsn, block_in, cotangent, image_live, image_set, expert_routes, expert_slots, gain_attn, gain_moe, w_qkv, w_out,
              w_router, w_up, w_down, qkv_first, qkv_second, out_first, out_second, router_first, router_second, up_first,
              up_second, down_first, down_second):
    ndev = dpn * fsn
    nx = 1 << ((fsn.bit_length() - 1) // 2)
    nz = fsn // nx
    ng = dpn // GRP
    r = D // ndev
    hs = w_up.shape[2]
    d = lax.axis_index("dp")
    q = d % GRP
    rings = [
        (nz, "fsdp", [(f, ((f // nx + 1) % nz) * nx + f % nx) for f in range(fsn)]),
        (nx, "fsdp", [(f, (f // nx) * nx + (f % nx + 1) % nx) for f in range(fsn)]),
        (ng, "dp", [(a, (a + GRP) % dpn) for a in range(dpn)]),
    ]

    def swap(v, bit):
        return lax.ppermute(v, "dp", [(a, a ^ bit) for a in range(dpn)])

    rel = [0, 2, 1, 3]

    tr = jnp.transpose
    small = jnp.concatenate(
        [
            qkv_first, out_first, router_first, tr(out_second),
            jnp.concatenate([w_router, gain_attn[:, None], gain_moe[:, None], jnp.zeros((r, AC - NE - 2), BF)], axis=1),
            jnp.zeros((r, AC), BF).at[0, 0:router_second.shape[0]].set(router_second),
        ],
        axis=1,
    )
    a2s = tr(qkv_second).reshape(3, r, AC)
    second = jnp.concatenate([a2s[0], a2s[1], a2s[2], jnp.zeros((r, 3 * AC), BF)], axis=1)
    front = jnp.stack([w_qkv[:, 0:D], w_qkv[:, D:2 * D], w_qkv[:, 2 * D:], w_out, small, second])
    front = lax.all_gather(front.reshape(6 * r, D), AXES, axis=0, tiled=True).reshape(ndev, 6, r, D)
    wq, wk, wv, wo, b4 = (front[:, j].reshape(D, D) for j in range(5))
    a2t = tr(front[:, 5, :, 0:3 * AC].reshape(ndev, r, 3, AC), (0, 2, 1, 3)).reshape(3 * D, AC)
    gains = jnp.concatenate(
        [b4[:, 4 * AC + NE].reshape(1, D), b4[:, 4 * AC + NE + 1].reshape(1, D), jnp.zeros((6, D), BF)], axis=0
    ).astype(F32)
    rm = front[:, 4, 0, 5 * AC:5 * AC + router_second.shape[0]].reshape(AC, NE)
    rm = jnp.pad(rm, ((0, 0), (0, AC - NE)))

    after = lambda v, *deps: lax.optimization_barrier((v,) + deps)[0]

    ef = jnp.concatenate([up_first, tr(down_second, (0, 2, 1))], axis=2).reshape(GRP, EL, r, 2 * AC)
    own = [lax.dynamic_index_in_dim(ef, q ^ j, 0, keepdims=False) for j in range(GRP)]
    sib_ef = swap(jnp.stack([own[1], own[3]]), 1)
    got_ef = swap(jnp.stack([own[2], sib_ef[1]]), 2)
    mine_ef = jnp.stack([own[0], sib_ef[0], got_ef[0], got_ef[1]])
    wpk = jnp.concatenate([tr(w_up, (0, 2, 1)), tr(up_second, (0, 2, 1)), tr(w_down, (0, 2, 1)), tr(down_first, (0, 2, 1))], axis=2)
    wpk = wpk.reshape(GRP, EL, hs, 2 * DW)
    own = [lax.dynamic_index_in_dim(wpk, q ^ j, 0, keepdims=False) for j in range(GRP)]
    sib = swap(jnp.stack([own[1], own[3]], axis=1), 1)
    near = jnp.stack([own[0], sib[:, 0]], axis=1).reshape(EL, 2 * hs, 2 * DW)
    send, _ = lax.optimization_barrier((jnp.stack([own[2], sib[:, 1]], axis=1), got_ef))
    got = swap(send, 2)
    far = got.reshape(EL, 2 * hs, 2 * DW)

    def hop(v, ring):
        return lax.ppermute(v, ring[1], ring[2])

    up = [[(u, ((u // nx + k) % nz) * nx + u % nx) for u in range(fsn)] for k in range(nz)]
    all_ef = jnp.concatenate([mine_ef] + [lax.ppermute(mine_ef, "fsdp", up[k]) for k in range(1, nz)])
    near, all_ef = lax.optimization_barrier((near, all_ef))
    for n, axis, perm in rings[1:]:
        rows = [all_ef]
        for _ in range(n - 1):
            rows.append(lax.ppermute(rows[-1], axis, perm))
        all_ef = jnp.concatenate(rows)
    near_x, all_ef = lax.optimization_barrier((near, all_ef))
    zn, xn, far = lax.optimization_barrier((hop(near, rings[0]), hop(near_x, rings[1]), far))
    z_row = [jnp.concatenate([near, far], axis=1), jnp.concatenate([zn, hop(far, rings[0])], axis=1)]
    x_row = [jnp.concatenate([xn, hop(far, rings[1])], axis=1)]
    z0, x0, block_in_late = lax.optimization_barrier((z_row[1], x_row[0], block_in))
    z_row[1], x_row[0] = z0, x0
    route = expert_routes.reshape(IMG, LEN, 2)
    slot = expert_slots.reshape(IMG, LEN, 2)
    ids = jnp.arange(NE, dtype=jnp.int32)[None, :, None, None]
    ok = (route[:, None] == ids) & (slot[:, None] >= 0) & (image_live[:, None, None, None] > 0)
    mine_slots = jnp.max(jnp.where(ok, slot[:, None], -1), axis=-1)
    mine_slots = jnp.pad(mine_slots, ((0, 8 - IMG), (0, 0), (0, SL - LEN)), constant_values=-1)
    mine_slots = tr(mine_slots, (1, 0, 2))

    def members(v):
        far = swap(v, 2)
        return [v, far, swap(v, 1), swap(far, 1)]

    def group(v):
        return jnp.stack(members(v))

    all_slots = lax.dynamic_slice_in_dim(group(mine_slots), q * EL, EL, axis=1)
    counts = jnp.max(all_slots, axis=(2, 3)) + 1
    steps = (counts + 15) // 16 * 16
    offs = jnp.concatenate([jnp.zeros((1, EL), jnp.int32), jnp.cumsum(steps, axis=0)], axis=0)
    offs = tr(offs).reshape(-1).astype(jnp.int32)
    firsts = jnp.min(jnp.where(all_slots >= 0, all_slots, CAP), axis=3)[:, :, 0:IMG].reshape(-1)
    all_sets = group(image_set).reshape(-1)
    cots = members(after(cotangent, got))

    f = lax.axis_index("fsdp")
    devs = jnp.arange(ndev, dtype=jnp.int32)
    dd, df = devs // fsn, devs % fsn
    gap = lambda mine, other, n: (mine - other) % n
    spot = (gap(d // GRP, dd // GRP, ng) * nx + gap(f % nx, df % nx, nx)) * nz + gap(f // nx, df // nx, nz)
    ef = jnp.take(all_ef, spot * GRP + ((dd % GRP) ^ q), axis=0)
    ef = tr(ef, (1, 0, 2, 3)).reshape(EL, D, 2 * AC)
    u1, d2 = ef[:, :, 0:AC], ef[:, :, AC:]

    offs, firsts, all_sets, block_in_late, *cots = lax.optimization_barrier((offs, firsts, all_sets, block_in_late, *cots))
    qkv, att, mid, x2, ad, probs = attention_forward(block_in_late, image_set, gains, wq, wk, wv, wo, b4, a2t, rm)
    for k in range(2, nz):
        z_row.append(hop(z_row[-1], rings[0]))
        x_row.append(hop(z_row[k - 1], rings[1]))
        if k + 1 < nz:
            z_row[k], x_row[k - 1] = lax.optimization_barrier((z_row[k], x_row[k - 1]))
    x2y = swap(x2, 2)
    x2y, *_ = lax.optimization_barrier((x2y, z_row[min(2, nz - 1)], x_row[1]))
    x2s = [x2, x2y, swap(x2, 1), swap(x2y, 1)]
    gates = lax.dynamic_slice_in_dim(tr(group(jnp.pad(probs, ((0, 8 - IMG), (0, 0), (0, 0)))), (0, 2, 1, 3)), q * EL, EL, axis=1)

    xa, ga, mk = dispatch(offs, firsts, all_sets, all_slots, gates, x2s, cots, u1, d2)
    def parts_of(rows):
        held = [v for row in rows for v in row]
        join = (ng * nx * nz) // 8
        if join <= 1:
            return held
        return [jnp.concatenate(held[k:k + join], axis=1) for k in range(0, len(held), join)]

    early = ng == 1 and nx == 2 and nz == 4
    if early:
        z_row[-1], x_row[-1], xa = lax.optimization_barrier((z_row[-1], x_row[-1], xa))
        tail = [hop(z_row[-1][0:1], rings[1]), hop(x_row[-1][1:2], rings[0])]
        a1, a2, go, gh = expert_some(offs, xa, ga, z_row + x_row)
        go = [go[k] for k in range(3)]
    else:
        x_row.append(hop(z_row[nz - 1], rings[1]))
        rows = [z_row, x_row]
        for _ in range(2, nx):
            rows.append([hop(v, rings[1]) for v in rows[-1]])
        held = [v for row in rows for v in row]
        rows = [held]
        for _ in range(1, ng):
            rows.append([hop(v, rings[2]) for v in rows[-1]])
        units = parts_of(rows)
        a1, a2, go, gh = expert_some(offs, xa, ga, units[:7])
        go = [go[k] for k in range(3)]
        tail = [units[7][0:1], units[7][1:2]]
    ob, gb, gl, gf = expert_last(offs, xa, ga, mk, a1, a2, u1, d2, tail)

    k = jnp.arange(ng * nx * nz, dtype=jnp.int32)
    kg, kx, kz = k // (nx * nz), k // nz % nx, k % nz
    column = (f // nx - kz) % nz * nx + (f % nx - kx) % nx
    rank = ((d // GRP - kg) % ng * GRP)[:, None] + (q ^ jnp.arange(GRP, dtype=jnp.int32))[None, :]
    spot = (rank * fsn + column[:, None]).reshape(-1)
    gf = jnp.take(gf.reshape(EL, 2, ndev, r, AC), spot, axis=2).reshape(EL, 2, ng * nx, nz * GRP * r, AC)
    simple = ng == 1 and nx == 2
    xback = [(v, u) for u, v in rings[1][2]]
    if simple:
        near_x = lax.ppermute(go[2], "fsdp", xback)
        near_x, ob = lax.optimization_barrier((near_x, ob))
        far_send = jnp.concatenate([gh, gl, gf[:, :, 1]], axis=2)
        far_x = lax.ppermute(far_send, "fsdp", xback)
    else:
        far_send = gf

    fe = (q * EL).reshape(1)
    cut = 2
    parts = []
    for lo, n in ((0, cut), (cut, IMG - cut)):
        ym, yf, yp, gm, gfar, gp = combine(lo, n, offs, firsts, fe, ob, gb, all_slots, gates, cots)
        if parts:
            gp, gy = lax.optimization_barrier((gp, parts[-1][-1]))
            parts[-1] = parts[-1][:-1] + (gy,)
        gc = swap(gp, 1)
        gs = (gfar.astype(F32) + gc[1].astype(F32)).astype(BF)
        gc, gs, ob, far_send = lax.optimization_barrier((gc, gs, ob, far_send))
        parts.append((lo, n, (ym, yf, yp), gm, gc, swap(gs, 2)))

    (lo, n, ya, ga1, gca, gya), (lo2, n2, yb, gb1, gcb, gyb) = parts
    spots = jnp.arange(ndev, dtype=jnp.int32)
    reach = spots % fsn
    column = (f // nx + reach % nz) % nz * nx + (f % nx + reach // nz) % nx
    order = (q ^ jnp.array([0, 2, 1, 3], jnp.int32)[spots // fsn % GRP]) * fsn + column
    order = (order if ng == 1 else spots).astype(jnp.int32)
    yca = swap(ya[2], 1)
    ycb = swap(yb[2], 1)
    add = lambda u, v: (u.astype(F32) + v.astype(F32)).astype(BF)
    ga1, gcb = lax.optimization_barrier((ga1, gcb))
    shared = (probs, mid, qkv, att, x2, ad, gains, wq, wk, wv, wo, b4, a2t, rm)
    first = backward(lo, n, ndev, image_set, image_live, order, block_in, cotangent, ga1, gca, gya, *shared, None)

    head, gyb, yca, ycb = lax.optimization_barrier((first[0], gyb, yca, ycb))
    ysend = jnp.concatenate([add(ya[1], yca[1]), add(yb[1], ycb[1])], axis=0)
    if simple:
        near_x, far_x, _ = lax.optimization_barrier((near_x, far_x, gyb))
        cut = GRP * hs
        s0 = add(go[0], near_x)
        s1 = add(go[1], far_x[:, :, 0:2 * cut])
        sf = add(gf[:, :, 0], far_x[:, :, 2 * cut:])
        hid = [s0[:, :, 0:cut], s0[:, :, cut:], s1[:, :, 0:cut], s1[:, :, cut:]]
        cols = [jnp.concatenate([hid[k], sf[:, :, k * GRP * r:(k + 1) * GRP * r]], axis=2) for k in range(nz)]
    else:
        cut = go[0].shape[2] * 4 // (ng * nx * nz)
        cols = []
        for k, v in enumerate(p for pair in go + [jnp.concatenate([gh, gl], axis=2)] for p in jnp.split(pair, pair.shape[2] // cut, axis=2)):
            at = k % nz * GRP * r
            cols.append(jnp.concatenate([v, gf[:, :, k // nz, at:at + GRP * r]], axis=2))
        for m, axis, perm in rings[2:0:-1]:
            back = [(v, u) for u, v in perm]
            part = len(cols) // m
            rows = [cols[k * part:(k + 1) * part] for k in range(m)]
            cols = rows[m - 1]
            for k in range(m - 2, -1, -1):
                cols = [add(lax.ppermute(v, axis, back), u) for v, u in zip(cols, rows[k])]
    down = [lax.ppermute(cols[k], "fsdp", [(u, ((u // nx - k) % nz) * nx + u % nx) for u in range(fsn)]) for k in range(1, nz)]
    yy = swap(ysend, 2)
    input_grad, mine, other = backward(lo2, n2, ndev, image_set, image_live, order, block_in, cotangent, gb1, gcb, gyb, *shared,
                                       (head, first[1]))
    mine, other, yy, *down = lax.optimization_barrier((mine, other, yy, *down))
    got_small = swap(other, 1) if ng == 1 else other
    got_small, yy, mid, own_cols, *down = lax.optimization_barrier((got_small, yy, mid, cols[0], *down))
    yya, yyb = yy[0:n], yy[n:]

    eg = (own_cols.astype(F32) + sum(v.astype(F32) for v in down)).astype(BF)
    eg = [jnp.concatenate([eg[:, :, j * hs:(j + 1) * hs], eg[:, :, GRP * hs + j * r:GRP * hs + (j + 1) * r]], axis=2) for j in range(GRP)]
    sib = swap(jnp.stack([eg[1], eg[3]]), 1)
    got = swap(jnp.stack([eg[2], sib[1]]), 2)
    got = jnp.concatenate([eg[0][None], sib[0:1], got], axis=0)
    at = jnp.stack([q ^ j for j in range(GRP)])
    eg = jnp.take(got, jnp.argsort(at), axis=0).reshape(NE, 2, hs + r, AC).astype(F32)
    ff = eg[:, :, hs:]
    eg = tr(eg[:, :, 0:hs], (1, 0, 3, 2))
    outs = []
    for at, m, y, yc, yy in ((lo, n, ya, yca, yya), (lo2, n2, yb, ycb, yyb)):
        total = mid[at:at + m] + y[0].astype(F32) + yc[0].astype(F32) + yy.astype(F32)
        outs.append(total[:, 0:LEN])
    block_out = (jnp.concatenate(outs, axis=0) * image_live.astype(F32)[:, None, None]).astype(BF)

    nrs = router_second.shape[0]
    if ng == 1:
        far = swap(add(mine[fsn:], got_small[fsn:]), 2)
        sm = add(add(mine[0:fsn], got_small[0:fsn]), far)
        for k in range(1, nx):
            perm = [(u, (u // nx) * nx + (u % nx + k) % nx) for u in range(fsn)]
            moved = lax.ppermute(sm[k * nz:(k + 1) * nz], "fsdp", perm)
            head = moved if k == 1 else add(head, moved)
        sm = add(sm[0:nz], head)
        total = sm[0].astype(F32)
        for k in range(1, nz):
            total = total + lax.ppermute(sm[k], "fsdp", up[k]).astype(F32)
        sm = total
    else:
        sm = jnp.concatenate([mine, other], axis=0)
        sm = lax.psum_scatter(sm, AXES, scatter_dimension=0, tiled=False).astype(F32)
    rs = tr(sm[7 * r:7 * r + NE]).reshape(-1)
    rs = lax.dynamic_slice_in_dim(rs, (d * fsn + f) * nrs, nrs)
    return (
        block_out,
        input_grad,
        sm[0:r],
        tr(sm[r:4 * r]),
        sm[4 * r:5 * r],
        tr(sm[5 * r:6 * r]),
        sm[6 * r:7 * r],
        rs,
        ff[:, 0],
        eg[0],
        eg[1],
        tr(ff[:, 1], (0, 2, 1)),
    )


def solution(mesh):
    dpn, fsn = mesh.shape["dp"], mesh.shape["fsdp"]
    both = ("dp", "fsdp")
    return jax.shard_map(
        functools.partial(on_device, dpn, fsn),
        mesh=mesh,
        in_specs=(
            P(both, None, None),
            P(both, None, None),
            P(both),
            P(both),
            P(both, None, None),
            P(both, None, None),
            P(both),
            P(both),
            P(both, None),
            P(both, None),
            P(both, None),
            P(None, None, both),
            P(None, None, both),
            P(both, None),
            P(None, both),
            P(both, None),
            P(None, both),
            P(both, None),
            P(both),
            P(None, both, None),
            P(None, None, both),
            P(None, None, both),
            P(None, None, both),
        ),
        out_specs=(
            P(both, None, None),
            P(both, None, None),
            P(both, None),
            P(None, both),
            P(both, None),
            P(None, both),
            P(both, None),
            P(both),
            P(None, both, None),
            P(None, None, both),
            P(None, None, both),
            P(None, None, both),
        ),
        check_vma=False,
    )
```
